32 devices in a mesh: grp: 2 (over y), sp: 8 (over z, x), ch: 2 (over core).
Axes of the slice: x: 2, y: 2, z: 4, core: 2. Of those that a mesh axis runs over, the one named last changes fastest.
Arguments:
- fine_state: float32 [2048, 4, 256], P('sp', ('grp', 'ch')), parts along dimension 1, may hold values from -6 to 6
- coarse_state: float32 [512, 4, 256], P('sp', ('grp', 'ch')), parts along dimension 1, may hold values from -6 to 6
- fine_senders: int32 [8192], P('sp'), may hold values from 0 to 511
- up_owner: int32 [2048, 1], P('sp'), may hold values from 0 to 7; in each aligned block of 256 rows (0 to 255, 256 to 511, ...) at most 64 rows name the same one
- up_local: int32 [2048], P('sp'), may hold values from 0 to 63
- coarse_owner: int32 [2048, 1], P('sp'), may hold values from 0 to 7; in each aligned block of 256 rows (0 to 255, 256 to 511, ...) at most 64 rows name the same one
- coarse_local: int32 [2048], P('sp'), may hold values from 0 to 63
- fine_w_send: float32 [2, 256, 256], replicated, may hold values from -0.375 to 0.375
- fine_w_recv: float32 [2, 256, 256], replicated, may hold values from -0.375 to 0.375
- fine_bias: float32 [2, 256], replicated, may hold values from -3 to 3
- fine_w_out: float32 [2, 256, 256], replicated, may hold values from -0.1875 to 0.1875
- up_w_in: float32 [256, 256], replicated, may hold values from -0.375 to 0.375
- up_bias: float32 [256], replicated, may hold values from -3 to 3
- up_w_out: float32 [256, 256], replicated, may hold values from -0.125 to 0.125
- coarse_w_send: float32 [256, 256], replicated, may hold values from -0.375 to 0.375
- coarse_w_recv: float32 [256, 256], replicated, may hold values from -0.375 to 0.375
- coarse_bias: float32 [256], replicated, may hold values from -3 to 3
- coarse_w_out: float32 [256, 256], replicated, may hold values from -0.1875 to 0.1875
- down_w_in: float32 [256, 256], replicated, may hold values from -0.375 to 0.375
- down_bias: float32 [256], replicated, may hold values from -3 to 3
- down_w_out: float32 [256, 256], replicated, may hold values from -0.375 to 0.375
Outputs:
- fine_out: float32 [2048, 4, 256], P('sp', ('grp', 'ch')), parts along dimension 1
- coarse_out: float32 [512, 4, 256], P('sp', ('grp', 'ch')), parts along dimension 1
The draws below stay inside these ranges and needn't reach their ends.
There are 2 independent parts, one for each index of `grp`. The reference program is written for one: setup_inputs(seed, part) draws one part's arguments, and reference() takes and returns one part's arrays. A program takes and returns all parts, laid end to end along the dimension named above; an argument that names none is the same for every part. Nothing has to cross between parts.
Inputs may be any that keep to these rules, and one draw needn't show every extreme that they name: `up_owner`: within the rows of one device, at most 64 fine nodes name the same dealt set; some dealt set is named exactly 64 times by one device's rows. `coarse_owner`: within the rows of one device, at most 64 coarse edges name the same dealt set; some dealt set is named exactly 64 times by one device's rows.
All inputs are finite; a program needn't handle non-finite values.
Results may differ from the reference program's by a relative error of at most 0.0001.
Values sent between devices are 32-bit elements; how exact they have to be, the bound alone decides.
No kernel may reach another device: no remote copies, remote signals or barrier semaphores. Data moves between devices by JAX's collectives and lax.ppermute only.
A program may use at most 64 MiB of HBM per device.

```python
import math
import jax
import jax.numpy as jnp
import numpy as np
from jax import lax

D = 256
HID = 256
SAMPLES = 2
FINE_DEV = 256
COARSE_DEV = 64
L_F = 2
DEG_F = 4
DEG_C = 4
HALO = 128
FINE = 2048
COARSE = 512
SLOT_CAP = 64
FETCH_CAP = 64
N_SP = 8


def plant(values, own_key, smallest, high):
    shape = values.shape
    spot = [jax.random.randint(jax.random.fold_in(own_key, axis), (), 0, shape[axis]) for axis in range(len(shape))]
    values = values.at[tuple(spot)].set(smallest)
    longest = shape.index(max(shape))
    spot[longest] = (spot[longest] + 1) % shape[longest]
    return values.at[tuple(spot)].set(high)


def levels(own_key, extent, cuts, low, top_value):
    def one(axis_at, shards_of):
        heights = jax.random.uniform(jax.random.fold_in(jax.random.fold_in(own_key, 6), axis_at), (shards_of,), jnp.float32, low / len(cuts), top_value / len(cuts))
        return jnp.repeat(jnp.exp(heights), extent[axis_at] // shards_of).reshape((-1,) + (1,) * (len(extent) - axis_at - 1))

    level = one(*cuts[0])
    for cut in cuts[1:]:
        level = level * one(*cut)
    return level


def deal_out(stream_key, own, number, rows, amount, top, bound, skew):
    ranking = jax.random.permutation(stream_key, amount)
    packed, common = portions_of(amount, rows * top, bound, skew, True), portions_of(amount, rows * top, bound, skew, False)
    places = jnp.arange(amount)

    def named(tallies, rotation):
        used = int((tallies > 0).sum())
        fixed = max(1, used // 4)
        passed = fixed + (places - fixed + rotation * (used - fixed)) % max(1, amount - fixed)
        return jnp.zeros((amount,), jnp.int32).at[ranking[jnp.where(places < fixed, places, passed)]].set(jnp.asarray(tallies, jnp.int32))

    tallies = jnp.where(number % 4 == 0, named(packed, number // 4), named(common, number - number // 4 - 1))
    mixed = jax.random.permutation(jax.random.fold_in(own, 3), amount)
    giver, sink = mixed[0:amount // 2 * 2:2], mixed[1:amount // 2 * 2:2]
    room = jnp.minimum(tallies[giver] - 1, bound - tallies[sink]) // 2
    room = jnp.where((giver == ranking[0]) | (sink == ranking[0]) | (tallies[sink] == 0), 0, jnp.maximum(room, 0))
    passed = jax.random.randint(jax.random.fold_in(own, 4), (amount // 2,), 0, 1 << 20) % (room + 1)
    tallies = tallies.at[giver].add(-passed).at[sink].add(passed)
    members = jnp.searchsorted(jnp.cumsum(tallies), jnp.arange(rows * top), side="right").astype(jnp.int32)
    grid = members.reshape(top, rows).T
    grid = grid[jax.random.permutation(jax.random.fold_in(own, 1), rows)]
    rotation = jax.random.randint(jax.random.fold_in(own, 2), (rows, 1), 0, top)
    return jnp.take_along_axis(grid, (jnp.arange(top)[None, :] + rotation) % top, axis=1)


def portions_of(number_of, total, reach, skew, full):
    loads = [(1 << 20) // math.isqrt(rank ** skew) + 1 for rank in range(1, number_of + 1)]
    largest = reach if full else min(reach, max(-(-total // number_of), total * loads[0] // sum(loads)))
    least = 1 if total - largest >= number_of - 1 else 0
    holding, rest = [largest] + [least] * (number_of - 1), total - largest - least * (number_of - 1)
    while rest > 0:
        movable = [i for i in range(1, number_of) if holding[i] < largest] or [i for i in range(1, number_of) if holding[i] < reach]
        whole, budget = sum([loads[i] for i in movable]), rest
        for i in movable:
            addition = min(reach - holding[i], max(1, budget * loads[i] // whole), rest)
            holding[i] = holding[i] + addition
            rest = rest - addition
    return np.array(holding)


def bell_draw(key, dims, deviation, most, pieces=(), kind=jnp.bfloat16):
    values = jax.random.normal(key, dims, jnp.float32) * deviation
    if len(pieces) > 0:
        values = levels(key, dims, pieces, -0.22, 0.18) * values
    return jnp.clip(values, min=-most, max=most).astype(kind)


def setup_inputs(seed: int = 0, part: int = 0) -> dict:
    seeds = jax.random.split(jax.random.key(seed), 22)
    own_keys = jax.random.split(jax.random.fold_in(seeds[21], part), 22)
    fine_state = bell_draw(own_keys[0], (FINE, SAMPLES, D), 1.0, 6.0, ((0, 8), (1, 2)), jnp.float32)
    coarse_state = bell_draw(own_keys[1], (COARSE, SAMPLES, D), 1.0, 6.0, ((0, 8), (1, 2)), jnp.float32)
    fine_senders = plant(jax.random.randint(seeds[2], (FINE * DEG_F,), 0, FINE_DEV + 2 * HALO), jax.random.fold_in(seeds[2], 1), 0, (FINE_DEV + 2 * HALO) - 1).astype(jnp.int32)
    up_owner_keys = jax.random.split(jax.random.fold_in(seeds[3], 1), FINE // FINE_DEV)
    up_owner_turns = jax.random.permutation(jax.random.fold_in(seeds[3], 3), FINE // FINE_DEV)
    up_owner = jax.vmap(lambda own, number: deal_out(jax.random.fold_in(seeds[3], 2), own, number, FINE_DEV, N_SP, 1, SLOT_CAP, 2))(up_owner_keys, up_owner_turns).reshape((FINE, 1))
    up_local = plant(jax.random.randint(seeds[4], (FINE,), 0, COARSE_DEV), jax.random.fold_in(seeds[4], 1), 0, COARSE_DEV - 1).astype(jnp.int32)
    coarse_owner_keys = jax.random.split(jax.random.fold_in(seeds[5], 1), (COARSE * DEG_C) // (COARSE_DEV * DEG_C))
    coarse_owner_turns = jax.random.permutation(jax.random.fold_in(seeds[5], 3), (COARSE * DEG_C) // (COARSE_DEV * DEG_C))
    coarse_owner = jax.vmap(lambda own, number: deal_out(jax.random.fold_in(seeds[5], 2), own, number, COARSE_DEV * DEG_C, N_SP, 1, FETCH_CAP, 1))(coarse_owner_keys, coarse_owner_turns).reshape((COARSE * DEG_C, 1))
    coarse_local = plant(jax.random.randint(seeds[6], (COARSE * DEG_C,), 0, COARSE_DEV), jax.random.fold_in(seeds[6], 1), 0, COARSE_DEV - 1).astype(jnp.int32)
    fine_w_send = bell_draw(seeds[7], (L_F, D, HID), D ** -0.5, 0.375, (), jnp.float32)
    fine_w_recv = bell_draw(seeds[8], (L_F, D, HID), D ** -0.5, 0.375, (), jnp.float32)
    fine_bias = bell_draw(seeds[9], (L_F, HID), 0.5, 3.0, (), jnp.float32)
    fine_w_out = bell_draw(seeds[10], (L_F, HID, D), (HID * DEG_F) ** -0.5, 0.1875, (), jnp.float32)
    up_w_in = bell_draw(seeds[11], (D, HID), D ** -0.5, 0.375, (), jnp.float32)
    up_bias = bell_draw(seeds[12], (HID,), 0.5, 3.0, (), jnp.float32)
    up_w_out = bell_draw(seeds[13], (HID, D), (HID * 8) ** -0.5, 0.125, (), jnp.float32)
    coarse_w_send = bell_draw(seeds[14], (D, HID), D ** -0.5, 0.375, (), jnp.float32)
    coarse_w_recv = bell_draw(seeds[15], (D, HID), D ** -0.5, 0.375, (), jnp.float32)
    coarse_bias = bell_draw(seeds[16], (HID,), 0.5, 3.0, (), jnp.float32)
    coarse_w_out = bell_draw(seeds[17], (HID, D), (HID * DEG_C) ** -0.5, 0.1875, (), jnp.float32)
    down_w_in = bell_draw(seeds[18], (D, HID), D ** -0.5, 0.375, (), jnp.float32)
    down_bias = bell_draw(seeds[19], (HID,), 0.5, 3.0, (), jnp.float32)
    down_w_out = bell_draw(seeds[20], (HID, D), HID ** -0.5, 0.375, (), jnp.float32)
    return dict(fine_state=fine_state, coarse_state=coarse_state, fine_senders=fine_senders, up_owner=up_owner, up_local=up_local, coarse_owner=coarse_owner, coarse_local=coarse_local, fine_w_send=fine_w_send, fine_w_recv=fine_w_recv, fine_bias=fine_bias, fine_w_out=fine_w_out, up_w_in=up_w_in, up_bias=up_bias, up_w_out=up_w_out, coarse_w_send=coarse_w_send, coarse_w_recv=coarse_w_recv, coarse_bias=coarse_bias, coarse_w_out=coarse_w_out, down_w_in=down_w_in, down_bias=down_bias, down_w_out=down_w_out)


epsilon = 1e-05
highest = lax.Precision.HIGHEST

def layer_norm(values):
    average = lax.optimization_barrier(jnp.mean(values, axis=-1, keepdims=True))
    centered = values - average
    spread = lax.optimization_barrier(jnp.mean(centered * centered, axis=-1, keepdims=True))
    return centered / jnp.sqrt(spread + epsilon)

def project(values, matrix):
    return jnp.einsum('nsd,dh->nsh', values, matrix, precision=highest, preferred_element_type=jnp.float32)

def reference(fine_state, coarse_state, fine_senders, up_owner, up_local, coarse_owner, coarse_local, fine_w_send, fine_w_recv, fine_bias, fine_w_out, up_w_in, up_bias, up_w_out, coarse_w_send, coarse_w_recv, coarse_bias, coarse_w_out, down_w_in, down_bias, down_w_out):
    edge_index = jnp.arange(FINE * DEG_F, dtype=jnp.int32)
    patch_of = edge_index // (FINE_DEV * DEG_F)
    senders = jnp.mod(patch_of * FINE_DEV + fine_senders - HALO, FINE).astype(jnp.int32).reshape(FINE, DEG_F)
    hidden_state = fine_state
    for layer_index in range(L_F):
        normed = layer_norm(hidden_state)
        outward = project(normed, fine_w_send[layer_index])
        inward = project(normed, fine_w_recv[layer_index]) + fine_bias[layer_index]
        summed = jnp.zeros_like(inward)
        for branch in range(DEG_F):
            summed = summed + jax.nn.silu(outward[senders[:, branch]] + inward)
        hidden_state = hidden_state + project(summed, fine_w_out[layer_index])
    parent = (up_owner[:, 0] * COARSE_DEV + up_local).astype(jnp.int32)
    messages = project(jax.nn.silu(project(layer_norm(hidden_state), up_w_in) + up_bias), up_w_out)
    coarse = coarse_state + jax.ops.segment_sum(messages, parent, num_segments=COARSE)
    normed = layer_norm(coarse)
    outward = project(normed, coarse_w_send)
    inward = project(normed, coarse_w_recv) + coarse_bias
    anchor = (coarse_owner[:, 0] * COARSE_DEV + coarse_local).astype(jnp.int32).reshape(COARSE, DEG_C)
    summed = jnp.zeros_like(inward)
    for branch in range(DEG_C):
        summed = summed + jax.nn.silu(outward[anchor[:, branch]] + inward)
    coarse_out = coarse + project(summed, coarse_w_out)
    downward = project(jax.nn.silu(project(layer_norm(coarse_out), down_w_in) + down_bias), down_w_out)
    fine_out = hidden_state + downward[parent]
    return (fine_out, coarse_out)
```

```python
import functools
import jax
import jax.numpy as jnp
from jax import lax
from jax.experimental import pallas as pl
from jax.experimental.pallas import tpu as pltpu
from jax.sharding import PartitionSpec as P

HALO = 128
LANES = 128


epsilon = 1e-05
highest = lax.Precision.HIGHEST


def extended_2(cells, sides, width):
    for axis, dim in sides:
        count = lax.axis_size(axis)
        head = lax.slice_in_dim(cells, 0, width, axis=dim)
        tail = lax.slice_in_dim(cells, cells.shape[dim] - width, cells.shape[dim], axis=dim)
        cells = jnp.concatenate(
            [
                lax.ppermute(tail, axis, [(i, (i + 1) % count) for i in range(count)]),
                cells,
                lax.ppermute(head, axis, [((i + 1) % count, i) for i in range(count)]),
            ],
            axis=dim,
        )
    return cells


def layer_norm(values):
    average = jnp.mean(values, axis=-1, keepdims=True)
    centered = values - average
    spread = jnp.mean(centered * centered, axis=-1, keepdims=True)
    return centered / jnp.sqrt(spread + epsilon)


def project(values, matrix):
    return jnp.einsum(
        "nsd,dh->nsh", values, matrix, precision=highest, preferred_element_type=jnp.float32
    )


def slot_ranks(owners, peer_count):
    matches = (owners[:, None] == jnp.arange(peer_count, dtype=jnp.int32)[None, :]).astype(
        jnp.int32
    )
    ranking = jnp.cumsum(matches, axis=0) - 1
    return jnp.sum(ranking * matches, axis=1)


def general_shards(
    fine_state,
    coarse_state,
    fine_senders,
    up_owner,
    up_local,
    coarse_owner,
    coarse_local,
    fine_w_send,
    fine_w_recv,
    fine_bias,
    fine_w_out,
    up_w_in,
    up_bias,
    up_w_out,
    coarse_w_send,
    coarse_w_recv,
    coarse_bias,
    coarse_w_out,
    down_w_in,
    down_bias,
    down_w_out,
):
    peer_count = lax.axis_size("sp")
    fine_rows = fine_state.shape[0]
    coarse_rows = coarse_state.shape[0]
    samples = fine_state.shape[1]
    feature_width = fine_state.shape[2]
    degree_fine = fine_senders.shape[0] // fine_rows
    degree_coarse = coarse_owner.shape[0] // coarse_rows
    hidden_state = fine_state
    for layer_index in range(fine_w_send.shape[0]):
        normed = layer_norm(hidden_state)
        outward = project(normed, fine_w_send[layer_index])
        inward = project(normed, fine_w_recv[layer_index]) + fine_bias[layer_index]
        extended = extended_2(outward, (("sp", 0),), HALO)
        gathered = extended[fine_senders].reshape(fine_rows, degree_fine, samples, -1)
        summed = jnp.sum(jax.nn.silu(gathered + inward[:, None]), axis=1)
        hidden_state = hidden_state + project(summed, fine_w_out[layer_index])
    capacity = max(4, 2 * fine_rows // peer_count)
    owners = up_owner[:, 0]
    places = owners * capacity + slot_ranks(owners, peer_count)
    targets = (
        jnp.full((peer_count * capacity,), -1.0, jnp.float32)
        .at[places]
        .set(up_local.astype(jnp.float32))
        .reshape(peer_count, capacity)
    )
    activated = jax.nn.silu(project(layer_norm(hidden_state), up_w_in) + up_bias)
    coarse_ids = jnp.arange(coarse_rows, dtype=jnp.float32)[:, None]
    messages = project(activated, up_w_out)
    outgoing = (
        jnp.zeros((peer_count * capacity, samples, feature_width), jnp.float32)
        .at[places]
        .set(messages)
        .reshape(peer_count, capacity, samples, feature_width)
    )
    arrived, sources = (
        lax.all_to_all(outgoing, "sp", split_axis=0, concat_axis=0, tiled=True),
        lax.all_to_all(targets, "sp", split_axis=0, concat_axis=0, tiled=True),
    )
    selector = (sources.reshape(1, -1) == coarse_ids).astype(jnp.float32)
    gained = jnp.einsum(
        "cr,rsd->csd",
        selector,
        arrived.reshape(peer_count * capacity, samples, feature_width),
        precision=highest,
        preferred_element_type=jnp.float32,
    )
    coarse = coarse_state + gained
    normed = layer_norm(coarse)
    outward = project(normed, coarse_w_send)
    inward = project(normed, coarse_w_recv) + coarse_bias
    anchor_owner = coarse_owner[:, 0]
    everything = lax.all_gather(outward, "sp", axis=0, tiled=True)
    picked = everything[anchor_owner * coarse_rows + coarse_local]
    edge_terms = picked.reshape(coarse_rows, degree_coarse, samples, -1)
    summed = jnp.sum(jax.nn.silu(edge_terms + inward[:, None]), axis=1)
    coarse_out = coarse + project(summed, coarse_w_out)
    downward = project(
        jax.nn.silu(project(layer_norm(coarse_out), down_w_in) + down_bias), down_w_out
    )
    wanted = jnp.maximum(sources.reshape(-1), 0.0).astype(jnp.int32)
    replies = downward[wanted].reshape(peer_count, capacity, samples, feature_width)
    answered = lax.all_to_all(replies, "sp", split_axis=0, concat_axis=0, tiled=True)
    fine_out = (
        hidden_state + answered.reshape(peer_count * capacity, samples, feature_width)[places]
    )
    return (fine_out, coarse_out)


f32 = jnp.float32
bf16 = jnp.bfloat16


def load_rows(ref, rows, parts, start=0):
    return jnp.concatenate(
        [ref[pl.ds(start * parts + j, rows, stride=parts), :] for j in range(parts)], axis=1
    )


def store_rows(ref, values, parts, start=0):
    for j in range(parts):
        ref[pl.ds(start * parts + j, values.shape[0], stride=parts), :] = values[
            :, j * LANES : (j + 1) * LANES
        ]


def halves(values):
    high = values.astype(bf16)
    return high, (values - high.astype(f32)).astype(bf16)


def mm(a, b):
    return jnp.dot(a, b, preferred_element_type=f32)


def times(values, matrix):
    vh, vl = halves(values)
    mh, ml = halves(matrix)
    return mm(vh, mh) + (mm(vl, mh) + mm(vh, ml))


def times_one_hot(one_hot, values):
    vh, vl = halves(values)
    return mm(one_hot, vh) + mm(one_hot, vl)


def unit(values):
    width = values.shape[1]
    average = jnp.sum(values, axis=1, keepdims=True) * (1.0 / width)
    centered = values - average
    spread = jnp.sum(centered * centered, axis=1, keepdims=True) * (1.0 / width)
    return centered * lax.rsqrt(spread + epsilon)


def gate(half):
    return half + half * jnp.tanh(half)


def columns_equal(column, count):
    ids = lax.broadcasted_iota(jnp.int32, (column.shape[0], count), 1)
    return jnp.where(ids == column, 1.0, 0.0).astype(bf16)


def near_kernel(first, state_ref, *refs):
    if first:
        index_ref, ws_ref, wr_ref, bias_ref, hot_ref, got_ref, into_ref = refs
    else:
        hot_ref, ws_ref, wr_ref, bias_ref, got_ref, into_ref = refs
    layer = 0 if first else 1
    rows, width = into_ref.shape
    parts = width // LANES
    edges, window = hot_ref.shape
    if first:
        columns = jnp.transpose(index_ref[...])
        blocks = edges // LANES
        for b in range(blocks):
            hot_ref[b * LANES : (b + 1) * LANES, :] = columns_equal(
                columns[:, b : b + 1], window
            )
    normed = unit(load_rows(state_ref, rows, parts))
    into_ref[...] = (times(normed, wr_ref[layer]) + bias_ref[layer : layer + 1, :]) * 0.5
    sends = times(normed, ws_ref[layer]) * 0.5
    got_ref[...] = times_one_hot(hot_ref[:, :rows], sends)


def far_sum(layer, swap_ref, diag_ref, state_ref, hot_ref, got_ref, into_ref, ws_ref, wo_ref):
    rows, width = into_ref.shape
    parts = width // LANES
    rim = swap_ref.shape[0] // parts
    degree = hot_ref.shape[0] // rows
    far = jnp.concatenate(
        [load_rows(swap_ref, rim, parts), load_rows(diag_ref, rim, parts)], axis=0
    )
    sends = times(unit(far), ws_ref[layer]) * 0.5
    high, low = halves(sends)
    total = None
    for k in range(degree):
        hot = hot_ref[k * rows : (k + 1) * rows, rows:]
        half = got_ref[k * rows : (k + 1) * rows, :] + into_ref[...] + (mm(hot, high) + mm(hot, low))
        total = gate(half) if total is None else total + gate(half)
    return load_rows(state_ref, rows, parts) + times(total, wo_ref[layer])


def far_kernel(
    odd_ref, swap_ref, diag_ref, state_ref, hot_ref, got_ref, into_ref, ws_ref, wo_ref,
    next_ref, out_swap_ref, out_diag_ref,
):
    parts = into_ref.shape[1] // LANES
    store_rows(
        next_ref,
        far_sum(0, swap_ref, diag_ref, state_ref, hot_ref, got_ref, into_ref, ws_ref, wo_ref),
        parts,
    )
    lines = out_swap_ref.shape[0]
    odd = odd_ref[0]
    last = next_ref.shape[0] - lines
    out_swap_ref[...] = next_ref[pl.ds(pl.multiple_of((1 - odd) * last, LANES), lines), :]
    out_diag_ref[...] = next_ref[pl.ds(pl.multiple_of(odd * last, LANES), lines), :]


def up_kernel(
    me_ref, swap_ref, diag_ref, state_ref, hot_ref, got_ref, into_ref, ws_ref, wo_ref,
    parent_ref, wi_ref, bias_ref, wu_ref, last_ref, *slot_refs,
):
    hidden = far_sum(
        1, swap_ref, diag_ref, state_ref, hot_ref, got_ref, into_ref, ws_ref, wo_ref
    )
    last_ref[...] = hidden
    rows, width = hidden.shape
    parts = width // LANES
    act = gate((times(unit(hidden), wi_ref[...]) + bias_ref[...]) * 0.5)
    messages = times(act, wu_ref[...])
    count = slot_refs[0].shape[0] // parts
    coarse = count * len(slot_refs)
    place = jnp.bitwise_xor(parent_ref[...], me_ref[0] * count)
    ids = lax.broadcasted_iota(jnp.int32, (coarse, rows), 0)
    select = jnp.where(ids == place, 1.0, 0.0).astype(bf16)
    sums = times_one_hot(select, messages)
    for k, slot in enumerate(slot_refs):
        store_rows(slot, sums[k * count : (k + 1) * count, :], parts)


def middle_kernel(state_ref, anchor_ref, *refs):
    out_ref = refs[-1]
    total = state_ref[...]
    for ref in refs[:-1]:
        total = total + ref[...]
    lines = total.shape[0]
    out_ref[:lines, :] = total
    out_ref[lines:, :] = anchor_ref[...]


def coarse_kernel(peers, anchor_lines, me_ref, last_ref, parent_ref, *refs):
    blocks = refs[:peers]
    cs_ref, cr_ref, cb_ref, co_ref, di_ref, db_ref, do_ref, fine_ref, coarse_ref = refs[peers:]
    rows, width = last_ref.shape
    parts = width // LANES
    count = coarse_ref.shape[0] // parts
    coarse = count * peers
    lines = coarse_ref.shape[0]
    flip = me_ref[0] * count
    middle = jnp.concatenate([load_rows(b, count, parts) for b in blocks], axis=0)
    normed = unit(middle)
    high, low = halves(times(normed, cs_ref[...]) * 0.5)
    into = (times(normed, cr_ref[...]) + cb_ref[...]) * 0.5
    anchors = [
        jnp.bitwise_xor(
            jnp.transpose(b[lines : lines + anchor_lines, :]).astype(jnp.int32), flip
        )
        for b in blocks
    ]
    per_line = LANES // count
    degree = 4
    total = None
    for k in range(degree):
        low_row = (k % per_line) * count
        column = jnp.concatenate(
            [
                a[low_row : low_row + count, k // per_line : k // per_line + 1]
                for a in anchors
            ],
            axis=0,
        )
        hot = columns_equal(column, coarse)
        half = into + (mm(hot, high) + mm(hot, low))
        total = gate(half) if total is None else total + gate(half)
    done = middle + times(total, co_ref[...])
    store_rows(coarse_ref, done[:count, :], parts)
    act = gate((times(unit(done), di_ref[...]) + db_ref[...]) * 0.5)
    down = times(act, do_ref[...])
    dh, dl = halves(down)
    places = jnp.bitwise_xor(jnp.transpose(parent_ref[...]), flip)
    for j in range(rows // LANES):
        hot = columns_equal(places[:, j : j + 1], coarse)
        store_rows(
            fine_ref,
            last_ref[j * LANES : (j + 1) * LANES, :] + (mm(hot, dh) + mm(hot, dl)),
            parts,
            start=j * LANES,
        )


VMEM = pl.BlockSpec(memory_space=pltpu.VMEM)
SMEM = pl.BlockSpec(memory_space=pltpu.SMEM)


def call(kernel, in_specs, out_shapes, name):
    return pl.pallas_call(
        kernel,
        in_specs=in_specs,
        out_specs=[VMEM] * len(out_shapes),
        out_shape=out_shapes,
        name=name,
        compiler_params=pltpu.CompilerParams(vmem_limit_bytes=32 * 2**20),
    )


def shape(*dims, kind=f32):
    return jax.ShapeDtypeStruct(dims, kind)


def kernel_shards(
    fine_state,
    coarse_state,
    fine_senders,
    up_owner,
    up_local,
    coarse_owner,
    coarse_local,
    fine_w_send,
    fine_w_recv,
    fine_bias,
    fine_w_out,
    up_w_in,
    up_bias,
    up_w_out,
    coarse_w_send,
    coarse_w_recv,
    coarse_bias,
    coarse_w_out,
    down_w_in,
    down_bias,
    down_w_out,
):
    peers = lax.axis_size("sp")
    me = lax.axis_index("sp").astype(jnp.int32)
    odd = me % 2
    rows, _, width = fine_state.shape
    count = coarse_state.shape[0]
    parts = width // LANES
    degree = fine_senders.shape[0] // rows
    degree_coarse = coarse_owner.shape[0] // count
    swap = [(i, i ^ 1) for i in range(peers)]
    diag = [(i, (i + 1 if i % 2 else i - 1) % peers) for i in range(peers)]
    rim = HALO * parts

    state = fine_state.reshape(rows * parts, LANES)
    last = (rows - HALO) * parts
    out_swap = lax.dynamic_slice(state, ((1 - odd) * last, 0), (rim, LANES))
    out_diag = lax.dynamic_slice(state, (odd * last, 0), (rim, LANES))

    before = jnp.where(odd == 1, rows, rows + HALO)
    after = jnp.where(odd == 1, rows + HALO, rows)
    index = jnp.where(
        fine_senders < HALO,
        fine_senders + before,
        jnp.where(
            fine_senders < HALO + rows,
            fine_senders - HALO,
            fine_senders - (HALO + rows) + after,
        ),
    )
    index = index.reshape(rows, degree).T.reshape(rows * degree // LANES, LANES)
    parent = up_owner[:, 0] * count + up_local
    anchor = (coarse_owner[:, 0] * count + coarse_local).reshape(count, degree_coarse).T
    anchor_lines = count * degree_coarse // LANES
    anchor = jnp.pad(
        anchor.astype(f32).reshape(anchor_lines, LANES), ((0, 8 - anchor_lines % 8), (0, 0))
    )
    odd_arg, me_arg = odd.reshape(1), me.reshape(1)

    edges, window = rows * degree, rows + 2 * HALO
    in_swap = lax.ppermute(out_swap, "sp", swap)
    in_diag = lax.ppermute(out_diag, "sp", diag)
    hot, got, into = call(
        functools.partial(near_kernel, True),
        [VMEM] * 5,
        [shape(edges, window, kind=bf16), shape(edges, width), shape(rows, width)],
        "near0",
    )(state, index, fine_w_send, fine_w_recv, fine_bias)
    state, out_swap, out_diag = call(
        far_kernel,
        [SMEM] + [VMEM] * 8,
        [shape(rows * parts, LANES), shape(rim, LANES), shape(rim, LANES)],
        "far0",
    )(odd_arg, in_swap, in_diag, state, hot, got, into, fine_w_send, fine_w_out)
    in_swap = lax.ppermute(out_swap, "sp", swap)
    in_diag = lax.ppermute(out_diag, "sp", diag)
    got, into = call(
        functools.partial(near_kernel, False),
        [VMEM] * 5,
        [shape(edges, width), shape(rows, width)],
        "near1",
    )(state, hot, fine_w_send, fine_w_recv, fine_bias)
    hidden, *slots = call(
        up_kernel,
        [SMEM] + [VMEM] * 12,
        [shape(rows, width)] + [shape(count * parts, LANES)] * peers,
        "up",
    )(
        me_arg, in_swap, in_diag, state, hot, got, into, fine_w_send, fine_w_out,
        parent.reshape(1, rows), up_w_in, up_bias.reshape(1, width), up_w_out,
    )
    arrived = [slots[0]] + [
        lax.ppermute(slots[k], "sp", [(i, i ^ k) for i in range(peers)]) for k in range(1, peers)
    ]
    (middle,) = call(
        middle_kernel,
        [VMEM] * (2 + peers),
        [shape(count * parts + anchor.shape[0], LANES)],
        "middle",
    )(coarse_state.reshape(count * parts, LANES), anchor, *arrived)
    columns = {0: middle}
    for k in range(2, peers, 2):
        columns[k] = lax.ppermute(middle, "sp", [(i, i ^ k) for i in range(peers)])
    for k in range(0, peers, 2):
        columns[k + 1] = lax.ppermute(columns[k], "sp", swap)
    fine_out, coarse_out = call(
        functools.partial(coarse_kernel, peers, anchor_lines),
        [SMEM] + [VMEM] * (9 + peers),
        [shape(rows * parts, LANES), shape(count * parts, LANES)],
        "coarse",
    )(
        me_arg, hidden, parent.reshape(rows // LANES, LANES),
        *[columns[k] for k in range(peers)],
        coarse_w_send, coarse_w_recv, coarse_bias.reshape(1, width), coarse_w_out,
        down_w_in, down_bias.reshape(1, width), down_w_out,
    )
    return (fine_out.reshape(fine_state.shape), coarse_out.reshape(coarse_state.shape))


def shards(*args):
    fine_state, coarse_state, fine_senders = args[0], args[1], args[2]
    coarse_owner, layers = args[5], args[7].shape[0]
    peers = lax.axis_size("sp")
    rows, samples, width = fine_state.shape
    count = coarse_state.shape[0]
    fits = (
        samples == 1
        and layers == 2
        and width % LANES == 0
        and peers % 2 == 0
        and peers & (peers - 1) == 0
        and rows % LANES == 0
        and rows >= HALO
        and count & (count - 1) == 0
        and LANES % count == 0
        and coarse_owner.shape[0] % LANES == 0
        and coarse_owner.shape[0] == 4 * count
        and fine_senders.shape[0] % (8 * LANES) == 0
        and peers * count <= 1024
    )
    return (kernel_shards if fits else general_shards)(*args)


def solution(mesh):
    in_specs = (
        P("sp", ("grp", "ch"), None),
        P("sp", ("grp", "ch"), None),
        P("sp"),
        P("sp", None),
        P("sp"),
        P("sp", None),
        P("sp"),
    ) + (P(),) * 14
    out_specs = (P("sp", ("grp", "ch"), None), P("sp", ("grp", "ch"), None))
    return jax.shard_map(shards, mesh=mesh, in_specs=in_specs, out_specs=out_specs, check_vma=False)
```

```python
import functools
import jax
import jax.numpy as jnp
from jax import lax
from jax.experimental import pallas as pl
from jax.experimental.pallas import tpu as pltpu
from jax.sharding import PartitionSpec as P

HALO = 128
LANES = 128


epsilon = 1e-05
highest = lax.Precision.HIGHEST


def extended_2(cells, sides, width):
    for axis, dim in sides:
        count = lax.axis_size(axis)
        head = lax.slice_in_dim(cells, 0, width, axis=dim)
        tail = lax.slice_in_dim(cells, cells.shape[dim] - width, cells.shape[dim], axis=dim)
        cells = jnp.concatenate(
            [
                lax.ppermute(tail, axis, [(i, (i + 1) % count) for i in range(count)]),
                cells,
                lax.ppermute(head, axis, [((i + 1) % count, i) for i in range(count)]),
            ],
            axis=dim,
        )
    return cells


def layer_norm(values):
    average = jnp.mean(values, axis=-1, keepdims=True)
    centered = values - average
    spread = jnp.mean(centered * centered, axis=-1, keepdims=True)
    return centered / jnp.sqrt(spread + epsilon)


def project(values, matrix):
    return jnp.einsum(
        "nsd,dh->nsh", values, matrix, precision=highest, preferred_element_type=jnp.float32
    )


def slot_ranks(owners, peer_count):
    matches = (owners[:, None] == jnp.arange(peer_count, dtype=jnp.int32)[None, :]).astype(
        jnp.int32
    )
    ranking = jnp.cumsum(matches, axis=0) - 1
    return jnp.sum(ranking * matches, axis=1)


def general_shards(
    fine_state,
    coarse_state,
    fine_senders,
    up_owner,
    up_local,
    coarse_owner,
    coarse_local,
    fine_w_send,
    fine_w_recv,
    fine_bias,
    fine_w_out,
    up_w_in,
    up_bias,
    up_w_out,
    coarse_w_send,
    coarse_w_recv,
    coarse_bias,
    coarse_w_out,
    down_w_in,
    down_bias,
    down_w_out,
):
    peer_count = lax.axis_size("sp")
    fine_rows = fine_state.shape[0]
    coarse_rows = coarse_state.shape[0]
    samples = fine_state.shape[1]
    feature_width = fine_state.shape[2]
    degree_fine = fine_senders.shape[0] // fine_rows
    degree_coarse = coarse_owner.shape[0] // coarse_rows
    hidden_state = fine_state
    for layer_index in range(fine_w_send.shape[0]):
        normed = layer_norm(hidden_state)
        outward = project(normed, fine_w_send[layer_index])
        inward = project(normed, fine_w_recv[layer_index]) + fine_bias[layer_index]
        extended = extended_2(outward, (("sp", 0),), HALO)
        gathered = extended[fine_senders].reshape(fine_rows, degree_fine, samples, -1)
        summed = jnp.sum(jax.nn.silu(gathered + inward[:, None]), axis=1)
        hidden_state = hidden_state + project(summed, fine_w_out[layer_index])
    capacity = max(4, 2 * fine_rows // peer_count)
    owners = up_owner[:, 0]
    places = owners * capacity + slot_ranks(owners, peer_count)
    targets = (
        jnp.full((peer_count * capacity,), -1.0, jnp.float32)
        .at[places]
        .set(up_local.astype(jnp.float32))
        .reshape(peer_count, capacity)
    )
    activated = jax.nn.silu(project(layer_norm(hidden_state), up_w_in) + up_bias)
    coarse_ids = jnp.arange(coarse_rows, dtype=jnp.float32)[:, None]
    messages = project(activated, up_w_out)
    outgoing = (
        jnp.zeros((peer_count * capacity, samples, feature_width), jnp.float32)
        .at[places]
        .set(messages)
        .reshape(peer_count, capacity, samples, feature_width)
    )
    arrived, sources = (
        lax.all_to_all(outgoing, "sp", split_axis=0, concat_axis=0, tiled=True),
        lax.all_to_all(targets, "sp", split_axis=0, concat_axis=0, tiled=True),
    )
    selector = (sources.reshape(1, -1) == coarse_ids).astype(jnp.float32)
    gained = jnp.einsum(
        "cr,rsd->csd",
        selector,
        arrived.reshape(peer_count * capacity, samples, feature_width),
        precision=highest,
        preferred_element_type=jnp.float32,
    )
    coarse = coarse_state + gained
    normed = layer_norm(coarse)
    outward = project(normed, coarse_w_send)
    inward = project(normed, coarse_w_recv) + coarse_bias
    anchor_owner = coarse_owner[:, 0]
    everything = lax.all_gather(outward, "sp", axis=0, tiled=True)
    picked = everything[anchor_owner * coarse_rows + coarse_local]
    edge_terms = picked.reshape(coarse_rows, degree_coarse, samples, -1)
    summed = jnp.sum(jax.nn.silu(edge_terms + inward[:, None]), axis=1)
    coarse_out = coarse + project(summed, coarse_w_out)
    downward = project(
        jax.nn.silu(project(layer_norm(coarse_out), down_w_in) + down_bias), down_w_out
    )
    wanted = jnp.maximum(sources.reshape(-1), 0.0).astype(jnp.int32)
    replies = downward[wanted].reshape(peer_count, capacity, samples, feature_width)
    answered = lax.all_to_all(replies, "sp", split_axis=0, concat_axis=0, tiled=True)
    fine_out = (
        hidden_state + answered.reshape(peer_count * capacity, samples, feature_width)[places]
    )
    return (fine_out, coarse_out)


f32 = jnp.float32
bf16 = jnp.bfloat16


def load_rows(ref, rows, parts, start=0):
    return jnp.concatenate(
        [ref[pl.ds(start * parts + j, rows, stride=parts), :] for j in range(parts)], axis=1
    )


def store_rows(ref, values, parts, start=0):
    for j in range(parts):
        ref[pl.ds(start * parts + j, values.shape[0], stride=parts), :] = values[
            :, j * LANES : (j + 1) * LANES
        ]


def halves(values):
    high = values.astype(bf16)
    return high, (values - high.astype(f32)).astype(bf16)


def mm(a, b):
    return jnp.dot(a, b, preferred_element_type=f32)


def times(values, matrix):
    vh, vl = halves(values)
    mh, ml = halves(matrix)
    return mm(vh, mh) + (mm(vl, mh) + mm(vh, ml))


def times_one_hot(one_hot, values):
    vh, vl = halves(values)
    return mm(one_hot, vh) + mm(one_hot, vl)


def unit(values):
    width = values.shape[1]
    average = jnp.sum(values, axis=1, keepdims=True) * (1.0 / width)
    centered = values - average
    spread = jnp.sum(centered * centered, axis=1, keepdims=True) * (1.0 / width)
    return centered * lax.rsqrt(spread + epsilon)


def gate(half):
    return half + half * jnp.tanh(half)


def columns_equal(column, count):
    ids = lax.broadcasted_iota(jnp.int32, (column.shape[0], count), 1)
    return jnp.where(ids == column, 1.0, 0.0).astype(bf16)


def near_kernel(first, state_ref, *refs):
    if first:
        (
            index_ref, ws_ref, wr_ref, bias_ref, up_ref, cb_ref, db_ref,
            hot_ref, got_ref, into_ref, pack_ref,
        ) = refs
        bias = bias_ref[0:1, :]
    else:
        hot_ref, ws_ref, wr_ref, pack_ref, got_ref, into_ref, high_ref, low_ref = refs
        bias = pack_ref[0:1, :]
    layer = 0 if first else 1
    rows, width = into_ref.shape
    parts = width // LANES
    if first:
        build_hot(hot_ref, jnp.transpose(index_ref[...]))
        pack_ref[...] = jnp.concatenate(
            [bias_ref[1:2, :], up_ref[...], cb_ref[...], db_ref[...]]
            + [jnp.zeros_like(up_ref[...])] * 4,
            axis=0,
        )
    normed = unit(load_rows(state_ref, rows, parts))
    into_ref[...] = (times(normed, wr_ref[layer]) + bias) * 0.5
    high, low = halves(times(normed, ws_ref[layer]) * 0.5)
    if not first:
        high_ref[...] = high
        low_ref[...] = low
    hot = hot_ref[:, :rows]
    got_ref[...] = mm(hot, high) + mm(hot, low)


def build_hot(hot_ref, columns):
    window = hot_ref.shape[1]
    for b in range(hot_ref.shape[0] // LANES):
        hot_ref[b * LANES : (b + 1) * LANES, :] = columns_equal(columns[:, b : b + 1], window)


def far_kernel(
    odd_ref, swap_ref, diag_ref, state_ref, hot_ref, got_ref, into_ref, ws_ref, wo_ref,
    index_ref, parent_ref, out_full_ref, out_half_ref,
):
    rows, width = into_ref.shape
    parts = width // LANES
    rim = swap_ref.shape[0] // parts
    degree = hot_ref.shape[0] // rows
    far = jnp.concatenate(
        [load_rows(swap_ref, rim, parts), load_rows(diag_ref, rim, parts)], axis=0
    )
    high, low = halves(times(unit(far), ws_ref[0]) * 0.5)
    total = None
    for k in range(degree):
        hot = hot_ref[k * rows : (k + 1) * rows, rows:]
        half = got_ref[k * rows : (k + 1) * rows, :] + into_ref[...] + (mm(hot, high) + mm(hot, low))
        total = gate(half) if total is None else total + gate(half)
    store_rows(out_full_ref, load_rows(state_ref, rows, parts) + times(total, wo_ref[0]), parts)
    lines = rows * parts
    senders = index_ref.shape[0]
    rest = out_full_ref.shape[0] - lines - senders
    out_full_ref[lines : lines + senders, :] = index_ref[...].astype(f32)
    out_full_ref[lines + senders :, :] = jnp.concatenate(
        [parent_ref[...].astype(f32), jnp.zeros((rest - parent_ref.shape[0], LANES), f32)], axis=0
    )
    half_lines = out_half_ref.shape[0]
    start = pl.multiple_of(odd_ref[0] * (lines - half_lines), LANES)
    out_half_ref[...] = out_full_ref[pl.ds(start, half_lines), :]


def up_kernel(
    peers, odd_ref, me_ref, full_ref, swap_ref, pair_ref, diag_ref, hot_ref, got_ref, into_ref,
    high_ref, low_ref, ws_ref, wr_ref, wo_ref, parent_ref, wi_ref, wu_ref, pack_ref,
    last_ref, *refs,
):
    slot_refs = refs[: peers // 2]
    hot2_ref, mh_ref, ml_ref, th_ref, tl_ref = refs[peers // 2 :]
    rows, width = into_ref.shape
    parts = width // LANES
    rim = diag_ref.shape[0] // parts
    degree = hot_ref.shape[0] // rows
    lines = rows * parts
    senders = hot_ref.shape[0] // LANES
    odd = odd_ref[0]
    mine_touch = pl.multiple_of((1 - odd) * (rows - rim), LANES)
    other_touch = pl.multiple_of(odd * (rows - rim), LANES)

    build_hot(
        hot2_ref, jnp.transpose(swap_ref[lines : lines + senders, :]).astype(jnp.int32)
    )
    other = load_rows(swap_ref, rows, parts)
    normed = unit(
        jnp.concatenate(
            [other, load_rows(pair_ref, rim, parts), load_rows(diag_ref, rim, parts)], axis=0
        )
    )
    high, low = halves(times(normed, ws_ref[1]) * 0.5)
    for src, t_ref, m_ref, own_ref in (
        (high, th_ref, mh_ref, high_ref), (low, tl_ref, ml_ref, low_ref),
    ):
        t_ref[:rows, :] = src[:rows, :]
        t_ref[rows : rows + rim, :] = own_ref[pl.ds(mine_touch, rim), :]
        t_ref[rows + rim :, :] = src[rows : rows + rim, :]
        m_ref[:rim, :] = t_ref[pl.ds(other_touch, rim), :]
        m_ref[rim:, :] = src[rows + rim :, :]
    into = (times(normed[:rows, :], wr_ref[1]) + pack_ref[0:1, :]) * 0.5
    total, total2 = None, None
    for k in range(degree):
        part = slice(k * rows, (k + 1) * rows)
        hot = hot_ref[part, rows:]
        half = got_ref[part, :] + into_ref[...] + (mm(hot, mh_ref[...]) + mm(hot, ml_ref[...]))
        total = gate(half) if total is None else total + gate(half)
        hot = hot2_ref[part, :]
        half = into + (mm(hot, th_ref[...]) + mm(hot, tl_ref[...]))
        total2 = gate(half) if total2 is None else total2 + gate(half)
    hidden = jnp.concatenate([load_rows(full_ref, rows, parts), other], axis=0) + times(
        jnp.concatenate([total, total2], axis=0), wo_ref[1]
    )
    last_ref[...] = hidden[:rows, :]
    act = gate((times(unit(hidden), wi_ref[...]) + pack_ref[1:2, :]) * 0.5)
    messages = times(act, wu_ref[...])
    count = slot_refs[0].shape[0] // parts
    coarse = count * len(slot_refs)
    first = lines + senders
    parents = [parent_ref[j : j + 1, :] for j in range(rows // LANES)] + [
        swap_ref[first + j : first + j + 1, :].astype(jnp.int32) for j in range(rows // LANES)
    ]
    place = jnp.bitwise_xor(jnp.concatenate(parents, axis=1), me_ref[0] * count)
    ids = lax.broadcasted_iota(jnp.int32, (coarse, 2 * rows), 0)
    ids = ids + jnp.bitwise_and(ids, -count)
    select = jnp.where(ids == place, 1.0, 0.0).astype(bf16)
    sums = times_one_hot(select, messages)
    for k, slot in enumerate(slot_refs):
        store_rows(slot, sums[k * count : (k + 1) * count, :], parts)


def middle_kernel(state_ref, anchor_ref, *refs):
    out_ref = refs[-1]
    total = state_ref[...]
    for ref in refs[:-1]:
        total = total + ref[...]
    lines = total.shape[0]
    out_ref[:lines, :] = total
    out_ref[lines:, :] = anchor_ref[...]


def coarse_kernel(peers, anchor_lines, me_ref, last_ref, parent_ref, *refs):
    blocks = refs[:peers]
    cs_ref, cr_ref, co_ref, di_ref, do_ref, pack_ref, fine_ref, coarse_ref = refs[peers:]
    rows, width = last_ref.shape
    parts = width // LANES
    count = coarse_ref.shape[0] // parts
    coarse = count * peers
    lines = coarse_ref.shape[0]
    flip = me_ref[0] * count
    middle = jnp.concatenate([load_rows(b, count, parts) for b in blocks], axis=0)
    normed = unit(middle)
    high, low = halves(times(normed, cs_ref[...]) * 0.5)
    into = (times(normed, cr_ref[...]) + pack_ref[2:3, :]) * 0.5
    anchors = [
        jnp.bitwise_xor(
            jnp.transpose(b[lines : lines + anchor_lines, :]).astype(jnp.int32), flip
        )
        for b in blocks
    ]
    per_line = LANES // count
    degree = 4
    total = None
    for k in range(degree):
        low_row = (k % per_line) * count
        column = jnp.concatenate(
            [
                a[low_row : low_row + count, k // per_line : k // per_line + 1]
                for a in anchors
            ],
            axis=0,
        )
        hot = columns_equal(column, coarse)
        half = into + (mm(hot, high) + mm(hot, low))
        total = gate(half) if total is None else total + gate(half)
    done = middle + times(total, co_ref[...])
    store_rows(coarse_ref, done[:count, :], parts)
    act = gate((times(unit(done), di_ref[...]) + pack_ref[3:4, :]) * 0.5)
    down = times(act, do_ref[...])
    dh, dl = halves(down)
    places = jnp.bitwise_xor(jnp.transpose(parent_ref[...]), flip)
    for j in range(rows // LANES):
        hot = columns_equal(places[:, j : j + 1], coarse)
        store_rows(
            fine_ref,
            last_ref[j * LANES : (j + 1) * LANES, :] + (mm(hot, dh) + mm(hot, dl)),
            parts,
            start=j * LANES,
        )


VMEM = pl.BlockSpec(memory_space=pltpu.VMEM)
SMEM = pl.BlockSpec(memory_space=pltpu.SMEM)


def call(kernel, in_specs, out_shapes, name, scratch=()):
    return pl.pallas_call(
        kernel,
        in_specs=in_specs,
        out_specs=[VMEM] * len(out_shapes),
        out_shape=out_shapes,
        scratch_shapes=scratch,
        name=name,
        compiler_params=pltpu.CompilerParams(vmem_limit_bytes=32 * 2**20),
    )


def shape(*dims, kind=f32):
    return jax.ShapeDtypeStruct(dims, kind)


def kernel_shards(
    fine_state,
    coarse_state,
    fine_senders,
    up_owner,
    up_local,
    coarse_owner,
    coarse_local,
    fine_w_send,
    fine_w_recv,
    fine_bias,
    fine_w_out,
    up_w_in,
    up_bias,
    up_w_out,
    coarse_w_send,
    coarse_w_recv,
    coarse_bias,
    coarse_w_out,
    down_w_in,
    down_bias,
    down_w_out,
):
    peers = lax.axis_size("sp")
    me = lax.axis_index("sp").astype(jnp.int32)
    odd = me % 2
    rows, _, width = fine_state.shape
    count = coarse_state.shape[0]
    parts = width // LANES
    degree = fine_senders.shape[0] // rows
    degree_coarse = coarse_owner.shape[0] // count
    swap = [(i, i ^ 1) for i in range(peers)]
    diag = [(i, (i + 1 if i % 2 else i - 1) % peers) for i in range(peers)]
    rim = HALO * parts

    state = fine_state.reshape(rows * parts, LANES)
    last = (rows - HALO) * parts
    out_swap = lax.dynamic_slice(state, ((1 - odd) * last, 0), (rim, LANES))
    out_diag = lax.dynamic_slice(state, (odd * last, 0), (rim, LANES))

    before = jnp.where(odd == 1, rows, rows + HALO)
    after = jnp.where(odd == 1, rows + HALO, rows)
    index = jnp.where(
        fine_senders < HALO,
        fine_senders + before,
        jnp.where(
            fine_senders < HALO + rows,
            fine_senders - HALO,
            fine_senders - (HALO + rows) + after,
        ),
    )
    index = index.reshape(rows, degree).T.reshape(rows * degree // LANES, LANES)
    parent = up_owner[:, 0] * count + up_local
    anchor = (coarse_owner[:, 0] * count + coarse_local).reshape(count, degree_coarse).T
    anchor_lines = count * degree_coarse // LANES
    anchor = jnp.pad(
        anchor.astype(f32).reshape(anchor_lines, LANES), ((0, 8 - anchor_lines % 8), (0, 0))
    )
    odd_arg, me_arg = odd.reshape(1), me.reshape(1)

    edges, window = rows * degree, rows + 2 * HALO
    parent = parent.reshape(rows // LANES, LANES)
    row = lambda bias: bias.reshape(1, width)
    pair = [(i, (i + 2 if i % 2 else i - 2) % peers) for i in range(peers)]
    full = rows * parts + -(-(edges + rows) // LANES // 8) * 8
    in_swap = lax.ppermute(out_swap, "sp", swap)
    in_diag = lax.ppermute(out_diag, "sp", diag)
    hot, got, into, pack = call(
        functools.partial(near_kernel, True),
        [VMEM] * 8,
        [
            shape(edges, window, kind=bf16), shape(edges, width), shape(rows, width),
            shape(8, width),
        ],
        "near0",
    )(
        state, index, fine_w_send, fine_w_recv, fine_bias, row(up_bias), row(coarse_bias),
        row(down_bias),
    )
    state, out_half = call(
        far_kernel,
        [SMEM] + [VMEM] * 10,
        [shape(full, LANES), shape(rim, LANES)],
        "far0",
    )(odd_arg, in_swap, in_diag, state, hot, got, into, fine_w_send, fine_w_out, index, parent)
    in_swap = lax.ppermute(state, "sp", swap)
    in_pair = lax.ppermute(out_half, "sp", pair)
    in_diag = lax.ppermute(out_half, "sp", diag)
    got, into, high, low = call(
        functools.partial(near_kernel, False),
        [VMEM] * 5,
        [shape(edges, width), shape(rows, width)] + [shape(rows, width, kind=bf16)] * 2,
        "near1",
    )(state, hot, fine_w_send, fine_w_recv, pack)
    hidden, *slots = call(
        functools.partial(up_kernel, peers),
        [SMEM] * 2 + [VMEM] * 16,
        [shape(rows, width)] + [shape(count * parts, LANES)] * (peers // 2),
        "up",
        [pltpu.VMEM((edges, window), bf16)]
        + [pltpu.VMEM((2 * HALO, width), bf16)] * 2
        + [pltpu.VMEM((window, width), bf16)] * 2,
    )(
        odd_arg, me_arg, state, in_swap, in_pair, in_diag, hot, got, into, high, low,
        fine_w_send, fine_w_recv, fine_w_out, parent, up_w_in, up_w_out, pack,
    )
    arrived = [slots[0]] + [
        lax.ppermute(slots[k], "sp", [(i, i ^ (2 * k)) for i in range(peers)])
        for k in range(1, peers // 2)
    ]
    (middle,) = call(
        middle_kernel,
        [VMEM] * (2 + peers // 2),
        [shape(count * parts + anchor.shape[0], LANES)],
        "middle",
    )(coarse_state.reshape(count * parts, LANES), anchor, *arrived)
    columns = {0: middle}
    for k in range(2, peers, 2):
        columns[k] = lax.ppermute(middle, "sp", [(i, i ^ k) for i in range(peers)])
    for k in range(0, peers, 2):
        columns[k + 1] = lax.ppermute(columns[k], "sp", swap)
    fine_out, coarse_out = call(
        functools.partial(coarse_kernel, peers, anchor_lines),
        [SMEM] + [VMEM] * (8 + peers),
        [shape(rows * parts, LANES), shape(count * parts, LANES)],
        "coarse",
    )(
        me_arg, hidden, parent,
        *[columns[k] for k in range(peers)],
        coarse_w_send, coarse_w_recv, coarse_w_out, down_w_in, down_w_out, pack,
    )
    return (fine_out.reshape(fine_state.shape), coarse_out.reshape(coarse_state.shape))


def shards(*args):
    fine_state, coarse_state, fine_senders = args[0], args[1], args[2]
    coarse_owner, layers = args[5], args[7].shape[0]
    peers = lax.axis_size("sp")
    rows, samples, width = fine_state.shape
    count = coarse_state.shape[0]
    fits = (
        samples == 1
        and layers == 2
        and width % LANES == 0
        and peers % 2 == 0
        and peers & (peers - 1) == 0
        and rows % LANES == 0
        and rows >= HALO
        and count & (count - 1) == 0
        and LANES % count == 0
        and coarse_owner.shape[0] % LANES == 0
        and coarse_owner.shape[0] == 4 * count
        and fine_senders.shape[0] % (8 * LANES) == 0
        and peers * count <= 1024
        and peers >= 4
        and rows >= 2 * HALO
    )
    return (kernel_shards if fits else general_shards)(*args)


def solution(mesh):
    in_specs = (
        P("sp", ("grp", "ch"), None),
        P("sp", ("grp", "ch"), None),
        P("sp"),
        P("sp", None),
        P("sp"),
        P("sp", None),
        P("sp"),
    ) + (P(),) * 14
    out_specs = (P("sp", ("grp", "ch"), None), P("sp", ("grp", "ch"), None))
    return jax.shard_map(shards, mesh=mesh, in_specs=in_specs, out_specs=out_specs, check_vma=False)
```

```python
import functools
import jax
import jax.numpy as jnp
from jax import lax
from jax.experimental import pallas as pl
from jax.experimental.pallas import tpu as pltpu
from jax.sharding import PartitionSpec as P

HALO = 128
LANES = 128


epsilon = 1e-05
highest = lax.Precision.HIGHEST


def extended_2(cells, sides, width):
    for axis, dim in sides:
        count = lax.axis_size(axis)
        head = lax.slice_in_dim(cells, 0, width, axis=dim)
        tail = lax.slice_in_dim(cells, cells.shape[dim] - width, cells.shape[dim], axis=dim)
        cells = jnp.concatenate(
            [
                lax.ppermute(tail, axis, [(i, (i + 1) % count) for i in range(count)]),
                cells,
                lax.ppermute(head, axis, [((i + 1) % count, i) for i in range(count)]),
            ],
            axis=dim,
        )
    return cells


def layer_norm(values):
    average = jnp.mean(values, axis=-1, keepdims=True)
    centered = values - average
    spread = jnp.mean(centered * centered, axis=-1, keepdims=True)
    return centered / jnp.sqrt(spread + epsilon)


def project(values, matrix):
    return jnp.einsum(
        "nsd,dh->nsh", values, matrix, precision=highest, preferred_element_type=jnp.float32
    )


def slot_ranks(owners, peer_count):
    matches = (owners[:, None] == jnp.arange(peer_count, dtype=jnp.int32)[None, :]).astype(
        jnp.int32
    )
    ranking = jnp.cumsum(matches, axis=0) - 1
    return jnp.sum(ranking * matches, axis=1)


def general_shards(
    fine_state,
    coarse_state,
    fine_senders,
    up_owner,
    up_local,
    coarse_owner,
    coarse_local,
    fine_w_send,
    fine_w_recv,
    fine_bias,
    fine_w_out,
    up_w_in,
    up_bias,
    up_w_out,
    coarse_w_send,
    coarse_w_recv,
    coarse_bias,
    coarse_w_out,
    down_w_in,
    down_bias,
    down_w_out,
):
    peer_count = lax.axis_size("sp")
    fine_rows = fine_state.shape[0]
    coarse_rows = coarse_state.shape[0]
    samples = fine_state.shape[1]
    feature_width = fine_state.shape[2]
    degree_fine = fine_senders.shape[0] // fine_rows
    degree_coarse = coarse_owner.shape[0] // coarse_rows
    hidden_state = fine_state
    for layer_index in range(fine_w_send.shape[0]):
        normed = layer_norm(hidden_state)
        outward = project(normed, fine_w_send[layer_index])
        inward = project(normed, fine_w_recv[layer_index]) + fine_bias[layer_index]
        extended = extended_2(outward, (("sp", 0),), HALO)
        gathered = extended[fine_senders].reshape(fine_rows, degree_fine, samples, -1)
        summed = jnp.sum(jax.nn.silu(gathered + inward[:, None]), axis=1)
        hidden_state = hidden_state + project(summed, fine_w_out[layer_index])
    capacity = max(4, 2 * fine_rows // peer_count)
    owners = up_owner[:, 0]
    places = owners * capacity + slot_ranks(owners, peer_count)
    targets = (
        jnp.full((peer_count * capacity,), -1.0, jnp.float32)
        .at[places]
        .set(up_local.astype(jnp.float32))
        .reshape(peer_count, capacity)
    )
    activated = jax.nn.silu(project(layer_norm(hidden_state), up_w_in) + up_bias)
    coarse_ids = jnp.arange(coarse_rows, dtype=jnp.float32)[:, None]
    messages = project(activated, up_w_out)
    outgoing = (
        jnp.zeros((peer_count * capacity, samples, feature_width), jnp.float32)
        .at[places]
        .set(messages)
        .reshape(peer_count, capacity, samples, feature_width)
    )
    arrived, sources = (
        lax.all_to_all(outgoing, "sp", split_axis=0, concat_axis=0, tiled=True),
        lax.all_to_all(targets, "sp", split_axis=0, concat_axis=0, tiled=True),
    )
    selector = (sources.reshape(1, -1) == coarse_ids).astype(jnp.float32)
    gained = jnp.einsum(
        "cr,rsd->csd",
        selector,
        arrived.reshape(peer_count * capacity, samples, feature_width),
        precision=highest,
        preferred_element_type=jnp.float32,
    )
    coarse = coarse_state + gained
    normed = layer_norm(coarse)
    outward = project(normed, coarse_w_send)
    inward = project(normed, coarse_w_recv) + coarse_bias
    anchor_owner = coarse_owner[:, 0]
    everything = lax.all_gather(outward, "sp", axis=0, tiled=True)
    picked = everything[anchor_owner * coarse_rows + coarse_local]
    edge_terms = picked.reshape(coarse_rows, degree_coarse, samples, -1)
    summed = jnp.sum(jax.nn.silu(edge_terms + inward[:, None]), axis=1)
    coarse_out = coarse + project(summed, coarse_w_out)
    downward = project(
        jax.nn.silu(project(layer_norm(coarse_out), down_w_in) + down_bias), down_w_out
    )
    wanted = jnp.maximum(sources.reshape(-1), 0.0).astype(jnp.int32)
    replies = downward[wanted].reshape(peer_count, capacity, samples, feature_width)
    answered = lax.all_to_all(replies, "sp", split_axis=0, concat_axis=0, tiled=True)
    fine_out = (
        hidden_state + answered.reshape(peer_count * capacity, samples, feature_width)[places]
    )
    return (fine_out, coarse_out)


f32 = jnp.float32
bf16 = jnp.bfloat16


def load_rows(ref, rows, parts, start=0):
    return jnp.concatenate(
        [ref[pl.ds(start * parts + j, rows, stride=parts), :] for j in range(parts)], axis=1
    )


def store_rows(ref, values, parts, start=0):
    for j in range(parts):
        ref[pl.ds(start * parts + j, values.shape[0], stride=parts), :] = values[
            :, j * LANES : (j + 1) * LANES
        ]


def halves(values):
    high = values.astype(bf16)
    return high, (values - high.astype(f32)).astype(bf16)


def mm(a, b):
    return jnp.dot(a, b, preferred_element_type=f32)


def times(values, high, low):
    vh, vl = halves(values)
    return mm(vh, high) + (mm(vl, high) + mm(vh, low))


def take(one_hot, high, low):
    return mm(one_hot, high) + mm(one_hot, low)


def unit(values):
    width = values.shape[1]
    average = jnp.sum(values, axis=1, keepdims=True) * (1.0 / width)
    centered = values - average
    spread = jnp.sum(centered * centered, axis=1, keepdims=True) * (1.0 / width)
    return centered * lax.rsqrt(spread + epsilon)


def gate(half):
    return half + half * jnp.tanh(half)


def equal(column, count):
    ids = lax.broadcasted_iota(jnp.int32, (column.shape[0], count), 1).astype(f32)
    return jnp.where(ids == column, 1.0, 0.0).astype(bf16)


def turned(lines):
    pad = jnp.zeros((LANES - lines.shape[0], LANES), f32)
    return jnp.transpose(jnp.concatenate([lines, pad], axis=0))


def edge_hot(hot_ref, turn_ref, lines, degree, nodes, flip=None):
    turn_ref[...] = turned(lines)
    step = LANES // degree
    for k in range(degree):
        spread = turn_ref[pl.ds(k, step, stride=degree), :]
        if flip is not None:
            spread = jnp.bitwise_xor(spread.astype(jnp.int32), flip).astype(f32)
        for line in range(lines.shape[0]):
            start = k * nodes + line * step
            hot_ref[start : start + step, :] = equal(
                spread[:, line : line + 1], hot_ref.shape[1]
            )


def split_into(high_ref, low_ref, *matrices):
    for j, matrix in enumerate(matrices):
        size = matrix.shape[0]
        high_ref[j * size : (j + 1) * size, :], low_ref[j * size : (j + 1) * size, :] = halves(
            matrix
        )


def weights(high_ref, low_ref, j):
    size = high_ref.shape[1]
    return high_ref[j * size : (j + 1) * size, :], low_ref[j * size : (j + 1) * size, :]


def start_kernel(
    count, place_ref, state_hbm, coarse_hbm, sender_hbm, owner_hbm, local_hbm, cowner_hbm,
    clocal_hbm, fb_hbm, ub_hbm, cb_hbm, db_hbm,
    state_ref, ints_ref, pack_ref, swap_ref, diag_ref,
    sender_ref, owner_ref, local_ref, cowner_ref, clocal_ref, fb_ref, ub_ref, cb_ref, db_ref,
    sems,
):
    odd = place_ref[0]
    rim = diag_ref.shape[0]
    far = state_hbm.shape[0] - rim
    own = coarse_hbm.shape[0]
    pairs = [
        (sender_hbm, sender_ref),
        (owner_hbm, owner_ref),
        (local_hbm, local_ref),
        (cowner_hbm, cowner_ref),
        (clocal_hbm, clocal_ref),
        (fb_hbm, fb_ref),
        (ub_hbm, ub_ref),
        (cb_hbm, cb_ref),
        (db_hbm, db_ref),
        (state_hbm.at[pl.ds(pl.multiple_of((1 - odd) * far, LANES), rim), :], swap_ref.at[0:rim, :]),
        (state_hbm.at[pl.ds(pl.multiple_of(odd * far, LANES), rim), :], diag_ref),
        (coarse_hbm, swap_ref.at[rim : rim + own, :]),
        (state_hbm, state_ref),
    ]
    copies = [pltpu.make_async_copy(a, b, sems.at[j]) for j, (a, b) in enumerate(pairs)]
    for copy in copies:
        copy.start()
    for copy in copies[:9]:
        copy.wait()
    parts = fb_ref.shape[1] // LANES
    rows = state_hbm.shape[0] // parts
    halo = rim // parts
    sender = sender_ref[...]
    before = rows + (1 - odd) * halo
    after = rows + odd * halo
    index = jnp.where(
        sender < halo,
        sender + before,
        jnp.where(sender < halo + rows, sender - halo, sender - (halo + rows) + after),
    )
    lines = [
        index.astype(f32),
        (owner_ref[...] * count + local_ref[...]).astype(f32),
        (cowner_ref[...] * count + clocal_ref[...]).astype(f32),
    ]
    rest = ints_ref.shape[0] - sum(x.shape[0] for x in lines)
    ints = jnp.concatenate(lines + [jnp.zeros((rest, LANES), f32)], axis=0)
    ints_ref[...] = ints
    swap_ref[rim + own :, :] = ints
    pack_ref[...] = jnp.concatenate(
        [fb_ref[...], ub_ref[...], cb_ref[...], db_ref[...]]
        + [jnp.zeros((3, fb_ref.shape[1]), f32)],
        axis=0,
    )
    for copy in copies[9:]:
        copy.wait()


def near_kernel(
    edges, state_ref, ints_ref, ws_ref, wr_ref, wo_ref, pack_ref,
    hot_ref, got_ref, into_ref, high_ref, low_ref, turn_ref,
):
    rows, width = into_ref.shape
    parts = width // LANES
    split_into(high_ref, low_ref, ws_ref[0], wo_ref[0])
    edge_hot(
        hot_ref, turn_ref, ints_ref[: edges // LANES, :], edges // rows, rows
    )
    normed = unit(load_rows(state_ref, rows, parts))
    into_ref[...] = (times(normed, *halves(wr_ref[0])) + pack_ref[0:1, :]) * 0.5
    high, low = halves(times(normed, *weights(high_ref, low_ref, 0)) * 0.5)
    got_ref[...] = take(hot_ref[:, :rows], high, low)


def far_kernel(
    place_ref, swap_ref, diag_ref, state_ref, hot_ref, got_ref, into_ref, high_ref, low_ref,
    out_full_ref, out_half_ref,
):
    rows, width = into_ref.shape
    parts = width // LANES
    rim = diag_ref.shape[0] // parts
    degree = hot_ref.shape[0] // rows
    far = jnp.concatenate(
        [load_rows(swap_ref, rim, parts), load_rows(diag_ref, rim, parts)], axis=0
    )
    high, low = halves(times(unit(far), *weights(high_ref, low_ref, 0)) * 0.5)
    total = None
    for k in range(degree):
        part = slice(k * rows, (k + 1) * rows)
        half = got_ref[part, :] + into_ref[...] + take(hot_ref[part, rows:], high, low)
        total = gate(half) if total is None else total + gate(half)
    store_rows(
        out_full_ref,
        load_rows(state_ref, rows, parts) + times(total, *weights(high_ref, low_ref, 1)),
        parts,
    )
    lines = out_half_ref.shape[0]
    start = pl.multiple_of(place_ref[0] * (rows * parts - lines), LANES)
    out_half_ref[...] = out_full_ref[pl.ds(start, lines), :]


def near2_kernel(
    edges, place_ref, state_ref, ints_ref, swap_ref, hot_ref, ws_ref, wr_ref, wo_ref, wi_ref,
    wu_ref, pack_ref,
    got_ref, into_ref, own_high_ref, own_low_ref, hot2_ref, select_ref, high_ref, low_ref,
    turn_ref,
):
    rows, width = into_ref.shape
    parts = width // LANES
    senders = edges // LANES
    first = swap_ref.shape[0] - ints_ref.shape[0]
    split_into(
        high_ref, low_ref, ws_ref[1], wr_ref[1], wo_ref[1], wi_ref[...], wu_ref[...]
    )
    normed = unit(load_rows(state_ref, rows, parts))
    into_ref[...] = (times(normed, *weights(high_ref, low_ref, 1)) + pack_ref[1:2, :]) * 0.5
    high, low = halves(times(normed, *weights(high_ref, low_ref, 0)) * 0.5)
    own_high_ref[...] = high
    own_low_ref[...] = low
    got_ref[...] = take(hot_ref[:, :rows], high, low)
    edge_hot(hot2_ref, turn_ref, swap_ref[first : first + senders, :], edges // rows, rows)
    flip = place_ref[1]
    line = senders
    for half, ref, base in ((0, ints_ref, 0), (1, swap_ref, first)):
        for j in range(rows // LANES):
            parent = ref[base + line + j : base + line + j + 1, :].astype(jnp.int32)
            parent = jnp.bitwise_xor(parent, flip)
            ids = lax.broadcasted_iota(jnp.int32, (select_ref.shape[0], LANES), 0)
            start = half * rows + j * LANES
            select_ref[:, start : start + LANES] = jnp.where(ids == parent, 1.0, 0.0).astype(
                bf16
            )


def messages(hidden, high_ref, low_ref, pack_ref):
    act = gate((times(unit(hidden), *weights(high_ref, low_ref, 3)) + pack_ref[2:3, :]) * 0.5)
    return halves(times(act, *weights(high_ref, low_ref, 4)))


def other_kernel(
    place_ref, swap_ref, pair_ref, own_high_ref, own_low_ref, hot_ref, select_ref, high_ref,
    low_ref, pack_ref,
    sums_ref, touch_high_ref, touch_low_ref, th_ref, tl_ref,
):
    rim, width = touch_high_ref.shape
    rows = own_high_ref.shape[0]
    parts = width // LANES
    degree = hot_ref.shape[0] // rows
    odd = place_ref[0]
    mine = pl.multiple_of((1 - odd) * (rows - rim), LANES)
    theirs = pl.multiple_of(odd * (rows - rim), LANES)
    other = load_rows(swap_ref, rows, parts)
    normed = unit(jnp.concatenate([other, load_rows(pair_ref, rim, parts)], axis=0))
    sends = halves(times(normed, *weights(high_ref, low_ref, 0)) * 0.5)
    for src, t_ref, own_ref, touch_ref in (
        (sends[0], th_ref, own_high_ref, touch_high_ref),
        (sends[1], tl_ref, own_low_ref, touch_low_ref),
    ):
        t_ref[:rows, :] = src[:rows, :]
        t_ref[rows : rows + rim, :] = own_ref[pl.ds(mine, rim), :]
        t_ref[rows + rim :, :] = src[rows:, :]
        touch_ref[...] = t_ref[pl.ds(theirs, rim), :]
    into = (times(normed[:rows, :], *weights(high_ref, low_ref, 1)) + pack_ref[1:2, :]) * 0.5
    total = None
    for k in range(degree):
        half = into + take(hot_ref[k * rows : (k + 1) * rows, :], th_ref[...], tl_ref[...])
        total = gate(half) if total is None else total + gate(half)
    hidden = other + times(total, *weights(high_ref, low_ref, 2))
    sums_ref[...] = take(select_ref[:, rows:], *messages(hidden, high_ref, low_ref, pack_ref))


def own_kernel(
    diag_ref, state_ref, hot_ref, got_ref, into_ref, touch_high_ref, touch_low_ref, sums_ref,
    select_ref, ints_ref, swap_ref, high_ref, low_ref, pack_ref,
    last_ref, *slot_refs,
):
    rows, width = into_ref.shape
    parts = width // LANES
    rim = diag_ref.shape[0] // parts
    degree = hot_ref.shape[0] // rows
    high, low = halves(
        times(unit(load_rows(diag_ref, rim, parts)), *weights(high_ref, low_ref, 0)) * 0.5
    )
    high = jnp.concatenate([touch_high_ref[...], high], axis=0)
    low = jnp.concatenate([touch_low_ref[...], low], axis=0)
    total = None
    for k in range(degree):
        part = slice(k * rows, (k + 1) * rows)
        half = got_ref[part, :] + into_ref[...] + take(hot_ref[part, rows:], high, low)
        total = gate(half) if total is None else total + gate(half)
    hidden = load_rows(state_ref, rows, parts) + times(total, *weights(high_ref, low_ref, 2))
    last_ref[...] = hidden
    sums = sums_ref[...] + take(
        select_ref[:, :rows], *messages(hidden, high_ref, low_ref, pack_ref)
    )
    size = sums.shape[0] // len(slot_refs)
    first = hot_ref.shape[0] // LANES + rows // LANES
    base = swap_ref.shape[0] - ints_ref.shape[0]
    anchor = (slot_refs[0].shape[0] - size * parts) // 4
    for j, slot in enumerate(slot_refs):
        store_rows(slot, sums[j * size : (j + 1) * size, :], parts)
        slot[size * parts :, :] = jnp.concatenate(
            [
                ints_ref[first : first + anchor, :],
                swap_ref[base + first : base + first + anchor, :],
                jnp.zeros((2 * anchor, LANES), f32),
            ],
            axis=0,
        )


def middle_kernel(state_ref, swap_ref, *refs):
    out_ref = refs[-1]
    own = state_ref.shape[0]
    lines = out_ref.shape[0]
    rim = swap_ref.shape[0] - own - 16
    total = jnp.concatenate([state_ref[...], swap_ref[rim : rim + own, :]], axis=0)
    for ref in refs[:-1]:
        total = total + ref[:lines, :]
    out_ref[...] = total


def edges_kernel(
    degree, rows, place_ref, ints_ref, cs_ref, cr_ref, co_ref, di_ref, do_ref, *refs
):
    *slot_refs, hot_ref, parent_ref, high_ref, low_ref, turn_ref = refs
    coarse = hot_ref.shape[1]
    flip = place_ref[1]
    split_into(
        high_ref, low_ref, cs_ref[...], cr_ref[...], co_ref[...], di_ref[...], do_ref[...]
    )
    count = coarse * degree // LANES // len(slot_refs)
    lines = jnp.concatenate(
        [ref[ref.shape[0] - 2 * count : ref.shape[0] - count, :] for ref in slot_refs], axis=0
    )
    edge_hot(hot_ref, turn_ref, lines, degree, coarse, flip)
    columns = turned(ints_ref[...])
    first = ints_ref.shape[0] // 2
    for j in range(rows // LANES):
        column = jnp.bitwise_xor(
            columns[:, first + j : first + j + 1].astype(jnp.int32), flip
        ).astype(f32)
        parent_ref[j * LANES : (j + 1) * LANES, :] = equal(column, coarse)


def coarse_kernel(last_ref, hot_ref, parent_ref, high_ref, low_ref, pack_ref, *refs):
    *blocks, fine_ref, coarse_ref = refs
    rows, width = last_ref.shape
    parts = width // LANES
    coarse = hot_ref.shape[1]
    each = coarse // len(blocks)
    middle = jnp.concatenate([load_rows(b, each, parts) for b in blocks], axis=0)
    normed = unit(middle)
    high, low = halves(times(normed, *weights(high_ref, low_ref, 0)) * 0.5)
    into = (times(normed, *weights(high_ref, low_ref, 1)) + pack_ref[3:4, :]) * 0.5
    total = None
    for k in range(hot_ref.shape[0] // coarse):
        half = into + take(hot_ref[k * coarse : (k + 1) * coarse, :], high, low)
        total = gate(half) if total is None else total + gate(half)
    done = middle + times(total, *weights(high_ref, low_ref, 2))
    store_rows(coarse_ref, done[: coarse_ref.shape[0] // parts, :], parts)
    act = gate((times(unit(done), *weights(high_ref, low_ref, 3)) + pack_ref[4:5, :]) * 0.5)
    down = halves(times(act, *weights(high_ref, low_ref, 4)))
    store_rows(fine_ref, last_ref[...] + take(parent_ref[...], *down), parts)


VMEM = pl.BlockSpec(memory_space=pltpu.VMEM)
SMEM = pl.BlockSpec(memory_space=pltpu.SMEM)
HBM = pl.BlockSpec(memory_space=pltpu.HBM)


def call(kernel, in_specs, out_shapes, name, scratch=()):
    return pl.pallas_call(
        kernel,
        in_specs=in_specs,
        out_specs=[VMEM] * len(out_shapes),
        out_shape=out_shapes,
        scratch_shapes=scratch,
        name=name,
        compiler_params=pltpu.CompilerParams(vmem_limit_bytes=32 * 2**20),
    )


def shape(*dims, kind=f32):
    return jax.ShapeDtypeStruct(dims, kind)


def kernel_shards(
    fine_state,
    coarse_state,
    fine_senders,
    up_owner,
    up_local,
    coarse_owner,
    coarse_local,
    fine_w_send,
    fine_w_recv,
    fine_bias,
    fine_w_out,
    up_w_in,
    up_bias,
    up_w_out,
    coarse_w_send,
    coarse_w_recv,
    coarse_bias,
    coarse_w_out,
    down_w_in,
    down_bias,
    down_w_out,
):
    peers = lax.axis_size("sp")
    me = lax.axis_index("sp").astype(jnp.int32)
    rows, _, width = fine_state.shape
    count = coarse_state.shape[0]
    parts = width // LANES
    edges = fine_senders.shape[0]
    coarse_edges = coarse_owner.shape[0]
    coarse = peers * count
    window = rows + 2 * HALO
    rim, own, full = HALO * parts, count * parts, rows * parts
    size = width
    swap = [(i, i ^ 1) for i in range(peers)]
    diag = [(i, (i + 1 if i % 2 else i - 1) % peers) for i in range(peers)]
    pair = [(i, (i + 2 if i % 2 else i - 2) % peers) for i in range(peers)]
    flips = [[(i, i ^ (2 * j)) for i in range(peers)] for j in range(peers // 2)]
    place = jnp.stack([me % 2, me * count])
    lines = lambda x: x.reshape(-1, LANES)
    row = lambda x: x.reshape(1, width)
    turn = pltpu.VMEM((LANES, LANES), f32)
    hot_shape = shape(edges, window, kind=bf16)
    small = lambda ref: pltpu.VMEM(ref.shape, ref.dtype)

    small_args = [
        lines(fine_senders), lines(up_owner), lines(up_local), lines(coarse_owner),
        lines(coarse_local), fine_bias, row(up_bias), row(coarse_bias), row(down_bias),
    ]
    state, ints, pack, out_swap, out_diag = call(
        functools.partial(start_kernel, count),
        [SMEM] + [HBM] * 11,
        [
            shape(full, LANES), shape(16, LANES), shape(8, width),
            shape(rim + own + 16, LANES), shape(rim, LANES),
        ],
        "start",
        [small(x) for x in small_args] + [pltpu.SemaphoreType.DMA((13,))],
    )(place, lines(fine_state), lines(coarse_state), *small_args)
    swap0 = lax.ppermute(out_swap, "sp", swap)
    diag0 = lax.ppermute(out_diag, "sp", diag)
    hot, got, into, high, low = call(
        functools.partial(near_kernel, edges),
        [VMEM] * 6,
        [hot_shape, shape(edges, width), shape(rows, width)]
        + [shape(2 * size, width, kind=bf16)] * 2,
        "near0",
        [turn],
    )(state, ints, fine_w_send, fine_w_recv, fine_w_out, pack)
    state, out_half = call(
        far_kernel,
        [SMEM] + [VMEM] * 8,
        [shape(full, LANES), shape(rim, LANES)],
        "far0",
    )(place, swap0, diag0, state, hot, got, into, high, low)
    swap1 = lax.ppermute(state, "sp", swap)
    diag1 = lax.ppermute(out_half, "sp", diag)
    pair1 = lax.ppermute(out_half, "sp", pair)
    got, into, own_high, own_low, hot2, select, high, low = call(
        functools.partial(near2_kernel, edges),
        [SMEM] + [VMEM] * 10,
        [shape(edges, width), shape(rows, width)]
        + [shape(rows, width, kind=bf16)] * 2
        + [hot_shape, shape(coarse, 2 * rows, kind=bf16)]
        + [shape(5 * size, width, kind=bf16)] * 2,
        "near1",
        [turn],
    )(
        place, state, ints, swap0, hot, fine_w_send, fine_w_recv, fine_w_out, up_w_in, up_w_out,
        pack,
    )
    sums, touch_high, touch_low = call(
        other_kernel,
        [SMEM] + [VMEM] * 9,
        [shape(coarse, width)] + [shape(HALO, width, kind=bf16)] * 2,
        "other",
        [pltpu.VMEM((window, width), bf16)] * 2,
    )(place, swap1, pair1, own_high, own_low, hot2, select, high, low, pack)
    hidden, *slots = call(
        own_kernel,
        [VMEM] * 14,
        [shape(rows, width)]
        + [shape(2 * own + 8 * coarse_edges // 256, LANES)] * (peers // 2),
        "own",
    )(
        diag1, state, hot, got, into, touch_high, touch_low, sums, select, ints, swap0, high,
        low, pack,
    )
    arrived = [slots[0]] + [
        lax.ppermute(slots[j], "sp", flips[j]) for j in range(1, peers // 2)
    ]
    (middle,) = call(
        middle_kernel,
        [VMEM] * (2 + peers // 2),
        [shape(2 * own, LANES)],
        "middle",
    )(lines(coarse_state), swap0, *arrived)
    blocks = [middle] + [lax.ppermute(middle, "sp", flips[j]) for j in range(1, peers // 2)]
    coarse_hot, parent_hot, high, low = call(
        functools.partial(edges_kernel, coarse_edges // count, rows),
        [SMEM] + [VMEM] * (6 + peers // 2),
        [
            shape(coarse_edges // count * coarse, coarse, kind=bf16),
            shape(rows, coarse, kind=bf16),
        ]
        + [shape(5 * size, width, kind=bf16)] * 2,
        "edges",
        [turn],
    )(
        place, ints, coarse_w_send, coarse_w_recv, coarse_w_out, down_w_in, down_w_out, *arrived
    )
    fine_out, coarse_out = call(
        coarse_kernel,
        [VMEM] * (6 + peers // 2),
        [shape(full, LANES), shape(own, LANES)],
        "coarse",
    )(hidden, coarse_hot, parent_hot, high, low, pack, *blocks)
    return (fine_out.reshape(fine_state.shape), coarse_out.reshape(coarse_state.shape))


def shards(*args):
    fine_state, coarse_state, fine_senders = args[0], args[1], args[2]
    coarse_owner, layers = args[5], args[7].shape[0]
    peers = lax.axis_size("sp")
    rows, samples, width = fine_state.shape
    count = coarse_state.shape[0]
    fits = (
        samples == 1
        and layers == 2
        and width % LANES == 0
        and peers % 2 == 0
        and peers & (peers - 1) == 0
        and rows % LANES == 0
        and rows >= HALO
        and count & (count - 1) == 0
        and LANES % count == 0
        and coarse_owner.shape[0] % LANES == 0
        and coarse_owner.shape[0] == 4 * count
        and fine_senders.shape[0] == 8 * LANES
        and rows == 2 * LANES
        and coarse_owner.shape[0] == 2 * LANES
        and width == args[7].shape[2]
        and peers * count <= 1024
        and peers >= 4
        and rows >= 2 * HALO
    )
    return (kernel_shards if fits else general_shards)(*args)


def solution(mesh):
    in_specs = (
        P("sp", ("grp", "ch"), None),
        P("sp", ("grp", "ch"), None),
        P("sp"),
        P("sp", None),
        P("sp"),
        P("sp", None),
        P("sp"),
    ) + (P(),) * 14
    out_specs = (P("sp", ("grp", "ch"), None), P("sp", ("grp", "ch"), None))
    return jax.shard_map(shards, mesh=mesh, in_specs=in_specs, out_specs=out_specs, check_vma=False)
```

```python
import functools
import jax
import jax.numpy as jnp
from jax import lax
from jax.experimental import pallas as pl
from jax.experimental.pallas import tpu as pltpu
from jax.sharding import PartitionSpec as P

HALO = 128
LANES = 128


epsilon = 1e-05
highest = lax.Precision.HIGHEST


def extended_2(cells, sides, width):
    for axis, dim in sides:
        count = lax.axis_size(axis)
        head = lax.slice_in_dim(cells, 0, width, axis=dim)
        tail = lax.slice_in_dim(cells, cells.shape[dim] - width, cells.shape[dim], axis=dim)
        cells = jnp.concatenate(
            [
                lax.ppermute(tail, axis, [(i, (i + 1) % count) for i in range(count)]),
                cells,
                lax.ppermute(head, axis, [((i + 1) % count, i) for i in range(count)]),
            ],
            axis=dim,
        )
    return cells


def layer_norm(values):
    average = jnp.mean(values, axis=-1, keepdims=True)
    centered = values - average
    spread = jnp.mean(centered * centered, axis=-1, keepdims=True)
    return centered / jnp.sqrt(spread + epsilon)


def project(values, matrix):
    return jnp.einsum(
        "nsd,dh->nsh", values, matrix, precision=highest, preferred_element_type=jnp.float32
    )


def slot_ranks(owners, peer_count):
    matches = (owners[:, None] == jnp.arange(peer_count, dtype=jnp.int32)[None, :]).astype(
        jnp.int32
    )
    ranking = jnp.cumsum(matches, axis=0) - 1
    return jnp.sum(ranking * matches, axis=1)


def general_shards(
    fine_state,
    coarse_state,
    fine_senders,
    up_owner,
    up_local,
    coarse_owner,
    coarse_local,
    fine_w_send,
    fine_w_recv,
    fine_bias,
    fine_w_out,
    up_w_in,
    up_bias,
    up_w_out,
    coarse_w_send,
    coarse_w_recv,
    coarse_bias,
    coarse_w_out,
    down_w_in,
    down_bias,
    down_w_out,
):
    peer_count = lax.axis_size("sp")
    fine_rows = fine_state.shape[0]
    coarse_rows = coarse_state.shape[0]
    samples = fine_state.shape[1]
    feature_width = fine_state.shape[2]
    degree_fine = fine_senders.shape[0] // fine_rows
    degree_coarse = coarse_owner.shape[0] // coarse_rows
    hidden_state = fine_state
    for layer_index in range(fine_w_send.shape[0]):
        normed = layer_norm(hidden_state)
        outward = project(normed, fine_w_send[layer_index])
        inward = project(normed, fine_w_recv[layer_index]) + fine_bias[layer_index]
        extended = extended_2(outward, (("sp", 0),), HALO)
        gathered = extended[fine_senders].reshape(fine_rows, degree_fine, samples, -1)
        summed = jnp.sum(jax.nn.silu(gathered + inward[:, None]), axis=1)
        hidden_state = hidden_state + project(summed, fine_w_out[layer_index])
    capacity = max(4, 2 * fine_rows // peer_count)
    owners = up_owner[:, 0]
    places = owners * capacity + slot_ranks(owners, peer_count)
    targets = (
        jnp.full((peer_count * capacity,), -1.0, jnp.float32)
        .at[places]
        .set(up_local.astype(jnp.float32))
        .reshape(peer_count, capacity)
    )
    activated = jax.nn.silu(project(layer_norm(hidden_state), up_w_in) + up_bias)
    coarse_ids = jnp.arange(coarse_rows, dtype=jnp.float32)[:, None]
    messages = project(activated, up_w_out)
    outgoing = (
        jnp.zeros((peer_count * capacity, samples, feature_width), jnp.float32)
        .at[places]
        .set(messages)
        .reshape(peer_count, capacity, samples, feature_width)
    )
    arrived, sources = (
        lax.all_to_all(outgoing, "sp", split_axis=0, concat_axis=0, tiled=True),
        lax.all_to_all(targets, "sp", split_axis=0, concat_axis=0, tiled=True),
    )
    selector = (sources.reshape(1, -1) == coarse_ids).astype(jnp.float32)
    gained = jnp.einsum(
        "cr,rsd->csd",
        selector,
        arrived.reshape(peer_count * capacity, samples, feature_width),
        precision=highest,
        preferred_element_type=jnp.float32,
    )
    coarse = coarse_state + gained
    normed = layer_norm(coarse)
    outward = project(normed, coarse_w_send)
    inward = project(normed, coarse_w_recv) + coarse_bias
    anchor_owner = coarse_owner[:, 0]
    everything = lax.all_gather(outward, "sp", axis=0, tiled=True)
    picked = everything[anchor_owner * coarse_rows + coarse_local]
    edge_terms = picked.reshape(coarse_rows, degree_coarse, samples, -1)
    summed = jnp.sum(jax.nn.silu(edge_terms + inward[:, None]), axis=1)
    coarse_out = coarse + project(summed, coarse_w_out)
    downward = project(
        jax.nn.silu(project(layer_norm(coarse_out), down_w_in) + down_bias), down_w_out
    )
    wanted = jnp.maximum(sources.reshape(-1), 0.0).astype(jnp.int32)
    replies = downward[wanted].reshape(peer_count, capacity, samples, feature_width)
    answered = lax.all_to_all(replies, "sp", split_axis=0, concat_axis=0, tiled=True)
    fine_out = (
        hidden_state + answered.reshape(peer_count * capacity, samples, feature_width)[places]
    )
    return (fine_out, coarse_out)


f32 = jnp.float32
bf16 = jnp.bfloat16


def load_rows(ref, rows, parts, start=0):
    return jnp.concatenate(
        [ref[pl.ds(start * parts + j, rows, stride=parts), :] for j in range(parts)], axis=1
    )


def store_rows(ref, values, parts, start=0):
    for j in range(parts):
        ref[pl.ds(start * parts + j, values.shape[0], stride=parts), :] = values[
            :, j * LANES : (j + 1) * LANES
        ]


def halves(values):
    high = values.astype(bf16)
    return high, (values - high.astype(f32)).astype(bf16)


def mm(a, b):
    return jnp.dot(a, b, preferred_element_type=f32)


def times(values, high, low):
    vh, vl = halves(values)
    return mm(vh, high) + (mm(vl, high) + mm(vh, low))


def take(one_hot, high, low):
    return mm(one_hot, high) + mm(one_hot, low)


def unit(values):
    width = values.shape[1]
    average = jnp.sum(values, axis=1, keepdims=True) * (1.0 / width)
    centered = values - average
    spread = jnp.sum(centered * centered, axis=1, keepdims=True) * (1.0 / width)
    return centered * lax.rsqrt(spread + epsilon)


def gate(half):
    return half + half * jnp.tanh(half)


def equal(column, count):
    ids = lax.broadcasted_iota(jnp.int32, (column.shape[0], count), 1).astype(f32)
    return jnp.where(ids == column, 1.0, 0.0).astype(bf16)


def turned(lines):
    pad = jnp.zeros((LANES - lines.shape[0], LANES), f32)
    return jnp.transpose(jnp.concatenate([lines, pad], axis=0))


def edge_hot(hot_ref, turn_ref, lines, degree, nodes, flip=None):
    turn_ref[...] = turned(lines)
    step = LANES // degree
    for k in range(degree):
        spread = turn_ref[pl.ds(k, step, stride=degree), :]
        if flip is not None:
            spread = jnp.bitwise_xor(spread.astype(jnp.int32), flip).astype(f32)
        for line in range(lines.shape[0]):
            start = k * nodes + line * step
            hot_ref[start : start + step, :] = equal(
                spread[:, line : line + 1], hot_ref.shape[1]
            )


def split_into(high_ref, low_ref, *matrices):
    for j, matrix in enumerate(matrices):
        size = matrix.shape[0]
        high_ref[j * size : (j + 1) * size, :], low_ref[j * size : (j + 1) * size, :] = halves(
            matrix
        )


def weights(high_ref, low_ref, j):
    size = high_ref.shape[1]
    return high_ref[j * size : (j + 1) * size, :], low_ref[j * size : (j + 1) * size, :]


def start_kernel(
    count, place_ref, state_hbm, sender_hbm, owner_hbm, local_hbm, cowner_hbm,
    clocal_hbm, fb_hbm, ub_hbm, cb_hbm, db_hbm,
    state_ref, ints_ref, pack_ref, swap_ref, diag_ref,
    sender_ref, owner_ref, local_ref, cowner_ref, clocal_ref, fb_ref, ub_ref, cb_ref, db_ref,
    sems,
):
    odd = place_ref[0]
    rim = diag_ref.shape[0]
    far = state_hbm.shape[0] - rim
    pairs = [
        (sender_hbm, sender_ref),
        (owner_hbm, owner_ref),
        (local_hbm, local_ref),
        (cowner_hbm, cowner_ref),
        (clocal_hbm, clocal_ref),
        (fb_hbm, fb_ref),
        (ub_hbm, ub_ref),
        (cb_hbm, cb_ref),
        (db_hbm, db_ref),
        (state_hbm.at[pl.ds(pl.multiple_of((1 - odd) * far, LANES), rim), :], swap_ref.at[0:rim, :]),
        (state_hbm.at[pl.ds(pl.multiple_of(odd * far, LANES), rim), :], diag_ref),
        (state_hbm, state_ref),
    ]
    copies = [pltpu.make_async_copy(a, b, sems.at[j]) for j, (a, b) in enumerate(pairs)]
    for copy in copies:
        copy.start()
    for copy in copies[:9]:
        copy.wait()
    parts = fb_ref.shape[1] // LANES
    rows = state_hbm.shape[0] // parts
    halo = rim // parts
    sender = sender_ref[...]
    before = rows + (1 - odd) * halo
    after = rows + odd * halo
    index = jnp.where(
        sender < halo,
        sender + before,
        jnp.where(sender < halo + rows, sender - halo, sender - (halo + rows) + after),
    )
    lines = [
        index.astype(f32),
        (owner_ref[...] * count + local_ref[...]).astype(f32),
        (cowner_ref[...] * count + clocal_ref[...]).astype(f32),
    ]
    rest = ints_ref.shape[0] - sum(x.shape[0] for x in lines)
    ints = jnp.concatenate(lines + [jnp.zeros((rest, LANES), f32)], axis=0)
    ints_ref[...] = ints
    swap_ref[rim:, :] = ints
    pack_ref[...] = jnp.concatenate(
        [fb_ref[...], ub_ref[...], cb_ref[...], db_ref[...]]
        + [jnp.zeros((3, fb_ref.shape[1]), f32)],
        axis=0,
    )
    for copy in copies[9:]:
        copy.wait()


def near_kernel(
    edges, state_ref, ints_ref, ws_hbm, wr_hbm, wo_hbm, pack_ref,
    hot_ref, got_ref, into_ref, high_ref, low_ref, turn_ref, ws_ref, wr_ref, wo_ref, sems,
):
    rows, width = into_ref.shape
    parts = width // LANES
    pairs = ((ws_hbm, ws_ref), (wr_hbm, wr_ref), (wo_hbm, wo_ref))
    copies = [
        pltpu.make_async_copy(a.at[0], b, sems.at[j]) for j, (a, b) in enumerate(pairs)
    ]
    for copy in copies:
        copy.start()
    edge_hot(hot_ref, turn_ref, ints_ref[: edges // LANES, :], edges // rows, rows)
    normed = unit(load_rows(state_ref, rows, parts))
    for copy in copies:
        copy.wait()
    split_into(high_ref, low_ref, ws_ref[...], wo_ref[...])
    into_ref[...] = (times(normed, *halves(wr_ref[...])) + pack_ref[0:1, :]) * 0.5
    high, low = halves(times(normed, *weights(high_ref, low_ref, 0)) * 0.5)
    got_ref[...] = take(hot_ref[:, :rows], high, low)


def far_kernel(
    place_ref, swap_ref, diag_ref, state_ref, hot_ref, got_ref, into_ref, high_ref, low_ref,
    out_full_ref, out_half_ref,
):
    rows, width = into_ref.shape
    parts = width // LANES
    rim = diag_ref.shape[0] // parts
    degree = hot_ref.shape[0] // rows
    far = jnp.concatenate(
        [load_rows(swap_ref, rim, parts), load_rows(diag_ref, rim, parts)], axis=0
    )
    high, low = halves(times(unit(far), *weights(high_ref, low_ref, 0)) * 0.5)
    total = None
    for k in range(degree):
        part = slice(k * rows, (k + 1) * rows)
        half = got_ref[part, :] + into_ref[...] + take(hot_ref[part, rows:], high, low)
        total = gate(half) if total is None else total + gate(half)
    store_rows(
        out_full_ref,
        load_rows(state_ref, rows, parts) + times(total, *weights(high_ref, low_ref, 1)),
        parts,
    )
    lines = out_half_ref.shape[0]
    start = pl.multiple_of(place_ref[0] * (rows * parts - lines), LANES)
    out_half_ref[...] = out_full_ref[pl.ds(start, lines), :]


def near2_kernel(
    edges, count, place_ref, state_ref, ints_ref, swap_ref, hot_ref, ws_ref, wr_ref, wo_ref, wi_ref,
    wu_ref, pack_ref,
    got_ref, into_ref, own_high_ref, own_low_ref, hot2_ref, select_ref, high_ref, low_ref,
    turn_ref,
):
    rows, width = into_ref.shape
    parts = width // LANES
    senders = edges // LANES
    first = swap_ref.shape[0] - ints_ref.shape[0]
    split_into(
        high_ref, low_ref, ws_ref[1], wr_ref[1], wo_ref[1], wi_ref[...], wu_ref[...]
    )
    normed = unit(load_rows(state_ref, rows, parts))
    into_ref[...] = (times(normed, *weights(high_ref, low_ref, 1)) + pack_ref[1:2, :]) * 0.5
    high, low = halves(times(normed, *weights(high_ref, low_ref, 0)) * 0.5)
    own_high_ref[...] = high
    own_low_ref[...] = low
    got_ref[...] = take(hot_ref[:, :rows], high, low)
    edge_hot(hot2_ref, turn_ref, swap_ref[first : first + senders, :], edges // rows, rows)
    flip = place_ref[1]
    line = senders
    for half, ref, base in ((0, ints_ref, 0), (1, swap_ref, first)):
        for j in range(rows // LANES):
            parent = ref[base + line + j : base + line + j + 1, :].astype(jnp.int32)
            parent = jnp.bitwise_xor(parent, flip)
            ids = lax.broadcasted_iota(jnp.int32, (select_ref.shape[0], LANES), 0)
            ids = ids + jnp.bitwise_and(ids, -count)
            start = half * rows + j * LANES
            select_ref[:, start : start + LANES] = jnp.where(ids == parent, 1.0, 0.0).astype(
                bf16
            )


def up_kernel(
    place_ref, swap_ref, pair_ref, diag_ref, state_ref, hot_ref, got_ref, into_ref, own_high_ref,
    own_low_ref, hot2_ref, select_ref, ints_ref, swap0_ref, high_ref, low_ref, pack_ref,
    last_ref, *refs,
):
    *slot_refs, th_ref, tl_ref = refs
    rows, width = into_ref.shape
    parts = width // LANES
    rim = diag_ref.shape[0] // parts
    degree = hot_ref.shape[0] // rows
    odd = place_ref[0]
    mine = pl.multiple_of((1 - odd) * (rows - rim), LANES)
    theirs = pl.multiple_of(odd * (rows - rim), LANES)
    other = load_rows(swap_ref, rows, parts)
    normed = unit(
        jnp.concatenate(
            [other, load_rows(pair_ref, rim, parts), load_rows(diag_ref, rim, parts)], axis=0
        )
    )
    sends = halves(times(normed, *weights(high_ref, low_ref, 0)) * 0.5)
    near = []
    for src, t_ref, own_ref in (
        (sends[0], th_ref, own_high_ref), (sends[1], tl_ref, own_low_ref),
    ):
        t_ref[:rows, :] = src[:rows, :]
        t_ref[rows : rows + rim, :] = own_ref[pl.ds(mine, rim), :]
        t_ref[rows + rim :, :] = src[rows : rows + rim, :]
        near.append(
            jnp.concatenate([t_ref[pl.ds(theirs, rim), :], src[rows + rim :, :]], axis=0)
        )
    into = (times(normed[:rows, :], *weights(high_ref, low_ref, 1)) + pack_ref[1:2, :]) * 0.5
    total, total2 = None, None
    for k in range(degree):
        part = slice(k * rows, (k + 1) * rows)
        half = got_ref[part, :] + into_ref[...] + take(hot_ref[part, rows:], *near)
        total = gate(half) if total is None else total + gate(half)
        half = into + take(hot2_ref[part, :], th_ref[...], tl_ref[...])
        total2 = gate(half) if total2 is None else total2 + gate(half)
    hidden = jnp.concatenate([load_rows(state_ref, rows, parts), other], axis=0) + times(
        jnp.concatenate([total, total2], axis=0), *weights(high_ref, low_ref, 2)
    )
    last_ref[...] = hidden[:rows, :]
    act = gate((times(unit(hidden), *weights(high_ref, low_ref, 3)) + pack_ref[2:3, :]) * 0.5)
    sums = take(select_ref[...], *halves(times(act, *weights(high_ref, low_ref, 4))))
    size = sums.shape[0] // len(slot_refs)
    first = hot_ref.shape[0] // LANES + rows // LANES
    base = swap0_ref.shape[0] - ints_ref.shape[0]
    anchor = (slot_refs[0].shape[0] - size * parts) // 4
    for j, slot in enumerate(slot_refs):
        store_rows(slot, sums[j * size : (j + 1) * size, :], parts)
        slot[size * parts :, :] = jnp.concatenate(
            [
                ints_ref[first : first + anchor, :],
                swap0_ref[base + first : base + first + anchor, :],
                jnp.zeros((2 * anchor, LANES), f32),
            ],
            axis=0,
        )


def middle_kernel(state_ref, *refs):
    out_ref = refs[-1]
    total = state_ref[...]
    for ref in refs[:-1]:
        total = total + ref[: out_ref.shape[0], :]
    out_ref[...] = total


def edges_kernel(
    degree, count, place_ref, ints_ref, cs_ref, cr_ref, co_ref, di_ref, do_ref, *refs
):
    *slot_refs, hot_ref, parent_ref, high_ref, low_ref, turn_ref = refs
    rows, coarse = parent_ref.shape
    flip = place_ref[1]
    split_into(
        high_ref, low_ref, cs_ref[...], cr_ref[...], co_ref[...], di_ref[...], do_ref[...]
    )
    columns = turned(ints_ref[...])
    first = ints_ref.shape[0] // 2
    for j in range(rows // LANES):
        column = jnp.bitwise_xor(
            columns[:, first + j : first + j + 1].astype(jnp.int32), flip
        ).astype(f32)
        parent_ref[j * LANES : (j + 1) * LANES, :] = equal(column, coarse)
    here = coarse * degree // LANES // len(slot_refs)
    lines = jnp.concatenate(
        [ref[ref.shape[0] - 2 * here : ref.shape[0] - here, :] for ref in slot_refs], axis=0
    )
    turn_ref[...] = turned(lines)
    step = LANES // degree
    lane = lax.broadcasted_iota(jnp.int32, (coarse, LANES), 1)
    table = jnp.zeros((coarse, LANES), f32)
    each = hot_ref.shape[0] // degree
    for k in range(degree):
        spread = jnp.bitwise_xor(
            turn_ref[pl.ds(k, step, stride=degree), :].astype(jnp.int32), flip
        )
        column = jnp.concatenate([spread[:, j : j + 1] for j in range(lines.shape[0])], axis=0)
        hot_ref[k * each : k * each + count, :] = equal(column[:count, :].astype(f32), coarse)
        high = jnp.right_shift(column, 8).astype(f32)
        low = jnp.bitwise_and(column, 255).astype(f32)
        table = jnp.where(lane == k, high, jnp.where(lane == degree + k, low, table))
    found = mm(parent_ref[...], table.astype(bf16))
    for k in range(degree):
        column = found[:, k : k + 1] * 256.0 + found[:, degree + k : degree + k + 1]
        hot_ref[k * each + count : (k + 1) * each, :] = equal(column, coarse)


def coarse_kernel(last_ref, hot_ref, parent_ref, high_ref, low_ref, pack_ref, *refs):
    *blocks, fine_ref, coarse_ref = refs
    rows, width = last_ref.shape
    parts = width // LANES
    count = coarse_ref.shape[0] // parts
    need = count + rows
    middle = jnp.concatenate([load_rows(b, count, parts) for b in blocks], axis=0)
    sends = halves(times(unit(middle), *weights(high_ref, low_ref, 0)) * 0.5)
    wanted = jnp.concatenate(
        [middle[:count, :], take(parent_ref[...], *halves(middle))], axis=0
    )
    into = (times(unit(wanted), *weights(high_ref, low_ref, 1)) + pack_ref[3:4, :]) * 0.5
    total = None
    for k in range(hot_ref.shape[0] // need):
        half = into + take(hot_ref[k * need : (k + 1) * need, :], *sends)
        total = gate(half) if total is None else total + gate(half)
    done = wanted + times(total, *weights(high_ref, low_ref, 2))
    store_rows(coarse_ref, done[:count, :], parts)
    act = gate(
        (times(unit(done[count:, :]), *weights(high_ref, low_ref, 3)) + pack_ref[4:5, :]) * 0.5
    )
    store_rows(fine_ref, last_ref[...] + times(act, *weights(high_ref, low_ref, 4)), parts)


VMEM = pl.BlockSpec(memory_space=pltpu.VMEM)
SMEM = pl.BlockSpec(memory_space=pltpu.SMEM)
HBM = pl.BlockSpec(memory_space=pltpu.HBM)


def call(kernel, in_specs, out_shapes, name, scratch=()):
    return pl.pallas_call(
        kernel,
        in_specs=in_specs,
        out_specs=[VMEM] * len(out_shapes),
        out_shape=out_shapes,
        scratch_shapes=scratch,
        name=name,
        compiler_params=pltpu.CompilerParams(vmem_limit_bytes=32 * 2**20),
    )


def shape(*dims, kind=f32):
    return jax.ShapeDtypeStruct(dims, kind)


def kernel_shards(
    fine_state,
    coarse_state,
    fine_senders,
    up_owner,
    up_local,
    coarse_owner,
    coarse_local,
    fine_w_send,
    fine_w_recv,
    fine_bias,
    fine_w_out,
    up_w_in,
    up_bias,
    up_w_out,
    coarse_w_send,
    coarse_w_recv,
    coarse_bias,
    coarse_w_out,
    down_w_in,
    down_bias,
    down_w_out,
):
    peers = lax.axis_size("sp")
    me = lax.axis_index("sp").astype(jnp.int32)
    rows, _, width = fine_state.shape
    count = coarse_state.shape[0]
    parts = width // LANES
    edges = fine_senders.shape[0]
    coarse_edges = coarse_owner.shape[0]
    coarse = peers * count
    window = rows + 2 * HALO
    rim, own, full = HALO * parts, count * parts, rows * parts
    size = width
    swap = [(i, i ^ 1) for i in range(peers)]
    diag = [(i, (i + 1 if i % 2 else i - 1) % peers) for i in range(peers)]
    pair = [(i, (i + 2 if i % 2 else i - 2) % peers) for i in range(peers)]
    flips = [[(i, i ^ (2 * j)) for i in range(peers)] for j in range(peers // 2)]
    place = jnp.stack([me % 2, me * count])
    lines = lambda x: x.reshape(-1, LANES)
    row = lambda x: x.reshape(1, width)
    turn = pltpu.VMEM((LANES, LANES), f32)
    hot_shape = shape(edges, window, kind=bf16)
    small = lambda ref: pltpu.VMEM(ref.shape, ref.dtype)

    small_args = [
        lines(fine_senders), lines(up_owner), lines(up_local), lines(coarse_owner),
        lines(coarse_local), fine_bias, row(up_bias), row(coarse_bias), row(down_bias),
    ]
    here = lambda *xs: [pltpu.with_memory_space_constraint(x, pltpu.HBM) for x in xs]
    state, ints, pack, out_swap, out_diag = call(
        functools.partial(start_kernel, count),
        [SMEM] + [HBM] * 10,
        [
            shape(full, LANES), shape(16, LANES), shape(8, width),
            shape(rim + 16, LANES), shape(rim, LANES),
        ],
        "start",
        [small(x) for x in small_args] + [pltpu.SemaphoreType.DMA((12,))],
    )(place, *here(lines(fine_state), *small_args))
    swap0 = lax.ppermute(out_swap, "sp", swap)
    diag0 = lax.ppermute(out_diag, "sp", diag)
    hot, got, into, high, low = call(
        functools.partial(near_kernel, edges),
        [VMEM] * 2 + [HBM] * 3 + [VMEM],
        [hot_shape, shape(edges, width), shape(rows, width)]
        + [shape(2 * size, width, kind=bf16)] * 2,
        "near0",
        [turn] + [pltpu.VMEM((size, width), f32)] * 3 + [pltpu.SemaphoreType.DMA((3,))],
    )(state, ints, *here(fine_w_send, fine_w_recv, fine_w_out), pack)
    state, out_half = call(
        far_kernel,
        [SMEM] + [VMEM] * 8,
        [shape(full, LANES), shape(rim, LANES)],
        "far0",
    )(place, swap0, diag0, state, hot, got, into, high, low)
    swap1 = lax.ppermute(state, "sp", swap)
    diag1 = lax.ppermute(out_half, "sp", diag)
    pair1 = lax.ppermute(out_half, "sp", pair)
    got, into, own_high, own_low, hot2, select, high, low = call(
        functools.partial(near2_kernel, edges, count),
        [SMEM] + [VMEM] * 10,
        [shape(edges, width), shape(rows, width)]
        + [shape(rows, width, kind=bf16)] * 2
        + [hot_shape, shape(coarse // 2, 2 * rows, kind=bf16)]
        + [shape(5 * size, width, kind=bf16)] * 2,
        "near1",
        [turn],
    )(
        place, state, ints, swap0, hot, fine_w_send, fine_w_recv, fine_w_out, up_w_in, up_w_out,
        pack,
    )
    hidden, *slots = call(
        up_kernel,
        [SMEM] + [VMEM] * 16,
        [shape(rows, width)]
        + [shape(own + 8 * coarse_edges // 256, LANES)] * (peers // 2),
        "up",
        [pltpu.VMEM((window, width), bf16)] * 2,
    )(
        place, swap1, pair1, diag1, state, hot, got, into, own_high, own_low, hot2, select, ints,
        swap0, high, low, pack,
    )
    arrived = [slots[0]] + [
        lax.ppermute(slots[j], "sp", flips[j]) for j in range(1, peers // 2)
    ]
    (middle,) = call(
        middle_kernel,
        [VMEM] * (1 + peers // 2),
        [shape(own, LANES)],
        "middle",
    )(lines(coarse_state), *arrived)
    columns = [middle] + [lax.ppermute(middle, "sp", flips[j]) for j in range(1, peers // 2)]
    blocks = []
    for block in columns:
        blocks += [block, lax.ppermute(block, "sp", swap)]
    degree = coarse_edges // count
    coarse_hot, parent_hot, high, low = call(
        functools.partial(edges_kernel, degree, count),
        [SMEM] + [VMEM] * (6 + peers // 2),
        [
            shape(degree * (count + rows), coarse, kind=bf16),
            shape(rows, coarse, kind=bf16),
        ]
        + [shape(5 * size, width, kind=bf16)] * 2,
        "edges",
        [turn],
    )(
        place, ints, coarse_w_send, coarse_w_recv, coarse_w_out, down_w_in, down_w_out, *arrived
    )
    fine_out, coarse_out = call(
        coarse_kernel,
        [VMEM] * (6 + peers),
        [shape(full, LANES), shape(own, LANES)],
        "coarse",
    )(hidden, coarse_hot, parent_hot, high, low, pack, *blocks)
    return (fine_out.reshape(fine_state.shape), coarse_out.reshape(coarse_state.shape))


def shards(*args):
    fine_state, coarse_state, fine_senders = args[0], args[1], args[2]
    coarse_owner, layers = args[5], args[7].shape[0]
    peers = lax.axis_size("sp")
    rows, samples, width = fine_state.shape
    count = coarse_state.shape[0]
    fits = (
        samples == 1
        and layers == 2
        and width % LANES == 0
        and peers % 2 == 0
        and peers & (peers - 1) == 0
        and rows % LANES == 0
        and rows >= HALO
        and count & (count - 1) == 0
        and LANES % count == 0
        and coarse_owner.shape[0] % LANES == 0
        and coarse_owner.shape[0] == 4 * count
        and fine_senders.shape[0] == 8 * LANES
        and rows == 2 * LANES
        and coarse_owner.shape[0] == 2 * LANES
        and width == args[7].shape[2]
        and peers * count <= 1024
        and peers >= 4
        and rows >= 2 * HALO
    )
    return (kernel_shards if fits else general_shards)(*args)


def solution(mesh):
    in_specs = (
        P("sp", ("grp", "ch"), None),
        P("sp", ("grp", "ch"), None),
        P("sp"),
        P("sp", None),
        P("sp"),
        P("sp", None),
        P("sp"),
    ) + (P(),) * 14
    out_specs = (P("sp", ("grp", "ch"), None), P("sp", ("grp", "ch"), None))
    return jax.shard_map(shards, mesh=mesh, in_specs=in_specs, out_specs=out_specs, check_vma=False)
```

```python
import functools
import jax
import jax.numpy as jnp
from jax import lax
from jax.experimental import pallas as pl
from jax.experimental.pallas import tpu as pltpu
from jax.sharding import PartitionSpec as P

HALO = 128
LANES = 128


epsilon = 1e-05
highest = lax.Precision.HIGHEST


def extended_2(cells, sides, width):
    for axis, dim in sides:
        count = lax.axis_size(axis)
        head = lax.slice_in_dim(cells, 0, width, axis=dim)
        tail = lax.slice_in_dim(cells, cells.shape[dim] - width, cells.shape[dim], axis=dim)
        cells = jnp.concatenate(
            [
                lax.ppermute(tail, axis, [(i, (i + 1) % count) for i in range(count)]),
                cells,
                lax.ppermute(head, axis, [((i + 1) % count, i) for i in range(count)]),
            ],
            axis=dim,
        )
    return cells


def layer_norm(values):
    average = jnp.mean(values, axis=-1, keepdims=True)
    centered = values - average
    spread = jnp.mean(centered * centered, axis=-1, keepdims=True)
    return centered / jnp.sqrt(spread + epsilon)


def project(values, matrix):
    return jnp.einsum(
        "nsd,dh->nsh", values, matrix, precision=highest, preferred_element_type=jnp.float32
    )


def slot_ranks(owners, peer_count):
    matches = (owners[:, None] == jnp.arange(peer_count, dtype=jnp.int32)[None, :]).astype(
        jnp.int32
    )
    ranking = jnp.cumsum(matches, axis=0) - 1
    return jnp.sum(ranking * matches, axis=1)


def general_shards(
    fine_state,
    coarse_state,
    fine_senders,
    up_owner,
    up_local,
    coarse_owner,
    coarse_local,
    fine_w_send,
    fine_w_recv,
    fine_bias,
    fine_w_out,
    up_w_in,
    up_bias,
    up_w_out,
    coarse_w_send,
    coarse_w_recv,
    coarse_bias,
    coarse_w_out,
    down_w_in,
    down_bias,
    down_w_out,
):
    peer_count = lax.axis_size("sp")
    fine_rows = fine_state.shape[0]
    coarse_rows = coarse_state.shape[0]
    samples = fine_state.shape[1]
    feature_width = fine_state.shape[2]
    degree_fine = fine_senders.shape[0] // fine_rows
    degree_coarse = coarse_owner.shape[0] // coarse_rows
    hidden_state = fine_state
    for layer_index in range(fine_w_send.shape[0]):
        normed = layer_norm(hidden_state)
        outward = project(normed, fine_w_send[layer_index])
        inward = project(normed, fine_w_recv[layer_index]) + fine_bias[layer_index]
        extended = extended_2(outward, (("sp", 0),), HALO)
        gathered = extended[fine_senders].reshape(fine_rows, degree_fine, samples, -1)
        summed = jnp.sum(jax.nn.silu(gathered + inward[:, None]), axis=1)
        hidden_state = hidden_state + project(summed, fine_w_out[layer_index])
    capacity = max(4, 2 * fine_rows // peer_count)
    owners = up_owner[:, 0]
    places = owners * capacity + slot_ranks(owners, peer_count)
    targets = (
        jnp.full((peer_count * capacity,), -1.0, jnp.float32)
        .at[places]
        .set(up_local.astype(jnp.float32))
        .reshape(peer_count, capacity)
    )
    activated = jax.nn.silu(project(layer_norm(hidden_state), up_w_in) + up_bias)
    coarse_ids = jnp.arange(coarse_rows, dtype=jnp.float32)[:, None]
    messages = project(activated, up_w_out)
    outgoing = (
        jnp.zeros((peer_count * capacity, samples, feature_width), jnp.float32)
        .at[places]
        .set(messages)
        .reshape(peer_count, capacity, samples, feature_width)
    )
    arrived, sources = (
        lax.all_to_all(outgoing, "sp", split_axis=0, concat_axis=0, tiled=True),
        lax.all_to_all(targets, "sp", split_axis=0, concat_axis=0, tiled=True),
    )
    selector = (sources.reshape(1, -1) == coarse_ids).astype(jnp.float32)
    gained = jnp.einsum(
        "cr,rsd->csd",
        selector,
        arrived.reshape(peer_count * capacity, samples, feature_width),
        precision=highest,
        preferred_element_type=jnp.float32,
    )
    coarse = coarse_state + gained
    normed = layer_norm(coarse)
    outward = project(normed, coarse_w_send)
    inward = project(normed, coarse_w_recv) + coarse_bias
    anchor_owner = coarse_owner[:, 0]
    everything = lax.all_gather(outward, "sp", axis=0, tiled=True)
    picked = everything[anchor_owner * coarse_rows + coarse_local]
    edge_terms = picked.reshape(coarse_rows, degree_coarse, samples, -1)
    summed = jnp.sum(jax.nn.silu(edge_terms + inward[:, None]), axis=1)
    coarse_out = coarse + project(summed, coarse_w_out)
    downward = project(
        jax.nn.silu(project(layer_norm(coarse_out), down_w_in) + down_bias), down_w_out
    )
    wanted = jnp.maximum(sources.reshape(-1), 0.0).astype(jnp.int32)
    replies = downward[wanted].reshape(peer_count, capacity, samples, feature_width)
    answered = lax.all_to_all(replies, "sp", split_axis=0, concat_axis=0, tiled=True)
    fine_out = (
        hidden_state + answered.reshape(peer_count * capacity, samples, feature_width)[places]
    )
    return (fine_out, coarse_out)


f32 = jnp.float32
bf16 = jnp.bfloat16


def load_rows(ref, rows, parts, start=0):
    return jnp.concatenate(
        [ref[pl.ds(start * parts + j, rows, stride=parts), :] for j in range(parts)], axis=1
    )


def store_rows(ref, values, parts, start=0):
    for j in range(parts):
        ref[pl.ds(start * parts + j, values.shape[0], stride=parts), :] = values[
            :, j * LANES : (j + 1) * LANES
        ]


def halves(values):
    high = values.astype(bf16)
    return high, (values - high.astype(f32)).astype(bf16)


def mm(a, b):
    return jnp.dot(a, b, preferred_element_type=f32)


def times(values, high, low):
    vh, vl = halves(values)
    return mm(vh, high) + (mm(vl, high) + mm(vh, low))


def take(one_hot, high, low):
    return mm(one_hot, high) + mm(one_hot, low)


def unit(values):
    width = values.shape[1]
    average = jnp.sum(values, axis=1, keepdims=True) * (1.0 / width)
    centered = values - average
    spread = jnp.sum(centered * centered, axis=1, keepdims=True) * (1.0 / width)
    return centered * lax.rsqrt(spread + epsilon)


def gate(half):
    return half + half * jnp.tanh(half)


def equal(column, count):
    ids = lax.broadcasted_iota(jnp.int32, (column.shape[0], count), 1).astype(f32)
    return jnp.where(ids == column, 1.0, 0.0).astype(bf16)


def turned(lines):
    pad = jnp.zeros((LANES - lines.shape[0], LANES), f32)
    return jnp.transpose(jnp.concatenate([lines, pad], axis=0))


def edge_hot(hot_ref, turn_ref, lines, degree, nodes, flip=None):
    turn_ref[...] = turned(lines)
    step = LANES // degree
    for k in range(degree):
        spread = turn_ref[pl.ds(k, step, stride=degree), :]
        if flip is not None:
            spread = jnp.bitwise_xor(spread.astype(jnp.int32), flip).astype(f32)
        for line in range(lines.shape[0]):
            start = k * nodes + line * step
            hot_ref[start : start + step, :] = equal(
                spread[:, line : line + 1], hot_ref.shape[1]
            )


def split_into(high_ref, low_ref, *matrices):
    for j, matrix in enumerate(matrices):
        size = matrix.shape[0]
        high_ref[j * size : (j + 1) * size, :], low_ref[j * size : (j + 1) * size, :] = halves(
            matrix
        )


def weights(high_ref, low_ref, j):
    size = high_ref.shape[1]
    return high_ref[j * size : (j + 1) * size, :], low_ref[j * size : (j + 1) * size, :]


def start_kernel(
    count, halo, place_ref, state_hbm, sender_hbm, owner_hbm, local_hbm, cowner_hbm,
    clocal_hbm, fb_hbm, ub_hbm, cb_hbm, db_hbm,
    state_ref, ints_ref, pack_ref,
    sender_ref, owner_ref, local_ref, cowner_ref, clocal_ref, fb_ref, ub_ref, cb_ref, db_ref,
    sems,
):
    odd = place_ref[0]
    pairs = [
        (sender_hbm, sender_ref),
        (owner_hbm, owner_ref),
        (local_hbm, local_ref),
        (cowner_hbm, cowner_ref),
        (clocal_hbm, clocal_ref),
        (fb_hbm, fb_ref),
        (ub_hbm, ub_ref),
        (cb_hbm, cb_ref),
        (db_hbm, db_ref),
        (state_hbm, state_ref),
    ]
    copies = [pltpu.make_async_copy(a, b, sems.at[j]) for j, (a, b) in enumerate(pairs)]
    for copy in copies:
        copy.start()
    for copy in copies[:-1]:
        copy.wait()
    rows = state_hbm.shape[0] * LANES // fb_ref.shape[1]
    sender = sender_ref[...]
    before = rows + (1 - odd) * halo
    after = rows + odd * halo
    index = jnp.where(
        sender < halo,
        sender + before,
        jnp.where(sender < halo + rows, sender - halo, sender - (halo + rows) + after),
    )
    lines = [
        index.astype(f32),
        (owner_ref[...] * count + local_ref[...]).astype(f32),
        (cowner_ref[...] * count + clocal_ref[...]).astype(f32),
    ]
    rest = ints_ref.shape[0] - sum(x.shape[0] for x in lines)
    ints_ref[...] = jnp.concatenate(lines + [jnp.zeros((rest, LANES), f32)], axis=0)
    pack_ref[...] = jnp.concatenate(
        [fb_ref[...], ub_ref[...], cb_ref[...], db_ref[...]]
        + [jnp.zeros((3, fb_ref.shape[1]), f32)],
        axis=0,
    )
    copies[-1].wait()


def near_kernel(
    edges, state_ref, ints_ref, ws_hbm, wr_hbm, wo_hbm, pack_ref,
    hot_ref, got_ref, into_ref, high_ref, low_ref, turn_ref, ws_ref, wr_ref, wo_ref, sems,
):
    rows, width = into_ref.shape
    parts = width // LANES
    pairs = ((ws_hbm, ws_ref), (wr_hbm, wr_ref), (wo_hbm, wo_ref))
    copies = [
        pltpu.make_async_copy(a.at[0], b, sems.at[j]) for j, (a, b) in enumerate(pairs)
    ]
    for copy in copies:
        copy.start()
    edge_hot(hot_ref, turn_ref, ints_ref[: edges // LANES, :], edges // rows, rows)
    normed = unit(load_rows(state_ref, rows, parts))
    for copy in copies:
        copy.wait()
    split_into(high_ref, low_ref, ws_ref[...], wo_ref[...])
    into_ref[...] = (times(normed, *halves(wr_ref[...])) + pack_ref[0:1, :]) * 0.5
    high, low = halves(times(normed, *weights(high_ref, low_ref, 0)) * 0.5)
    got_ref[...] = take(hot_ref[:, :rows], high, low)


def far_kernel(
    place_ref, swap_ref, diag_ref, state_ref, hot_ref, got_ref, into_ref, high_ref, low_ref,
    out_full_ref, out_half_ref,
):
    rows, width = into_ref.shape
    parts = width // LANES
    rim = diag_ref.shape[0] // parts
    degree = hot_ref.shape[0] // rows
    far = jnp.concatenate(
        [load_rows(swap_ref, rim, parts), load_rows(diag_ref, rim, parts)], axis=0
    )
    high, low = halves(times(unit(far), *weights(high_ref, low_ref, 0)) * 0.5)
    total = None
    for k in range(degree):
        part = slice(k * rows, (k + 1) * rows)
        half = got_ref[part, :] + into_ref[...] + take(hot_ref[part, rows:], high, low)
        total = gate(half) if total is None else total + gate(half)
    store_rows(
        out_full_ref,
        load_rows(state_ref, rows, parts) + times(total, *weights(high_ref, low_ref, 1)),
        parts,
    )
    lines = out_half_ref.shape[0]
    start = pl.multiple_of(place_ref[0] * (rows * parts - lines), LANES)
    out_half_ref[...] = out_full_ref[pl.ds(start, lines), :]


def near2_kernel(
    edges, count, place_ref, state_ref, ints_ref, ints0_ref, hot_ref, ws_ref, wr_ref, wo_ref, wi_ref,
    wu_ref, pack_ref,
    got_ref, into_ref, own_high_ref, own_low_ref, hot2_ref, select_ref, high_ref, low_ref,
    turn_ref,
):
    rows, width = into_ref.shape
    parts = width // LANES
    senders = edges // LANES
    split_into(
        high_ref, low_ref, ws_ref[1], wr_ref[1], wo_ref[1], wi_ref[...], wu_ref[...]
    )
    normed = unit(load_rows(state_ref, rows, parts))
    into_ref[...] = (times(normed, *weights(high_ref, low_ref, 1)) + pack_ref[1:2, :]) * 0.5
    high, low = halves(times(normed, *weights(high_ref, low_ref, 0)) * 0.5)
    own_high_ref[...] = high
    own_low_ref[...] = low
    got_ref[...] = take(hot_ref[:, :rows], high, low)
    edge_hot(hot2_ref, turn_ref, ints0_ref[:senders, :], edges // rows, rows)
    flip = place_ref[1]
    line = senders
    for half, ref in ((0, ints_ref), (1, ints0_ref)):
        for j in range(rows // LANES):
            parent = ref[line + j : line + j + 1, :].astype(jnp.int32)
            parent = jnp.bitwise_xor(parent, flip)
            ids = lax.broadcasted_iota(jnp.int32, (select_ref.shape[0], LANES), 0)
            ids = ids + jnp.bitwise_and(ids, -count)
            start = half * rows + j * LANES
            select_ref[:, start : start + LANES] = jnp.where(ids == parent, 1.0, 0.0).astype(
                bf16
            )


def halo_kernel(
    place_ref, pair_ref, diag_ref, own_high_ref, own_low_ref, hot2_ref, high_ref, low_ref,
    got2_ref, diag_high_ref, diag_low_ref,
):
    rim, width = diag_high_ref.shape
    rows = own_high_ref.shape[0]
    parts = width // LANES
    mine = pl.multiple_of((1 - place_ref[0]) * (rows - rim), LANES)
    normed = unit(
        jnp.concatenate(
            [load_rows(pair_ref, rim, parts), load_rows(diag_ref, rim, parts)], axis=0
        )
    )
    high, low = halves(times(normed, *weights(high_ref, low_ref, 0)) * 0.5)
    diag_high_ref[...] = high[rim:, :]
    diag_low_ref[...] = low[rim:, :]
    got2_ref[...] = take(
        hot2_ref[:, rows:],
        jnp.concatenate([own_high_ref[pl.ds(mine, rim), :], high[:rim, :]], axis=0),
        jnp.concatenate([own_low_ref[pl.ds(mine, rim), :], low[:rim, :]], axis=0),
    )


def up_kernel(
    place_ref, swap_ref, diag_high_ref, diag_low_ref, state_ref, hot_ref, got_ref, into_ref,
    hot2_ref, got2_ref, select_ref, ints_ref, ints0_ref, high_ref, low_ref, pack_ref,
    last_ref, *refs,
):
    *slot_refs, th_ref, tl_ref = refs
    rows, width = into_ref.shape
    parts = width // LANES
    rim = diag_high_ref.shape[0]
    degree = hot_ref.shape[0] // rows
    theirs = pl.multiple_of(place_ref[0] * (rows - rim), LANES)
    other = load_rows(swap_ref, rows, parts)
    normed = unit(other)
    high, low = halves(times(normed, *weights(high_ref, low_ref, 0)) * 0.5)
    th_ref[...] = high
    tl_ref[...] = low
    near = (
        jnp.concatenate([th_ref[pl.ds(theirs, rim), :], diag_high_ref[...]], axis=0),
        jnp.concatenate([tl_ref[pl.ds(theirs, rim), :], diag_low_ref[...]], axis=0),
    )
    into = (times(normed, *weights(high_ref, low_ref, 1)) + pack_ref[1:2, :]) * 0.5
    total, total2 = None, None
    for k in range(degree):
        part = slice(k * rows, (k + 1) * rows)
        half = got_ref[part, :] + into_ref[...] + take(hot_ref[part, rows:], *near)
        total = gate(half) if total is None else total + gate(half)
        half = got2_ref[part, :] + into + take(hot2_ref[part, :rows], high, low)
        total2 = gate(half) if total2 is None else total2 + gate(half)
    hidden = jnp.concatenate([load_rows(state_ref, rows, parts), other], axis=0) + times(
        jnp.concatenate([total, total2], axis=0), *weights(high_ref, low_ref, 2)
    )
    last_ref[...] = hidden[:rows, :]
    act = gate((times(unit(hidden), *weights(high_ref, low_ref, 3)) + pack_ref[2:3, :]) * 0.5)
    sums = take(select_ref[...], *halves(times(act, *weights(high_ref, low_ref, 4))))
    size = sums.shape[0] // len(slot_refs)
    first = hot_ref.shape[0] // LANES + rows // LANES
    anchor = (slot_refs[0].shape[0] - size * parts) // 4
    for j, slot in enumerate(slot_refs):
        store_rows(slot, sums[j * size : (j + 1) * size, :], parts)
        slot[size * parts :, :] = jnp.concatenate(
            [
                ints_ref[first : first + anchor, :],
                ints0_ref[first : first + anchor, :],
                jnp.zeros((2 * anchor, LANES), f32),
            ],
            axis=0,
        )


def middle_kernel(state_ref, *refs):
    out_ref = refs[-1]
    total = state_ref[...]
    for ref in refs[:-1]:
        total = total + ref[: out_ref.shape[0], :]
    out_ref[...] = total


def position(ids, flip, count, coarse):
    ids = jnp.bitwise_xor(ids.astype(jnp.int32), flip)
    slot = jnp.right_shift(ids, count.bit_length() - 1)
    return (
        jnp.bitwise_and(ids, count - 1)
        + jnp.right_shift(slot, 1) * count
        + jnp.bitwise_and(slot, 1) * (coarse // 2)
    )


def edges_kernel(
    degree, count, place_ref, ints_ref, cs_ref, cr_ref, co_ref, di_ref, do_ref, *refs
):
    *slot_refs, hot_ref, parent_ref, high_ref, low_ref, turn_ref = refs
    rows, coarse = parent_ref.shape
    flip = place_ref[1]
    split_into(
        high_ref, low_ref, cs_ref[...], cr_ref[...], co_ref[...], di_ref[...], do_ref[...]
    )
    columns = turned(ints_ref[...])
    first = ints_ref.shape[0] // 2
    for j in range(rows // LANES):
        column = position(columns[:, first + j : first + j + 1], flip, count, coarse).astype(f32)
        parent_ref[j * LANES : (j + 1) * LANES, :] = equal(column, coarse)
    here = coarse * degree // LANES // len(slot_refs)
    line = here // 2
    lines = jnp.concatenate(
        [
            ref[ref.shape[0] - 2 * here + side * line : ref.shape[0] - 2 * here + (side + 1) * line, :]
            for side in range(2)
            for ref in slot_refs
        ],
        axis=0,
    )
    turn_ref[...] = turned(lines)
    step = LANES // degree
    lane = lax.broadcasted_iota(jnp.int32, (coarse, LANES), 1)
    table = jnp.zeros((coarse, LANES), f32)
    each = hot_ref.shape[0] // degree
    for k in range(degree):
        spread = position(turn_ref[pl.ds(k, step, stride=degree), :], flip, count, coarse)
        column = jnp.concatenate([spread[:, j : j + 1] for j in range(lines.shape[0])], axis=0)
        hot_ref[k * each : k * each + count, :] = equal(column[:count, :].astype(f32), coarse)
        high = jnp.right_shift(column, 8).astype(f32)
        low = jnp.bitwise_and(column, 255).astype(f32)
        table = jnp.where(lane == k, high, jnp.where(lane == degree + k, low, table))
    found = mm(parent_ref[...], table.astype(bf16))
    for k in range(degree):
        column = found[:, k : k + 1] * 256.0 + found[:, degree + k : degree + k + 1]
        hot_ref[k * each + count : (k + 1) * each, :] = equal(column, coarse)


def column_kernel(hot_ref, parent_ref, high_ref, low_ref, *refs):
    *blocks, got_ref, wanted_ref = refs
    rows, width = wanted_ref.shape
    parts = width // LANES
    count = blocks[0].shape[0] // parts
    middle = jnp.concatenate([load_rows(b, count, parts) for b in blocks], axis=0)
    half = count * len(blocks)
    sends = halves(times(unit(middle), *weights(high_ref, low_ref, 0)) * 0.5)
    got_ref[...] = take(hot_ref[:, :half], *sends)
    wanted_ref[:count, :] = middle[:count, :]
    wanted_ref[count:, :] = take(parent_ref[:, :half], *halves(middle))


def coarse_kernel(
    last_ref, hot_ref, parent_ref, got_ref, wanted_ref, high_ref, low_ref, pack_ref, *refs
):
    *blocks, fine_ref, coarse_ref = refs
    rows, width = last_ref.shape
    parts = width // LANES
    count = coarse_ref.shape[0] // parts
    need = count + rows
    middle = jnp.concatenate([load_rows(b, count, parts) for b in blocks], axis=0)
    half = count * len(blocks)
    sends = halves(times(unit(middle), *weights(high_ref, low_ref, 0)) * 0.5)
    wanted = jnp.concatenate(
        [
            wanted_ref[:count, :],
            wanted_ref[count:, :] + take(parent_ref[:, half:], *halves(middle)),
        ],
        axis=0,
    )
    into = (times(unit(wanted), *weights(high_ref, low_ref, 1)) + pack_ref[3:4, :]) * 0.5
    total = None
    for k in range(hot_ref.shape[0] // need):
        part = slice(k * need, (k + 1) * need)
        term = gate(got_ref[part, :] + into + take(hot_ref[part, half:], *sends))
        total = term if total is None else total + term
    done = wanted + times(total, *weights(high_ref, low_ref, 2))
    store_rows(coarse_ref, done[:count, :], parts)
    act = gate(
        (times(unit(done[count:, :]), *weights(high_ref, low_ref, 3)) + pack_ref[4:5, :]) * 0.5
    )
    store_rows(fine_ref, last_ref[...] + times(act, *weights(high_ref, low_ref, 4)), parts)


VMEM = pl.BlockSpec(memory_space=pltpu.VMEM)
SMEM = pl.BlockSpec(memory_space=pltpu.SMEM)
HBM = pl.BlockSpec(memory_space=pltpu.HBM)


def call(kernel, in_specs, out_shapes, name, scratch=()):
    return pl.pallas_call(
        kernel,
        in_specs=in_specs,
        out_specs=[VMEM] * len(out_shapes),
        out_shape=out_shapes,
        scratch_shapes=scratch,
        name=name,
        compiler_params=pltpu.CompilerParams(vmem_limit_bytes=32 * 2**20),
    )


def shape(*dims, kind=f32):
    return jax.ShapeDtypeStruct(dims, kind)


def kernel_shards(
    fine_state,
    coarse_state,
    fine_senders,
    up_owner,
    up_local,
    coarse_owner,
    coarse_local,
    fine_w_send,
    fine_w_recv,
    fine_bias,
    fine_w_out,
    up_w_in,
    up_bias,
    up_w_out,
    coarse_w_send,
    coarse_w_recv,
    coarse_bias,
    coarse_w_out,
    down_w_in,
    down_bias,
    down_w_out,
):
    peers = lax.axis_size("sp")
    me = lax.axis_index("sp").astype(jnp.int32)
    rows, _, width = fine_state.shape
    count = coarse_state.shape[0]
    parts = width // LANES
    edges = fine_senders.shape[0]
    coarse_edges = coarse_owner.shape[0]
    coarse = peers * count
    window = rows + 2 * HALO
    rim, own, full = HALO * parts, count * parts, rows * parts
    size = width
    swap = [(i, i ^ 1) for i in range(peers)]
    diag = [(i, (i + 1 if i % 2 else i - 1) % peers) for i in range(peers)]
    pair = [(i, (i + 2 if i % 2 else i - 2) % peers) for i in range(peers)]
    flips = [[(i, i ^ (2 * j)) for i in range(peers)] for j in range(peers // 2)]
    place = jnp.stack([me % 2, me * count])
    lines = lambda x: x.reshape(-1, LANES)
    row = lambda x: x.reshape(1, width)
    turn = pltpu.VMEM((LANES, LANES), f32)
    here = lambda *xs: [pltpu.with_memory_space_constraint(x, pltpu.HBM) for x in xs]
    hot_shape = shape(edges, window, kind=bf16)
    small = lambda ref: pltpu.VMEM(ref.shape, ref.dtype)

    small_args = [
        lines(fine_senders), lines(up_owner), lines(up_local), lines(coarse_owner),
        lines(coarse_local), fine_bias, row(up_bias), row(coarse_bias), row(down_bias),
    ]
    flat = lines(fine_state)
    out_swap = lax.dynamic_slice(flat, ((1 - me % 2) * (full - rim), 0), (rim, LANES))
    out_diag = lax.dynamic_slice(flat, (me % 2 * (full - rim), 0), (rim, LANES))
    swap0 = lax.ppermute(out_swap, "sp", swap)
    diag0 = lax.ppermute(out_diag, "sp", diag)
    state, ints, pack = call(
        functools.partial(start_kernel, count, HALO),
        [SMEM] + [HBM] * 10,
        [shape(full, LANES), shape(16, LANES), shape(8, width)],
        "start",
        [small(x) for x in small_args] + [pltpu.SemaphoreType.DMA((10,))],
    )(place, *here(flat, *small_args))
    ints0 = lax.ppermute(ints, "sp", swap)
    hot, got, into, high, low = call(
        functools.partial(near_kernel, edges),
        [VMEM] * 2 + [HBM] * 3 + [VMEM],
        [hot_shape, shape(edges, width), shape(rows, width)]
        + [shape(2 * size, width, kind=bf16)] * 2,
        "near0",
        [turn] + [pltpu.VMEM((size, width), f32)] * 3 + [pltpu.SemaphoreType.DMA((3,))],
    )(state, ints, *here(fine_w_send, fine_w_recv, fine_w_out), pack)
    state, out_half = call(
        far_kernel,
        [SMEM] + [VMEM] * 8,
        [shape(full, LANES), shape(rim, LANES)],
        "far0",
    )(place, swap0, diag0, state, hot, got, into, high, low)
    swap1 = lax.ppermute(state, "sp", swap)
    diag1 = lax.ppermute(out_half, "sp", diag)
    pair1 = lax.ppermute(out_half, "sp", pair)
    got, into, own_high, own_low, hot2, select, high, low = call(
        functools.partial(near2_kernel, edges, count),
        [SMEM] + [VMEM] * 10,
        [shape(edges, width), shape(rows, width)]
        + [shape(rows, width, kind=bf16)] * 2
        + [hot_shape, shape(coarse // 2, 2 * rows, kind=bf16)]
        + [shape(5 * size, width, kind=bf16)] * 2,
        "near1",
        [turn],
    )(
        place, state, ints, ints0, hot, fine_w_send, fine_w_recv, fine_w_out, up_w_in, up_w_out,
        pack,
    )
    got2, diag_high, diag_low = call(
        halo_kernel,
        [SMEM] + [VMEM] * 7,
        [shape(edges, width)] + [shape(HALO, width, kind=bf16)] * 2,
        "halo",
    )(place, pair1, diag1, own_high, own_low, hot2, high, low)
    hidden, *slots = call(
        up_kernel,
        [SMEM] + [VMEM] * 15,
        [shape(rows, width)]
        + [shape(own + 8 * coarse_edges // 256, LANES)] * (peers // 2),
        "up",
        [pltpu.VMEM((rows, width), bf16)] * 2,
    )(
        place, swap1, diag_high, diag_low, state, hot, got, into, hot2, got2, select, ints, ints0,
        high, low, pack,
    )
    arrived = [slots[0]] + [
        lax.ppermute(slots[j], "sp", flips[j]) for j in range(1, peers // 2)
    ]
    (middle,) = call(
        middle_kernel,
        [VMEM] * (1 + peers // 2),
        [shape(own, LANES)],
        "middle",
    )(lines(coarse_state), *arrived)
    columns = [middle] + [lax.ppermute(middle, "sp", flips[j]) for j in range(1, peers // 2)]
    across = [lax.ppermute(block, "sp", swap) for block in columns]
    degree = coarse_edges // count
    coarse_hot, parent_hot, high, low = call(
        functools.partial(edges_kernel, degree, count),
        [SMEM] + [VMEM] * (6 + peers // 2),
        [
            shape(degree * (count + rows), coarse, kind=bf16),
            shape(rows, coarse, kind=bf16),
        ]
        + [shape(5 * size, width, kind=bf16)] * 2,
        "edges",
        [turn],
    )(
        place, ints, coarse_w_send, coarse_w_recv, coarse_w_out, down_w_in, down_w_out, *arrived
    )
    got, wanted = call(
        column_kernel,
        [VMEM] * (4 + peers // 2),
        [shape(degree * (count + rows), width), shape(count + rows, width)],
        "column",
    )(coarse_hot, parent_hot, high, low, *columns)
    fine_out, coarse_out = call(
        coarse_kernel,
        [VMEM] * (8 + peers // 2),
        [shape(full, LANES), shape(own, LANES)],
        "coarse",
    )(hidden, coarse_hot, parent_hot, got, wanted, high, low, pack, *across)
    return (fine_out.reshape(fine_state.shape), coarse_out.reshape(coarse_state.shape))


def shards(*args):
    fine_state, coarse_state, fine_senders = args[0], args[1], args[2]
    coarse_owner, layers = args[5], args[7].shape[0]
    peers = lax.axis_size("sp")
    rows, samples, width = fine_state.shape
    count = coarse_state.shape[0]
    fits = (
        samples == 1
        and layers == 2
        and width % LANES == 0
        and peers % 2 == 0
        and peers & (peers - 1) == 0
        and rows % LANES == 0
        and rows >= HALO
        and count & (count - 1) == 0
        and LANES % count == 0
        and coarse_owner.shape[0] % LANES == 0
        and coarse_owner.shape[0] == 4 * count
        and fine_senders.shape[0] == 8 * LANES
        and rows == 2 * LANES
        and coarse_owner.shape[0] == 2 * LANES
        and width == args[7].shape[2]
        and peers * count <= 1024
        and peers >= 4
        and rows >= 2 * HALO
    )
    return (kernel_shards if fits else general_shards)(*args)


def solution(mesh):
    in_specs = (
        P("sp", ("grp", "ch"), None),
        P("sp", ("grp", "ch"), None),
        P("sp"),
        P("sp", None),
        P("sp"),
        P("sp", None),
        P("sp"),
    ) + (P(),) * 14
    out_specs = (P("sp", ("grp", "ch"), None), P("sp", ("grp", "ch"), None))
    return jax.shard_map(shards, mesh=mesh, in_specs=in_specs, out_specs=out_specs, check_vma=False)
```

```python
import functools
import jax
import jax.numpy as jnp
from jax import lax
from jax.experimental import pallas as pl
from jax.experimental.pallas import tpu as pltpu
from jax.sharding import PartitionSpec as P

HALO = 128
LANES = 128


epsilon = 1e-05
highest = lax.Precision.HIGHEST


def extended_2(cells, sides, width):
    for axis, dim in sides:
        count = lax.axis_size(axis)
        head = lax.slice_in_dim(cells, 0, width, axis=dim)
        tail = lax.slice_in_dim(cells, cells.shape[dim] - width, cells.shape[dim], axis=dim)
        cells = jnp.concatenate(
            [
                lax.ppermute(tail, axis, [(i, (i + 1) % count) for i in range(count)]),
                cells,
                lax.ppermute(head, axis, [((i + 1) % count, i) for i in range(count)]),
            ],
            axis=dim,
        )
    return cells


def layer_norm(values):
    average = jnp.mean(values, axis=-1, keepdims=True)
    centered = values - average
    spread = jnp.mean(centered * centered, axis=-1, keepdims=True)
    return centered / jnp.sqrt(spread + epsilon)


def project(values, matrix):
    return jnp.einsum(
        "nsd,dh->nsh", values, matrix, precision=highest, preferred_element_type=jnp.float32
    )


def slot_ranks(owners, peer_count):
    matches = (owners[:, None] == jnp.arange(peer_count, dtype=jnp.int32)[None, :]).astype(
        jnp.int32
    )
    ranking = jnp.cumsum(matches, axis=0) - 1
    return jnp.sum(ranking * matches, axis=1)


def general_shards(
    fine_state,
    coarse_state,
    fine_senders,
    up_owner,
    up_local,
    coarse_owner,
    coarse_local,
    fine_w_send,
    fine_w_recv,
    fine_bias,
    fine_w_out,
    up_w_in,
    up_bias,
    up_w_out,
    coarse_w_send,
    coarse_w_recv,
    coarse_bias,
    coarse_w_out,
    down_w_in,
    down_bias,
    down_w_out,
):
    peer_count = lax.axis_size("sp")
    fine_rows = fine_state.shape[0]
    coarse_rows = coarse_state.shape[0]
    samples = fine_state.shape[1]
    feature_width = fine_state.shape[2]
    degree_fine = fine_senders.shape[0] // fine_rows
    degree_coarse = coarse_owner.shape[0] // coarse_rows
    hidden_state = fine_state
    for layer_index in range(fine_w_send.shape[0]):
        normed = layer_norm(hidden_state)
        outward = project(normed, fine_w_send[layer_index])
        inward = project(normed, fine_w_recv[layer_index]) + fine_bias[layer_index]
        extended = extended_2(outward, (("sp", 0),), HALO)
        gathered = extended[fine_senders].reshape(fine_rows, degree_fine, samples, -1)
        summed = jnp.sum(jax.nn.silu(gathered + inward[:, None]), axis=1)
        hidden_state = hidden_state + project(summed, fine_w_out[layer_index])
    capacity = max(4, 2 * fine_rows // peer_count)
    owners = up_owner[:, 0]
    places = owners * capacity + slot_ranks(owners, peer_count)
    targets = (
        jnp.full((peer_count * capacity,), -1.0, jnp.float32)
        .at[places]
        .set(up_local.astype(jnp.float32))
        .reshape(peer_count, capacity)
    )
    activated = jax.nn.silu(project(layer_norm(hidden_state), up_w_in) + up_bias)
    coarse_ids = jnp.arange(coarse_rows, dtype=jnp.float32)[:, None]
    messages = project(activated, up_w_out)
    outgoing = (
        jnp.zeros((peer_count * capacity, samples, feature_width), jnp.float32)
        .at[places]
        .set(messages)
        .reshape(peer_count, capacity, samples, feature_width)
    )
    arrived, sources = (
        lax.all_to_all(outgoing, "sp", split_axis=0, concat_axis=0, tiled=True),
        lax.all_to_all(targets, "sp", split_axis=0, concat_axis=0, tiled=True),
    )
    selector = (sources.reshape(1, -1) == coarse_ids).astype(jnp.float32)
    gained = jnp.einsum(
        "cr,rsd->csd",
        selector,
        arrived.reshape(peer_count * capacity, samples, feature_width),
        precision=highest,
        preferred_element_type=jnp.float32,
    )
    coarse = coarse_state + gained
    normed = layer_norm(coarse)
    outward = project(normed, coarse_w_send)
    inward = project(normed, coarse_w_recv) + coarse_bias
    anchor_owner = coarse_owner[:, 0]
    everything = lax.all_gather(outward, "sp", axis=0, tiled=True)
    picked = everything[anchor_owner * coarse_rows + coarse_local]
    edge_terms = picked.reshape(coarse_rows, degree_coarse, samples, -1)
    summed = jnp.sum(jax.nn.silu(edge_terms + inward[:, None]), axis=1)
    coarse_out = coarse + project(summed, coarse_w_out)
    downward = project(
        jax.nn.silu(project(layer_norm(coarse_out), down_w_in) + down_bias), down_w_out
    )
    wanted = jnp.maximum(sources.reshape(-1), 0.0).astype(jnp.int32)
    replies = downward[wanted].reshape(peer_count, capacity, samples, feature_width)
    answered = lax.all_to_all(replies, "sp", split_axis=0, concat_axis=0, tiled=True)
    fine_out = (
        hidden_state + answered.reshape(peer_count * capacity, samples, feature_width)[places]
    )
    return (fine_out, coarse_out)


f32 = jnp.float32
bf16 = jnp.bfloat16


def load_rows(ref, rows, parts, start=0):
    return jnp.concatenate(
        [ref[pl.ds(start * parts + j, rows, stride=parts), :] for j in range(parts)], axis=1
    )


def store_rows(ref, values, parts, start=0):
    for j in range(parts):
        ref[pl.ds(start * parts + j, values.shape[0], stride=parts), :] = values[
            :, j * LANES : (j + 1) * LANES
        ]


def halves(values):
    high = values.astype(bf16)
    return high, (values - high.astype(f32)).astype(bf16)


def mm(a, b):
    return jnp.dot(a, b, preferred_element_type=f32)


def times(values, high, low):
    vh, vl = halves(values)
    return mm(vh, high) + (mm(vl, high) + mm(vh, low))


def take(one_hot, high, low):
    return mm(one_hot, high) + mm(one_hot, low)


def unit(values):
    width = values.shape[1]
    average = jnp.sum(values, axis=1, keepdims=True) * (1.0 / width)
    centered = values - average
    spread = jnp.sum(centered * centered, axis=1, keepdims=True) * (1.0 / width)
    return centered * lax.rsqrt(spread + epsilon)


def gate(half):
    return half + half * jnp.tanh(half)


def equal(column, count):
    ids = lax.broadcasted_iota(jnp.int32, (column.shape[0], count), 1).astype(f32)
    return jnp.where(ids == column, 1.0, 0.0).astype(bf16)


def turned(lines):
    pad = jnp.zeros((LANES - lines.shape[0], LANES), f32)
    return jnp.transpose(jnp.concatenate([lines, pad], axis=0))


def edge_hot(hot_ref, turn_ref, lines, degree, nodes, flip=None):
    turn_ref[...] = turned(lines)
    step = LANES // degree
    for k in range(degree):
        spread = turn_ref[pl.ds(k, step, stride=degree), :]
        if flip is not None:
            spread = jnp.bitwise_xor(spread.astype(jnp.int32), flip).astype(f32)
        for line in range(lines.shape[0]):
            start = k * nodes + line * step
            hot_ref[start : start + step, :] = equal(
                spread[:, line : line + 1], hot_ref.shape[1]
            )


def split_into(high_ref, low_ref, *matrices):
    for j, matrix in enumerate(matrices):
        size = matrix.shape[0]
        high_ref[j * size : (j + 1) * size, :], low_ref[j * size : (j + 1) * size, :] = halves(
            matrix
        )


def weights(high_ref, low_ref, j):
    size = high_ref.shape[1]
    return high_ref[j * size : (j + 1) * size, :], low_ref[j * size : (j + 1) * size, :]


def start_kernel(
    count, halo, place_ref, state_hbm, sender_hbm, owner_hbm, local_hbm, cowner_hbm,
    clocal_hbm, fb_hbm, ub_hbm, cb_hbm, db_hbm,
    state_ref, ints_ref, pack_ref,
    sender_ref, owner_ref, local_ref, cowner_ref, clocal_ref, fb_ref, ub_ref, cb_ref, db_ref,
    sems,
):
    odd = place_ref[0]
    pairs = [
        (sender_hbm, sender_ref),
        (owner_hbm, owner_ref),
        (local_hbm, local_ref),
        (cowner_hbm, cowner_ref),
        (clocal_hbm, clocal_ref),
        (fb_hbm, fb_ref),
        (ub_hbm, ub_ref),
        (cb_hbm, cb_ref),
        (db_hbm, db_ref),
        (state_hbm, state_ref),
    ]
    copies = [pltpu.make_async_copy(a, b, sems.at[j]) for j, (a, b) in enumerate(pairs)]
    for copy in copies:
        copy.start()
    for copy in copies[:-1]:
        copy.wait()
    rows = state_hbm.shape[0] * LANES // fb_ref.shape[1]
    sender = sender_ref[...]
    before = rows + (1 - odd) * halo
    after = rows + odd * halo
    index = jnp.where(
        sender < halo,
        sender + before,
        jnp.where(sender < halo + rows, sender - halo, sender - (halo + rows) + after),
    )
    lines = [
        index.astype(f32),
        (owner_ref[...] * count + local_ref[...]).astype(f32),
        (cowner_ref[...] * count + clocal_ref[...]).astype(f32),
    ]
    rest = ints_ref.shape[0] - sum(x.shape[0] for x in lines)
    ints_ref[...] = jnp.concatenate(lines + [jnp.zeros((rest, LANES), f32)], axis=0)
    pack_ref[...] = jnp.concatenate(
        [fb_ref[...], ub_ref[...], cb_ref[...], db_ref[...]]
        + [jnp.zeros((3, fb_ref.shape[1]), f32)],
        axis=0,
    )
    copies[-1].wait()


def near_kernel(
    edges, state_ref, ints_ref, ws_hbm, wr_hbm, wo_hbm, pack_ref,
    hot_ref, got_ref, into_ref, high_ref, low_ref, turn_ref, ws_ref, wr_ref, wo_ref, sems,
):
    rows, width = into_ref.shape
    parts = width // LANES
    pairs = ((ws_hbm, ws_ref), (wr_hbm, wr_ref), (wo_hbm, wo_ref))
    copies = [
        pltpu.make_async_copy(a.at[0], b, sems.at[j]) for j, (a, b) in enumerate(pairs)
    ]
    for copy in copies:
        copy.start()
    edge_hot(hot_ref, turn_ref, ints_ref[: edges // LANES, :], edges // rows, rows)
    normed = unit(load_rows(state_ref, rows, parts))
    for copy in copies:
        copy.wait()
    split_into(high_ref, low_ref, ws_ref[...], wo_ref[...])
    into_ref[...] = (times(normed, *halves(wr_ref[...])) + pack_ref[0:1, :]) * 0.5
    high, low = halves(times(normed, *weights(high_ref, low_ref, 0)) * 0.5)
    got_ref[...] = take(hot_ref[:, :rows], high, low)


def far_kernel(
    place_ref, swap_ref, diag_ref, state_ref, hot_ref, got_ref, into_ref, high_ref, low_ref,
    out_full_ref, out_half_ref,
):
    rows, width = into_ref.shape
    parts = width // LANES
    rim = diag_ref.shape[0] // parts
    degree = hot_ref.shape[0] // rows
    far = jnp.concatenate(
        [load_rows(swap_ref, rim, parts), load_rows(diag_ref, rim, parts)], axis=0
    )
    high, low = halves(times(unit(far), *weights(high_ref, low_ref, 0)) * 0.5)
    total = None
    for k in range(degree):
        part = slice(k * rows, (k + 1) * rows)
        half = got_ref[part, :] + into_ref[...] + take(hot_ref[part, rows:], high, low)
        total = gate(half) if total is None else total + gate(half)
    store_rows(
        out_full_ref,
        load_rows(state_ref, rows, parts) + times(total, *weights(high_ref, low_ref, 1)),
        parts,
    )
    lines = out_half_ref.shape[0]
    start = pl.multiple_of(place_ref[0] * (rows * parts - lines), LANES)
    out_half_ref[...] = out_full_ref[pl.ds(start, lines), :]


def near2_kernel(
    edges, count, place_ref, state_ref, ints_ref, ints0_ref, hot_ref, ws_ref, wr_ref, wo_ref, wi_ref,
    wu_ref, pack_ref,
    got_ref, into_ref, own_high_ref, own_low_ref, hot2_ref, select_ref, high_ref, low_ref,
    turn_ref,
):
    rows, width = into_ref.shape
    parts = width // LANES
    senders = edges // LANES
    split_into(
        high_ref, low_ref, ws_ref[1], wr_ref[1], wo_ref[1], wi_ref[...], wu_ref[...]
    )
    normed = unit(load_rows(state_ref, rows, parts))
    into_ref[...] = (times(normed, *weights(high_ref, low_ref, 1)) + pack_ref[1:2, :]) * 0.5
    high, low = halves(times(normed, *weights(high_ref, low_ref, 0)) * 0.5)
    own_high_ref[...] = high
    own_low_ref[...] = low
    got_ref[...] = take(hot_ref[:, :rows], high, low)
    edge_hot(hot2_ref, turn_ref, ints0_ref[:senders, :], edges // rows, rows)
    flip = place_ref[1]
    line = senders
    for half, ref in ((0, ints_ref), (1, ints0_ref)):
        for j in range(rows // LANES):
            parent = ref[line + j : line + j + 1, :].astype(jnp.int32)
            parent = jnp.bitwise_xor(parent, flip)
            ids = lax.broadcasted_iota(jnp.int32, (select_ref.shape[0], LANES), 0)
            ids = ids + jnp.bitwise_and(ids, -count)
            start = half * rows + j * LANES
            select_ref[:, start : start + LANES] = jnp.where(ids == parent, 1.0, 0.0).astype(
                bf16
            )


def halo_kernel(
    place_ref, pair_ref, diag_ref, own_high_ref, own_low_ref, hot2_ref, high_ref, low_ref,
    got2_ref, diag_high_ref, diag_low_ref,
):
    rim, width = diag_high_ref.shape
    rows = own_high_ref.shape[0]
    parts = width // LANES
    mine = pl.multiple_of((1 - place_ref[0]) * (rows - rim), LANES)
    normed = unit(
        jnp.concatenate(
            [load_rows(pair_ref, rim, parts), load_rows(diag_ref, rim, parts)], axis=0
        )
    )
    high, low = halves(times(normed, *weights(high_ref, low_ref, 0)) * 0.5)
    diag_high_ref[...] = high[rim:, :]
    diag_low_ref[...] = low[rim:, :]
    got2_ref[...] = take(
        hot2_ref[:, rows:],
        jnp.concatenate([own_high_ref[pl.ds(mine, rim), :], high[:rim, :]], axis=0),
        jnp.concatenate([own_low_ref[pl.ds(mine, rim), :], low[:rim, :]], axis=0),
    )


def up_kernel(
    place_ref, swap_ref, diag_high_ref, diag_low_ref, state_ref, hot_ref, got_ref, into_ref,
    hot2_ref, got2_ref, select_ref, ints_ref, ints0_ref, high_ref, low_ref, pack_ref,
    last_ref, *refs,
):
    *slot_refs, th_ref, tl_ref = refs
    rows, width = into_ref.shape
    parts = width // LANES
    rim = diag_high_ref.shape[0]
    degree = hot_ref.shape[0] // rows
    theirs = pl.multiple_of(place_ref[0] * (rows - rim), LANES)
    other = load_rows(swap_ref, rows, parts)
    normed = unit(other)
    high, low = halves(times(normed, *weights(high_ref, low_ref, 0)) * 0.5)
    th_ref[...] = high
    tl_ref[...] = low
    near = (
        jnp.concatenate([th_ref[pl.ds(theirs, rim), :], diag_high_ref[...]], axis=0),
        jnp.concatenate([tl_ref[pl.ds(theirs, rim), :], diag_low_ref[...]], axis=0),
    )
    into = (times(normed, *weights(high_ref, low_ref, 1)) + pack_ref[1:2, :]) * 0.5
    total, total2 = None, None
    for k in range(degree):
        part = slice(k * rows, (k + 1) * rows)
        half = got_ref[part, :] + into_ref[...] + take(hot_ref[part, rows:], *near)
        total = gate(half) if total is None else total + gate(half)
        half = got2_ref[part, :] + into + take(hot2_ref[part, :rows], high, low)
        total2 = gate(half) if total2 is None else total2 + gate(half)
    hidden = jnp.concatenate([load_rows(state_ref, rows, parts), other], axis=0) + times(
        jnp.concatenate([total, total2], axis=0), *weights(high_ref, low_ref, 2)
    )
    last_ref[...] = hidden[:rows, :]
    act = gate((times(unit(hidden), *weights(high_ref, low_ref, 3)) + pack_ref[2:3, :]) * 0.5)
    sums = take(select_ref[...], *halves(times(act, *weights(high_ref, low_ref, 4))))
    size = sums.shape[0] // len(slot_refs)
    first = hot_ref.shape[0] // LANES + rows // LANES
    anchor = (slot_refs[0].shape[0] - size * parts) // 4
    for j, slot in enumerate(slot_refs):
        store_rows(slot, sums[j * size : (j + 1) * size, :], parts)
        slot[size * parts :, :] = jnp.concatenate(
            [
                ints_ref[first : first + anchor, :],
                ints0_ref[first : first + anchor, :],
                jnp.zeros((2 * anchor, LANES), f32),
            ],
            axis=0,
        )


def middle_kernel(state_ref, *refs):
    out_ref = refs[-1]
    total = state_ref[...]
    for ref in refs[:-1]:
        total = total + ref[: out_ref.shape[0], :]
    out_ref[...] = total


def position(ids, flip, count, coarse):
    ids = jnp.bitwise_xor(ids.astype(jnp.int32), flip)
    slot = jnp.right_shift(ids, count.bit_length() - 1)
    return (
        jnp.bitwise_and(ids, count - 1)
        + jnp.right_shift(slot, 1) * count
        + jnp.bitwise_and(slot, 1) * (coarse // 2)
    )


def split_kernel(cs_ref, cr_ref, co_ref, di_ref, do_ref, high_ref, low_ref):
    split_into(
        high_ref, low_ref, cs_ref[...], cr_ref[...], co_ref[...], di_ref[...], do_ref[...]
    )


def edges_kernel(degree, count, place_ref, ints_ref, *refs):
    *slot_refs, hot_ref, parent_ref, turn_ref = refs
    rows, coarse = parent_ref.shape
    flip = place_ref[1]
    columns = turned(ints_ref[...])
    first = ints_ref.shape[0] // 2
    for j in range(rows // LANES):
        column = position(columns[:, first + j : first + j + 1], flip, count, coarse).astype(f32)
        parent_ref[j * LANES : (j + 1) * LANES, :] = equal(column, coarse)
    here = coarse * degree // LANES // len(slot_refs)
    line = here // 2
    lines = jnp.concatenate(
        [
            ref[ref.shape[0] - 2 * here + side * line : ref.shape[0] - 2 * here + (side + 1) * line, :]
            for side in range(2)
            for ref in slot_refs
        ],
        axis=0,
    )
    turn_ref[...] = turned(lines)
    step = LANES // degree
    lane = lax.broadcasted_iota(jnp.int32, (coarse, LANES), 1)
    table = jnp.zeros((coarse, LANES), f32)
    each = hot_ref.shape[0] // degree
    for k in range(degree):
        spread = position(turn_ref[pl.ds(k, step, stride=degree), :], flip, count, coarse)
        column = jnp.concatenate([spread[:, j : j + 1] for j in range(lines.shape[0])], axis=0)
        hot_ref[k * each : k * each + count, :] = equal(column[:count, :].astype(f32), coarse)
        high = jnp.right_shift(column, 8).astype(f32)
        low = jnp.bitwise_and(column, 255).astype(f32)
        table = jnp.where(lane == k, high, jnp.where(lane == degree + k, low, table))
    found = mm(parent_ref[...], table.astype(bf16))
    for k in range(degree):
        column = found[:, k : k + 1] * 256.0 + found[:, degree + k : degree + k + 1]
        hot_ref[k * each + count : (k + 1) * each, :] = equal(column, coarse)


def column_kernel(hot_ref, parent_ref, high_ref, low_ref, *refs):
    *blocks, got_ref, wanted_ref = refs
    _, width = wanted_ref.shape
    parts = width // LANES
    count = blocks[0].shape[0] // parts
    middle = jnp.concatenate([load_rows(b, count, parts) for b in blocks], axis=0)
    half = count * len(blocks)
    sends = halves(times(unit(middle), *weights(high_ref, low_ref, 0)) * 0.5)
    got_ref[...] = take(hot_ref[:, :half], *sends)
    wanted_ref[:count, :] = middle[:count, :]
    wanted_ref[count:, :] = take(parent_ref[:, :half], *halves(middle))


def coarse_kernel(
    last_ref, hot_ref, parent_ref, got_ref, wanted_ref, high_ref, low_ref, pack_ref, *refs
):
    *blocks, fine_ref, coarse_ref = refs
    rows, width = last_ref.shape
    parts = width // LANES
    count = coarse_ref.shape[0] // parts
    need = count + rows
    middle = jnp.concatenate([load_rows(b, count, parts) for b in blocks], axis=0)
    half = count * len(blocks)
    sends = halves(times(unit(middle), *weights(high_ref, low_ref, 0)) * 0.5)
    wanted = jnp.concatenate(
        [
            wanted_ref[:count, :],
            wanted_ref[count:, :] + take(parent_ref[:, half:], *halves(middle)),
        ],
        axis=0,
    )
    into = (times(unit(wanted), *weights(high_ref, low_ref, 1)) + pack_ref[3:4, :]) * 0.5
    total = None
    for k in range(hot_ref.shape[0] // need):
        part = slice(k * need, (k + 1) * need)
        term = gate(got_ref[part, :] + into + take(hot_ref[part, half:], *sends))
        total = term if total is None else total + term
    done = wanted + times(total, *weights(high_ref, low_ref, 2))
    store_rows(coarse_ref, done[:count, :], parts)
    act = gate(
        (times(unit(done[count:, :]), *weights(high_ref, low_ref, 3)) + pack_ref[4:5, :]) * 0.5
    )
    store_rows(fine_ref, last_ref[...] + times(act, *weights(high_ref, low_ref, 4)), parts)


VMEM = pl.BlockSpec(memory_space=pltpu.VMEM)
SMEM = pl.BlockSpec(memory_space=pltpu.SMEM)
HBM = pl.BlockSpec(memory_space=pltpu.HBM)


def call(kernel, in_specs, out_shapes, scratch=()):
    return pl.pallas_call(
        kernel,
        in_specs=in_specs,
        out_specs=[VMEM] * len(out_shapes),
        out_shape=out_shapes,
        scratch_shapes=scratch,
        compiler_params=pltpu.CompilerParams(vmem_limit_bytes=32 * 2**20),
    )


def move(values, pairs):
    return lax.ppermute(values, "sp", pairs)


def shape(*dims, kind=f32):
    return jax.ShapeDtypeStruct(dims, kind)


def kernel_shards(
    fine_state,
    coarse_state,
    fine_senders,
    up_owner,
    up_local,
    coarse_owner,
    coarse_local,
    fine_w_send,
    fine_w_recv,
    fine_bias,
    fine_w_out,
    up_w_in,
    up_bias,
    up_w_out,
    coarse_w_send,
    coarse_w_recv,
    coarse_bias,
    coarse_w_out,
    down_w_in,
    down_bias,
    down_w_out,
):
    peers = lax.axis_size("sp")
    me = lax.axis_index("sp").astype(jnp.int32)
    rows, _, width = fine_state.shape
    count = coarse_state.shape[0]
    parts = width // LANES
    edges = fine_senders.shape[0]
    coarse_edges = coarse_owner.shape[0]
    coarse = peers * count
    window = rows + 2 * HALO
    rim, own, full = HALO * parts, count * parts, rows * parts
    size = width
    swap = [(i, i ^ 1) for i in range(peers)]
    diag = [(i, (i + 1 if i % 2 else i - 1) % peers) for i in range(peers)]
    pair = [(i, (i + 2 if i % 2 else i - 2) % peers) for i in range(peers)]
    flips = [[(i, i ^ (2 * j)) for i in range(peers)] for j in range(peers // 2)]
    place = jnp.stack([me % 2, me * count])
    lines = lambda x: x.reshape(-1, LANES)
    row = lambda x: x.reshape(1, width)
    turn = pltpu.VMEM((LANES, LANES), f32)
    here = lambda *xs: [pltpu.with_memory_space_constraint(x, pltpu.HBM) for x in xs]
    hot_shape = shape(edges, window, kind=bf16)
    small = lambda ref: pltpu.VMEM(ref.shape, ref.dtype)

    small_args = [
        lines(fine_senders), lines(up_owner), lines(up_local), lines(coarse_owner),
        lines(coarse_local), fine_bias, row(up_bias), row(coarse_bias), row(down_bias),
    ]
    flat = lines(fine_state)
    out_swap = lax.dynamic_slice(flat, ((1 - me % 2) * (full - rim), 0), (rim, LANES))
    out_diag = lax.dynamic_slice(flat, (me % 2 * (full - rim), 0), (rim, LANES))
    swap0 = move(out_swap, swap)
    diag0 = move(out_diag, diag)
    state, ints, pack = call(
        functools.partial(start_kernel, count, HALO),
        [SMEM] + [HBM] * 10,
        [shape(full, LANES), shape(16, LANES), shape(8, width)],
        [small(x) for x in small_args] + [pltpu.SemaphoreType.DMA((10,))],
    )(place, *here(flat, *small_args))
    ints0 = move(ints, swap)
    hot, got, into, high, low = call(
        functools.partial(near_kernel, edges),
        [VMEM] * 2 + [HBM] * 3 + [VMEM],
        [hot_shape, shape(edges, width), shape(rows, width)]
        + [shape(2 * size, width, kind=bf16)] * 2,
        [turn] + [pltpu.VMEM((size, width), f32)] * 3 + [pltpu.SemaphoreType.DMA((3,))],
    )(state, ints, *here(fine_w_send, fine_w_recv, fine_w_out), pack)
    state, out_half = call(
        far_kernel, [SMEM] + [VMEM] * 8, [shape(full, LANES), shape(rim, LANES)]
    )(place, swap0, diag0, state, hot, got, into, high, low)
    swap1 = move(state, swap)
    diag1 = move(out_half, diag)
    pair1 = move(out_half, pair)
    got, into, own_high, own_low, hot2, select, high, low = call(
        functools.partial(near2_kernel, edges, count),
        [SMEM] + [VMEM] * 10,
        [shape(edges, width), shape(rows, width)]
        + [shape(rows, width, kind=bf16)] * 2
        + [hot_shape, shape(coarse // 2, 2 * rows, kind=bf16)]
        + [shape(5 * size, width, kind=bf16)] * 2,
        [turn],
    )(
        place, state, ints, ints0, hot, fine_w_send, fine_w_recv, fine_w_out, up_w_in, up_w_out,
        pack,
    )
    got2, diag_high, diag_low = call(
        halo_kernel,
        [SMEM] + [VMEM] * 7,
        [shape(edges, width)] + [shape(HALO, width, kind=bf16)] * 2,
    )(place, pair1, diag1, own_high, own_low, hot2, high, low)
    hidden, *slots = call(
        up_kernel,
        [SMEM] + [VMEM] * 15,
        [shape(rows, width)]
        + [shape(own + 8 * coarse_edges // 256, LANES)] * (peers // 2),
        [pltpu.VMEM((rows, width), bf16)] * 2,
    )(
        place, swap1, diag_high, diag_low, state, hot, got, into, hot2, got2, select, ints, ints0,
        high, low, pack,
    )
    arrived = [slots[0]] + [move(slots[j], flips[j]) for j in range(1, peers // 2)]
    (middle,) = call(
        middle_kernel, [VMEM] * (1 + peers // 2), [shape(own, LANES)]
    )(lines(coarse_state), *arrived)
    columns = [middle] + [move(middle, flips[j]) for j in range(1, peers // 2)]
    across = [move(block, swap) for block in columns]
    degree = coarse_edges // count
    coarse_hot, parent_hot = call(
        functools.partial(edges_kernel, degree, count),
        [SMEM] + [VMEM] * (1 + peers // 2),
        [
            shape(degree * (count + rows), coarse, kind=bf16),
            shape(rows, coarse, kind=bf16),
        ],
        [turn],
    )(place, ints, *arrived)
    high, low = call(
        split_kernel, [VMEM] * 5, [shape(5 * size, width, kind=bf16)] * 2
    )(coarse_w_send, coarse_w_recv, coarse_w_out, down_w_in, down_w_out)
    got, wanted = call(
        column_kernel,
        [VMEM] * (4 + peers // 2),
        [shape(degree * (count + rows), width), shape(count + rows, width)],
    )(coarse_hot, parent_hot, high, low, *columns)
    fine_out, coarse_out = call(
        coarse_kernel, [VMEM] * (8 + peers // 2), [shape(full, LANES), shape(own, LANES)]
    )(hidden, coarse_hot, parent_hot, got, wanted, high, low, pack, *across)
    return (fine_out.reshape(fine_state.shape), coarse_out.reshape(coarse_state.shape))


def shards(*args):
    fine_state, coarse_state, fine_senders = args[0], args[1], args[2]
    coarse_owner, layers = args[5], args[7].shape[0]
    peers = lax.axis_size("sp")
    rows, samples, width = fine_state.shape
    count = coarse_state.shape[0]
    fits = (
        samples == 1
        and layers == 2
        and width % LANES == 0
        and peers % 2 == 0
        and peers & (peers - 1) == 0
        and rows % LANES == 0
        and rows >= HALO
        and count & (count - 1) == 0
        and LANES % count == 0
        and coarse_owner.shape[0] % LANES == 0
        and coarse_owner.shape[0] == 4 * count
        and fine_senders.shape[0] == 8 * LANES
        and rows == 2 * LANES
        and coarse_owner.shape[0] == 2 * LANES
        and width == args[7].shape[2]
        and peers * count <= 1024
        and peers >= 4
        and rows >= 2 * HALO
    )
    if not fits:
        return general_shards(*args)
    return kernel_shards(*args)


def solution(mesh):
    in_specs = (
        P("sp", ("grp", "ch"), None),
        P("sp", ("grp", "ch"), None),
        P("sp"),
        P("sp", None),
        P("sp"),
        P("sp", None),
        P("sp"),
    ) + (P(),) * 14
    out_specs = (P("sp", ("grp", "ch"), None), P("sp", ("grp", "ch"), None))
    return jax.shard_map(shards, mesh=mesh, in_specs=in_specs, out_specs=out_specs, check_vma=False)
```

```python
import functools
import jax
import jax.numpy as jnp
from jax import lax
from jax.experimental import pallas as pl
from jax.experimental.pallas import tpu as pltpu
from jax.sharding import PartitionSpec as P

HALO = 128
LANES = 128


epsilon = 1e-05
highest = lax.Precision.HIGHEST


def extended_2(cells, sides, width):
    for axis, dim in sides:
        count = lax.axis_size(axis)
        head = lax.slice_in_dim(cells, 0, width, axis=dim)
        tail = lax.slice_in_dim(cells, cells.shape[dim] - width, cells.shape[dim], axis=dim)
        cells = jnp.concatenate(
            [
                lax.ppermute(tail, axis, [(i, (i + 1) % count) for i in range(count)]),
                cells,
                lax.ppermute(head, axis, [((i + 1) % count, i) for i in range(count)]),
            ],
            axis=dim,
        )
    return cells


def layer_norm(values):
    average = jnp.mean(values, axis=-1, keepdims=True)
    centered = values - average
    spread = jnp.mean(centered * centered, axis=-1, keepdims=True)
    return centered / jnp.sqrt(spread + epsilon)


def project(values, matrix):
    return jnp.einsum(
        "nsd,dh->nsh", values, matrix, precision=highest, preferred_element_type=jnp.float32
    )


def slot_ranks(owners, peer_count):
    matches = (owners[:, None] == jnp.arange(peer_count, dtype=jnp.int32)[None, :]).astype(
        jnp.int32
    )
    ranking = jnp.cumsum(matches, axis=0) - 1
    return jnp.sum(ranking * matches, axis=1)


def general_shards(
    fine_state,
    coarse_state,
    fine_senders,
    up_owner,
    up_local,
    coarse_owner,
    coarse_local,
    fine_w_send,
    fine_w_recv,
    fine_bias,
    fine_w_out,
    up_w_in,
    up_bias,
    up_w_out,
    coarse_w_send,
    coarse_w_recv,
    coarse_bias,
    coarse_w_out,
    down_w_in,
    down_bias,
    down_w_out,
):
    peer_count = lax.axis_size("sp")
    fine_rows = fine_state.shape[0]
    coarse_rows = coarse_state.shape[0]
    samples = fine_state.shape[1]
    feature_width = fine_state.shape[2]
    degree_fine = fine_senders.shape[0] // fine_rows
    degree_coarse = coarse_owner.shape[0] // coarse_rows
    hidden_state = fine_state
    for layer_index in range(fine_w_send.shape[0]):
        normed = layer_norm(hidden_state)
        outward = project(normed, fine_w_send[layer_index])
        inward = project(normed, fine_w_recv[layer_index]) + fine_bias[layer_index]
        extended = extended_2(outward, (("sp", 0),), HALO)
        gathered = extended[fine_senders].reshape(fine_rows, degree_fine, samples, -1)
        summed = jnp.sum(jax.nn.silu(gathered + inward[:, None]), axis=1)
        hidden_state = hidden_state + project(summed, fine_w_out[layer_index])
    capacity = max(4, 2 * fine_rows // peer_count)
    owners = up_owner[:, 0]
    places = owners * capacity + slot_ranks(owners, peer_count)
    targets = (
        jnp.full((peer_count * capacity,), -1.0, jnp.float32)
        .at[places]
        .set(up_local.astype(jnp.float32))
        .reshape(peer_count, capacity)
    )
    activated = jax.nn.silu(project(layer_norm(hidden_state), up_w_in) + up_bias)
    coarse_ids = jnp.arange(coarse_rows, dtype=jnp.float32)[:, None]
    messages = project(activated, up_w_out)
    outgoing = (
        jnp.zeros((peer_count * capacity, samples, feature_width), jnp.float32)
        .at[places]
        .set(messages)
        .reshape(peer_count, capacity, samples, feature_width)
    )
    arrived, sources = (
        lax.all_to_all(outgoing, "sp", split_axis=0, concat_axis=0, tiled=True),
        lax.all_to_all(targets, "sp", split_axis=0, concat_axis=0, tiled=True),
    )
    selector = (sources.reshape(1, -1) == coarse_ids).astype(jnp.float32)
    gained = jnp.einsum(
        "cr,rsd->csd",
        selector,
        arrived.reshape(peer_count * capacity, samples, feature_width),
        precision=highest,
        preferred_element_type=jnp.float32,
    )
    coarse = coarse_state + gained
    normed = layer_norm(coarse)
    outward = project(normed, coarse_w_send)
    inward = project(normed, coarse_w_recv) + coarse_bias
    anchor_owner = coarse_owner[:, 0]
    everything = lax.all_gather(outward, "sp", axis=0, tiled=True)
    picked = everything[anchor_owner * coarse_rows + coarse_local]
    edge_terms = picked.reshape(coarse_rows, degree_coarse, samples, -1)
    summed = jnp.sum(jax.nn.silu(edge_terms + inward[:, None]), axis=1)
    coarse_out = coarse + project(summed, coarse_w_out)
    downward = project(
        jax.nn.silu(project(layer_norm(coarse_out), down_w_in) + down_bias), down_w_out
    )
    wanted = jnp.maximum(sources.reshape(-1), 0.0).astype(jnp.int32)
    replies = downward[wanted].reshape(peer_count, capacity, samples, feature_width)
    answered = lax.all_to_all(replies, "sp", split_axis=0, concat_axis=0, tiled=True)
    fine_out = (
        hidden_state + answered.reshape(peer_count * capacity, samples, feature_width)[places]
    )
    return (fine_out, coarse_out)


f32 = jnp.float32
bf16 = jnp.bfloat16


def load_rows(ref, rows, parts, start=0):
    return jnp.concatenate(
        [ref[pl.ds(start * parts + j, rows, stride=parts), :] for j in range(parts)], axis=1
    )


def store_rows(ref, values, parts, start=0):
    for j in range(parts):
        ref[pl.ds(start * parts + j, values.shape[0], stride=parts), :] = values[
            :, j * LANES : (j + 1) * LANES
        ]


def halves(values):
    high = values.astype(bf16)
    return high, (values - high.astype(f32)).astype(bf16)


def mm(a, b):
    return jnp.dot(a, b, preferred_element_type=f32)


def times(values, high, low):
    vh, vl = halves(values)
    return mm(vh, high) + (mm(vl, high) + mm(vh, low))


def take(one_hot, high, low):
    return mm(one_hot, high) + mm(one_hot, low)


def place():
    return lax.axis_index("sp").astype(jnp.int32)


def unit(values):
    width = values.shape[1]
    average = jnp.sum(values, axis=1, keepdims=True) * (1.0 / width)
    centered = values - average
    spread = jnp.sum(centered * centered, axis=1, keepdims=True) * (1.0 / width)
    return centered * lax.rsqrt(spread + epsilon)


def gate(half):
    return half + half * jnp.tanh(half)


def equal(column, count):
    ids = lax.broadcasted_iota(jnp.int32, (column.shape[0], count), 1).astype(f32)
    return jnp.where(ids == column, 1.0, 0.0).astype(bf16)


def turned(lines):
    pad = jnp.zeros((LANES - lines.shape[0], LANES), f32)
    return jnp.transpose(jnp.concatenate([lines, pad], axis=0))


def edge_hot(hot_ref, turn_ref, lines, degree, nodes, flip=None):
    turn_ref[...] = turned(lines)
    step = LANES // degree
    for k in range(degree):
        spread = turn_ref[pl.ds(k, step, stride=degree), :]
        if flip is not None:
            spread = jnp.bitwise_xor(spread.astype(jnp.int32), flip).astype(f32)
        for line in range(lines.shape[0]):
            start = k * nodes + line * step
            hot_ref[start : start + step, :] = equal(
                spread[:, line : line + 1], hot_ref.shape[1]
            )


def split_into(high_ref, low_ref, *matrices):
    for j, matrix in enumerate(matrices):
        size = matrix.shape[0]
        high_ref[j * size : (j + 1) * size, :], low_ref[j * size : (j + 1) * size, :] = halves(
            matrix
        )


def weights(high_ref, low_ref, j):
    size = high_ref.shape[1]
    return high_ref[j * size : (j + 1) * size, :], low_ref[j * size : (j + 1) * size, :]


def start_kernel(
    count, halo, state_hbm, sender_hbm, owner_hbm, local_hbm, cowner_hbm,
    clocal_hbm, fb_hbm, ub_hbm, cb_hbm, db_hbm,
    state_ref, ints_ref, pack_ref,
    sender_ref, owner_ref, local_ref, cowner_ref, clocal_ref, fb_ref, ub_ref, cb_ref, db_ref,
    sems,
):
    odd = place() % 2
    pairs = [
        (sender_hbm, sender_ref),
        (owner_hbm, owner_ref),
        (local_hbm, local_ref),
        (cowner_hbm, cowner_ref),
        (clocal_hbm, clocal_ref),
        (fb_hbm, fb_ref),
        (ub_hbm, ub_ref),
        (cb_hbm, cb_ref),
        (db_hbm, db_ref),
        (state_hbm, state_ref),
    ]
    copies = [pltpu.make_async_copy(a, b, sems.at[j]) for j, (a, b) in enumerate(pairs)]
    for copy in copies:
        copy.start()
    for copy in copies[:-1]:
        copy.wait()
    rows = state_hbm.shape[0] * LANES // fb_ref.shape[1]
    sender = sender_ref[...]
    before = rows + (1 - odd) * halo
    after = rows + odd * halo
    index = jnp.where(
        sender < halo,
        sender + before,
        jnp.where(sender < halo + rows, sender - halo, sender - (halo + rows) + after),
    )
    lines = [
        index.astype(f32),
        (owner_ref[...] * count + local_ref[...]).astype(f32),
        (cowner_ref[...] * count + clocal_ref[...]).astype(f32),
    ]
    rest = ints_ref.shape[0] - sum(x.shape[0] for x in lines)
    ints_ref[...] = jnp.concatenate(lines + [jnp.zeros((rest, LANES), f32)], axis=0)
    pack_ref[...] = jnp.concatenate(
        [fb_ref[...], ub_ref[...], cb_ref[...], db_ref[...]]
        + [jnp.zeros((3, fb_ref.shape[1]), f32)],
        axis=0,
    )
    copies[-1].wait()


def near_kernel(
    edges, state_ref, ints_ref, ws_hbm, wr_hbm, wo_hbm, pack_ref,
    hot_ref, got_ref, into_ref, high_ref, low_ref, turn_ref, ws_ref, wr_ref, wo_ref, sems,
):
    rows, width = into_ref.shape
    parts = width // LANES
    pairs = ((ws_hbm, ws_ref), (wr_hbm, wr_ref), (wo_hbm, wo_ref))
    copies = [
        pltpu.make_async_copy(a.at[0], b, sems.at[j]) for j, (a, b) in enumerate(pairs)
    ]
    for copy in copies:
        copy.start()
    edge_hot(hot_ref, turn_ref, ints_ref[: edges // LANES, :], edges // rows, rows)
    normed = unit(load_rows(state_ref, rows, parts))
    for copy in copies:
        copy.wait()
    split_into(high_ref, low_ref, ws_ref[...], wo_ref[...])
    into_ref[...] = (times(normed, *halves(wr_ref[...])) + pack_ref[0:1, :]) * 0.5
    high, low = halves(times(normed, *weights(high_ref, low_ref, 0)) * 0.5)
    got_ref[...] = take(hot_ref[:, :rows], high, low)


def far_kernel(
    swap_ref, diag_ref, ints0_ref, state_ref, hot_ref, got_ref, into_ref, high_ref, low_ref,
    out_full_ref, out_half_ref,
):
    rows, width = into_ref.shape
    parts = width // LANES
    rim = diag_ref.shape[0] // parts
    degree = hot_ref.shape[0] // rows
    far = jnp.concatenate(
        [load_rows(swap_ref, rim, parts), load_rows(diag_ref, rim, parts)], axis=0
    )
    high, low = halves(times(unit(far), *weights(high_ref, low_ref, 0)) * 0.5)
    total = None
    for k in range(degree):
        part = slice(k * rows, (k + 1) * rows)
        half = got_ref[part, :] + into_ref[...] + take(hot_ref[part, rows:], high, low)
        total = gate(half) if total is None else total + gate(half)
    store_rows(
        out_full_ref,
        load_rows(state_ref, rows, parts) + times(total, *weights(high_ref, low_ref, 1)),
        parts,
    )
    lines = out_half_ref.shape[0]
    start = pl.multiple_of(place() % 2 * (rows * parts - lines), LANES)
    out_half_ref[...] = out_full_ref[pl.ds(start, lines), :]


def near2_kernel(
    edges, count, state_ref, ints_ref, ints0_ref, hot_ref, ws_ref, wr_ref, wo_ref, wi_ref,
    wu_ref, pack_ref,
    got_ref, into_ref, own_high_ref, own_low_ref, hot2_ref, select_ref, high_ref, low_ref,
    turn_ref,
):
    rows, width = into_ref.shape
    parts = width // LANES
    senders = edges // LANES
    split_into(
        high_ref, low_ref, ws_ref[1], wr_ref[1], wo_ref[1], wi_ref[...], wu_ref[...]
    )
    normed = unit(load_rows(state_ref, rows, parts))
    into_ref[...] = (times(normed, *weights(high_ref, low_ref, 1)) + pack_ref[1:2, :]) * 0.5
    high, low = halves(times(normed, *weights(high_ref, low_ref, 0)) * 0.5)
    own_high_ref[...] = high
    own_low_ref[...] = low
    got_ref[...] = take(hot_ref[:, :rows], high, low)
    edge_hot(hot2_ref, turn_ref, ints0_ref[:senders, :], edges // rows, rows)
    flip = place() * count
    line = senders
    for half, ref in ((0, ints_ref), (1, ints0_ref)):
        for j in range(rows // LANES):
            parent = ref[line + j : line + j + 1, :].astype(jnp.int32)
            parent = jnp.bitwise_xor(parent, flip)
            ids = lax.broadcasted_iota(jnp.int32, (select_ref.shape[0], LANES), 0)
            ids = ids + jnp.bitwise_and(ids, -count)
            start = half * rows + j * LANES
            select_ref[:, start : start + LANES] = jnp.where(ids == parent, 1.0, 0.0).astype(
                bf16
            )


def up_kernel(
    swap_ref, pair_ref, diag_ref, state_ref, hot_ref, got_ref, into_ref, own_high_ref,
    own_low_ref, hot2_ref, select_ref, ints_ref, ints0_ref, high_ref, low_ref, pack_ref,
    last_ref, *refs,
):
    *slot_refs, th_ref, tl_ref = refs
    rows, width = into_ref.shape
    parts = width // LANES
    rim = diag_ref.shape[0] // parts
    degree = hot_ref.shape[0] // rows
    odd = place() % 2
    mine = pl.multiple_of((1 - odd) * (rows - rim), LANES)
    theirs = pl.multiple_of(odd * (rows - rim), LANES)
    other = load_rows(swap_ref, rows, parts)
    normed = unit(
        jnp.concatenate(
            [other, load_rows(pair_ref, rim, parts), load_rows(diag_ref, rim, parts)], axis=0
        )
    )
    sends = halves(times(normed, *weights(high_ref, low_ref, 0)) * 0.5)
    near = []
    for src, t_ref, own_ref in (
        (sends[0], th_ref, own_high_ref), (sends[1], tl_ref, own_low_ref),
    ):
        t_ref[:rows, :] = src[:rows, :]
        t_ref[rows : rows + rim, :] = own_ref[pl.ds(mine, rim), :]
        t_ref[rows + rim :, :] = src[rows : rows + rim, :]
        near.append(
            jnp.concatenate([t_ref[pl.ds(theirs, rim), :], src[rows + rim :, :]], axis=0)
        )
    into = (times(normed[:rows, :], *weights(high_ref, low_ref, 1)) + pack_ref[1:2, :]) * 0.5
    total, total2 = None, None
    for k in range(degree):
        part = slice(k * rows, (k + 1) * rows)
        half = got_ref[part, :] + into_ref[...] + take(hot_ref[part, rows:], *near)
        total = gate(half) if total is None else total + gate(half)
        half = into + take(hot2_ref[part, :], th_ref[...], tl_ref[...])
        total2 = gate(half) if total2 is None else total2 + gate(half)
    hidden = jnp.concatenate([load_rows(state_ref, rows, parts), other], axis=0) + times(
        jnp.concatenate([total, total2], axis=0), *weights(high_ref, low_ref, 2)
    )
    last_ref[...] = hidden[:rows, :]
    act = gate((times(unit(hidden), *weights(high_ref, low_ref, 3)) + pack_ref[2:3, :]) * 0.5)
    sums = take(select_ref[...], *halves(times(act, *weights(high_ref, low_ref, 4))))
    size = sums.shape[0] // len(slot_refs)
    first = hot_ref.shape[0] // LANES + rows // LANES
    anchor = (slot_refs[0].shape[0] - size * parts) // 4
    for j, slot in enumerate(slot_refs):
        store_rows(slot, sums[j * size : (j + 1) * size, :], parts)
        slot[size * parts :, :] = jnp.concatenate(
            [
                ints_ref[first : first + anchor, :],
                ints0_ref[first : first + anchor, :],
                jnp.zeros((2 * anchor, LANES), f32),
            ],
            axis=0,
        )


def middle_kernel(state_ref, *refs):
    out_ref = refs[-1]
    total = state_ref[...]
    for ref in refs[:-1]:
        total = total + ref[: out_ref.shape[0], :]
    out_ref[...] = total


def position(ids, flip, count, coarse):
    ids = jnp.bitwise_xor(ids.astype(jnp.int32), flip)
    slot = jnp.right_shift(ids, count.bit_length() - 1)
    return (
        jnp.bitwise_and(ids, count - 1)
        + jnp.right_shift(slot, 1) * count
        + jnp.bitwise_and(slot, 1) * (coarse // 2)
    )


def split_kernel(cs_ref, cr_ref, co_ref, di_ref, do_ref, high_ref, low_ref):
    split_into(
        high_ref, low_ref, cs_ref[...], cr_ref[...], co_ref[...], di_ref[...], do_ref[...]
    )


def edges_kernel(degree, count, ints_ref, *refs):
    *slot_refs, hot_ref, parent_ref, turn_ref = refs
    rows, coarse = parent_ref.shape
    flip = place() * count
    columns = turned(ints_ref[...])
    first = ints_ref.shape[0] // 2
    for j in range(rows // LANES):
        column = position(columns[:, first + j : first + j + 1], flip, count, coarse).astype(f32)
        parent_ref[j * LANES : (j + 1) * LANES, :] = equal(column, coarse)
    here = coarse * degree // LANES // len(slot_refs)
    line = here // 2
    lines = jnp.concatenate(
        [
            ref[ref.shape[0] - 2 * here + side * line : ref.shape[0] - 2 * here + (side + 1) * line, :]
            for side in range(2)
            for ref in slot_refs
        ],
        axis=0,
    )
    turn_ref[...] = turned(lines)
    step = LANES // degree
    lane = lax.broadcasted_iota(jnp.int32, (coarse, LANES), 1)
    table = jnp.zeros((coarse, LANES), f32)
    each = hot_ref.shape[0] // degree
    for k in range(degree):
        spread = position(turn_ref[pl.ds(k, step, stride=degree), :], flip, count, coarse)
        column = jnp.concatenate([spread[:, j : j + 1] for j in range(lines.shape[0])], axis=0)
        hot_ref[k * each : k * each + count, :] = equal(column[:count, :].astype(f32), coarse)
        high = jnp.right_shift(column, 8).astype(f32)
        low = jnp.bitwise_and(column, 255).astype(f32)
        table = jnp.where(lane == k, high, jnp.where(lane == degree + k, low, table))
    found = mm(parent_ref[...], table.astype(bf16))
    for k in range(degree):
        column = found[:, k : k + 1] * 256.0 + found[:, degree + k : degree + k + 1]
        hot_ref[k * each + count : (k + 1) * each, :] = equal(column, coarse)


def column_kernel(hot_ref, parent_ref, high_ref, low_ref, *refs):
    *blocks, got_ref, wanted_ref = refs
    _, width = wanted_ref.shape
    parts = width // LANES
    count = blocks[0].shape[0] // parts
    middle = jnp.concatenate([load_rows(b, count, parts) for b in blocks], axis=0)
    half = count * len(blocks)
    sends = halves(times(unit(middle), *weights(high_ref, low_ref, 0)) * 0.5)
    got_ref[...] = take(hot_ref[:, :half], *sends)
    wanted_ref[:count, :] = middle[:count, :]
    wanted_ref[count:, :] = take(parent_ref[:, :half], *halves(middle))


def coarse_kernel(
    last_ref, hot_ref, parent_ref, got_ref, wanted_ref, high_ref, low_ref, pack_ref, *refs
):
    *blocks, fine_hbm, coarse_hbm, fine_ref, coarse_ref, sems = refs
    rows, width = last_ref.shape
    parts = width // LANES
    count = coarse_ref.shape[0] // parts
    need = count + rows
    middle = jnp.concatenate([load_rows(b, count, parts) for b in blocks], axis=0)
    half = count * len(blocks)
    sends = halves(times(unit(middle), *weights(high_ref, low_ref, 0)) * 0.5)
    wanted = jnp.concatenate(
        [
            wanted_ref[:count, :],
            wanted_ref[count:, :] + take(parent_ref[:, half:], *halves(middle)),
        ],
        axis=0,
    )
    into = (times(unit(wanted), *weights(high_ref, low_ref, 1)) + pack_ref[3:4, :]) * 0.5
    total = None
    for k in range(hot_ref.shape[0] // need):
        part = slice(k * need, (k + 1) * need)
        term = gate(got_ref[part, :] + into + take(hot_ref[part, half:], *sends))
        total = term if total is None else total + term
    done = wanted + times(total, *weights(high_ref, low_ref, 2))
    store_rows(coarse_ref, done[:count, :], parts)
    copies = [pltpu.make_async_copy(coarse_ref, coarse_hbm, sems.at[0])]
    copies[0].start()
    act = gate(
        (times(unit(done[count:, :]), *weights(high_ref, low_ref, 3)) + pack_ref[4:5, :]) * 0.5
    )
    size = rows // 2
    for j in range(2):
        down = times(act[j * size : (j + 1) * size, :], *weights(high_ref, low_ref, 4))
        store_rows(fine_ref, last_ref[j * size : (j + 1) * size, :] + down, parts, j * size)
        piece = pl.ds(j * size * parts, size * parts)
        copies.append(
            pltpu.make_async_copy(fine_ref.at[piece, :], fine_hbm.at[piece, :], sems.at[j + 1])
        )
        copies[-1].start()
    for copy in copies:
        copy.wait()


VMEM = pl.BlockSpec(memory_space=pltpu.VMEM)
SMEM = pl.BlockSpec(memory_space=pltpu.SMEM)
HBM = pl.BlockSpec(memory_space=pltpu.HBM)


def call(kernel, in_specs, out_shapes, scratch=(), out_spec=VMEM):
    return pl.pallas_call(
        kernel,
        in_specs=in_specs,
        out_specs=[out_spec] * len(out_shapes),
        out_shape=out_shapes,
        scratch_shapes=scratch,
        compiler_params=pltpu.CompilerParams(vmem_limit_bytes=32 * 2**20),
    )


def move(values, pairs):
    return lax.ppermute(values, "sp", pairs)


def shape(*dims, kind=f32):
    return jax.ShapeDtypeStruct(dims, kind)


def kernel_shards(
    fine_state,
    coarse_state,
    fine_senders,
    up_owner,
    up_local,
    coarse_owner,
    coarse_local,
    fine_w_send,
    fine_w_recv,
    fine_bias,
    fine_w_out,
    up_w_in,
    up_bias,
    up_w_out,
    coarse_w_send,
    coarse_w_recv,
    coarse_bias,
    coarse_w_out,
    down_w_in,
    down_bias,
    down_w_out,
):
    peers = lax.axis_size("sp")
    me = lax.axis_index("sp").astype(jnp.int32)
    rows, _, width = fine_state.shape
    count = coarse_state.shape[0]
    parts = width // LANES
    edges = fine_senders.shape[0]
    coarse_edges = coarse_owner.shape[0]
    coarse = peers * count
    window = rows + 2 * HALO
    rim, own, full = HALO * parts, count * parts, rows * parts
    size = width
    swap = [(i, i ^ 1) for i in range(peers)]
    diag = [(i, (i + 1 if i % 2 else i - 1) % peers) for i in range(peers)]
    pair = [(i, (i + 2 if i % 2 else i - 2) % peers) for i in range(peers)]
    flips = [[(i, i ^ (2 * j)) for i in range(peers)] for j in range(peers // 2)]
    lines = lambda x: x.reshape(-1, LANES)
    row = lambda x: x.reshape(1, width)
    turn = pltpu.VMEM((LANES, LANES), f32)
    here = lambda *xs: [pltpu.with_memory_space_constraint(x, pltpu.HBM) for x in xs]
    hot_shape = shape(edges, window, kind=bf16)
    small = lambda ref: pltpu.VMEM(ref.shape, ref.dtype)

    small_args = [
        lines(fine_senders), lines(up_owner), lines(up_local), lines(coarse_owner),
        lines(coarse_local), fine_bias, row(up_bias), row(coarse_bias), row(down_bias),
    ]
    flat = lines(fine_state)
    out_swap = lax.dynamic_slice(flat, ((1 - me % 2) * (full - rim), 0), (rim, LANES))
    out_diag = lax.dynamic_slice(flat, (me % 2 * (full - rim), 0), (rim, LANES))
    swap0 = move(out_swap, swap)
    diag0 = move(out_diag, diag)
    state, ints, pack = call(
        functools.partial(start_kernel, count, HALO),
        [HBM] * 10,
        [shape(full, LANES), shape(16, LANES), shape(8, width)],
        [small(x) for x in small_args] + [pltpu.SemaphoreType.DMA((10,))],
    )(*here(flat, *small_args))
    ints0 = move(ints, swap)
    hot, got, into, high, low = call(
        functools.partial(near_kernel, edges),
        [VMEM] * 2 + [HBM] * 3 + [VMEM],
        [hot_shape, shape(edges, width), shape(rows, width)]
        + [shape(2 * size, width, kind=bf16)] * 2,
        [turn] + [pltpu.VMEM((size, width), f32)] * 3 + [pltpu.SemaphoreType.DMA((3,))],
    )(state, ints, *here(fine_w_send, fine_w_recv, fine_w_out), pack)
    state, out_half = call(
        far_kernel, [VMEM] * 9, [shape(full, LANES), shape(rim, LANES)]
    )(swap0, diag0, ints0, state, hot, got, into, high, low)
    swap1 = move(state, swap)
    diag1 = move(out_half, diag)
    pair1 = move(out_half, pair)
    got, into, own_high, own_low, hot2, select, high, low = call(
        functools.partial(near2_kernel, edges, count),
        [VMEM] * 10,
        [shape(edges, width), shape(rows, width)]
        + [shape(rows, width, kind=bf16)] * 2
        + [hot_shape, shape(coarse // 2, 2 * rows, kind=bf16)]
        + [shape(5 * size, width, kind=bf16)] * 2,
        [turn],
    )(
        state, ints, ints0, hot, fine_w_send, fine_w_recv, fine_w_out, up_w_in, up_w_out,
        pack,
    )
    hidden, *slots = call(
        up_kernel,
        [VMEM] * 16,
        [shape(rows, width)]
        + [shape(own + 8 * coarse_edges // 256, LANES)] * (peers // 2),
        [pltpu.VMEM((window, width), bf16)] * 2,
    )(
        swap1, pair1, diag1, state, hot, got, into, own_high, own_low, hot2, select, ints, ints0,
        high, low, pack,
    )
    arrived = [slots[0]] + [move(slots[j], flips[j]) for j in range(1, peers // 2)]
    (middle,) = call(
        middle_kernel, [VMEM] * (1 + peers // 2), [shape(own, LANES)]
    )(lines(coarse_state), *arrived)
    columns = [middle] + [move(middle, flips[j]) for j in range(1, peers // 2)]
    across = [move(block, swap) for block in columns]
    degree = coarse_edges // count
    coarse_hot, parent_hot = call(
        functools.partial(edges_kernel, degree, count),
        [VMEM] * (1 + peers // 2),
        [
            shape(degree * (count + rows), coarse, kind=bf16),
            shape(rows, coarse, kind=bf16),
        ],
        [turn],
    )(ints, *arrived)
    high, low = call(
        split_kernel, [VMEM] * 5, [shape(5 * size, width, kind=bf16)] * 2
    )(coarse_w_send, coarse_w_recv, coarse_w_out, down_w_in, down_w_out)
    got, wanted = call(
        column_kernel,
        [VMEM] * (4 + peers // 2),
        [shape(degree * (count + rows), width), shape(count + rows, width)],
    )(coarse_hot, parent_hot, high, low, *columns)
    fine_out, coarse_out = call(
        coarse_kernel,
        [VMEM] * (8 + peers // 2),
        [shape(full, LANES), shape(own, LANES)],
        [
            pltpu.VMEM((full, LANES), f32), pltpu.VMEM((own, LANES), f32),
            pltpu.SemaphoreType.DMA((3,)),
        ],
        HBM,
    )(hidden, coarse_hot, parent_hot, got, wanted, high, low, pack, *across)
    return (fine_out.reshape(fine_state.shape), coarse_out.reshape(coarse_state.shape))


def shards(*args):
    fine_state, coarse_state, fine_senders = args[0], args[1], args[2]
    coarse_owner, layers = args[5], args[7].shape[0]
    peers = lax.axis_size("sp")
    rows, samples, width = fine_state.shape
    count = coarse_state.shape[0]
    fits = (
        samples == 1
        and layers == 2
        and width % LANES == 0
        and peers % 2 == 0
        and peers & (peers - 1) == 0
        and rows % LANES == 0
        and rows >= HALO
        and count & (count - 1) == 0
        and LANES % count == 0
        and coarse_owner.shape[0] % LANES == 0
        and coarse_owner.shape[0] == 4 * count
        and fine_senders.shape[0] == 8 * LANES
        and rows == 2 * LANES
        and coarse_owner.shape[0] == 2 * LANES
        and width == args[7].shape[2]
        and peers * count <= 1024
        and peers >= 4
        and rows >= 2 * HALO
    )
    if not fits:
        return general_shards(*args)
    return kernel_shards(*args)


def solution(mesh):
    in_specs = (
        P("sp", ("grp", "ch"), None),
        P("sp", ("grp", "ch"), None),
        P("sp"),
        P("sp", None),
        P("sp"),
        P("sp", None),
        P("sp"),
    ) + (P(),) * 14
    out_specs = (P("sp", ("grp", "ch"), None), P("sp", ("grp", "ch"), None))
    return jax.shard_map(shards, mesh=mesh, in_specs=in_specs, out_specs=out_specs, check_vma=False)
```

```python
import functools
import jax
import jax.numpy as jnp
from jax import lax
from jax.experimental import pallas as pl
from jax.experimental.pallas import tpu as pltpu
from jax.sharding import PartitionSpec as P

HALO = 128
LANES = 128


epsilon = 1e-05
highest = lax.Precision.HIGHEST


def extended_2(cells, sides, width):
    for axis, dim in sides:
        count = lax.axis_size(axis)
        head = lax.slice_in_dim(cells, 0, width, axis=dim)
        tail = lax.slice_in_dim(cells, cells.shape[dim] - width, cells.shape[dim], axis=dim)
        cells = jnp.concatenate(
            [
                lax.ppermute(tail, axis, [(i, (i + 1) % count) for i in range(count)]),
                cells,
                lax.ppermute(head, axis, [((i + 1) % count, i) for i in range(count)]),
            ],
            axis=dim,
        )
    return cells


def layer_norm(values):
    average = jnp.mean(values, axis=-1, keepdims=True)
    centered = values - average
    spread = jnp.mean(centered * centered, axis=-1, keepdims=True)
    return centered / jnp.sqrt(spread + epsilon)


def project(values, matrix):
    return jnp.einsum(
        "nsd,dh->nsh", values, matrix, precision=highest, preferred_element_type=jnp.float32
    )


def slot_ranks(owners, peer_count):
    matches = (owners[:, None] == jnp.arange(peer_count, dtype=jnp.int32)[None, :]).astype(
        jnp.int32
    )
    ranking = jnp.cumsum(matches, axis=0) - 1
    return jnp.sum(ranking * matches, axis=1)


def general_shards(
    fine_state,
    coarse_state,
    fine_senders,
    up_owner,
    up_local,
    coarse_owner,
    coarse_local,
    fine_w_send,
    fine_w_recv,
    fine_bias,
    fine_w_out,
    up_w_in,
    up_bias,
    up_w_out,
    coarse_w_send,
    coarse_w_recv,
    coarse_bias,
    coarse_w_out,
    down_w_in,
    down_bias,
    down_w_out,
):
    peer_count = lax.axis_size("sp")
    fine_rows = fine_state.shape[0]
    coarse_rows = coarse_state.shape[0]
    samples = fine_state.shape[1]
    feature_width = fine_state.shape[2]
    degree_fine = fine_senders.shape[0] // fine_rows
    degree_coarse = coarse_owner.shape[0] // coarse_rows
    hidden_state = fine_state
    for layer_index in range(fine_w_send.shape[0]):
        normed = layer_norm(hidden_state)
        outward = project(normed, fine_w_send[layer_index])
        inward = project(normed, fine_w_recv[layer_index]) + fine_bias[layer_index]
        extended = extended_2(outward, (("sp", 0),), HALO)
        gathered = extended[fine_senders].reshape(fine_rows, degree_fine, samples, -1)
        summed = jnp.sum(jax.nn.silu(gathered + inward[:, None]), axis=1)
        hidden_state = hidden_state + project(summed, fine_w_out[layer_index])
    capacity = max(4, 2 * fine_rows // peer_count)
    owners = up_owner[:, 0]
    places = owners * capacity + slot_ranks(owners, peer_count)
    targets = (
        jnp.full((peer_count * capacity,), -1.0, jnp.float32)
        .at[places]
        .set(up_local.astype(jnp.float32))
        .reshape(peer_count, capacity)
    )
    activated = jax.nn.silu(project(layer_norm(hidden_state), up_w_in) + up_bias)
    coarse_ids = jnp.arange(coarse_rows, dtype=jnp.float32)[:, None]
    messages = project(activated, up_w_out)
    outgoing = (
        jnp.zeros((peer_count * capacity, samples, feature_width), jnp.float32)
        .at[places]
        .set(messages)
        .reshape(peer_count, capacity, samples, feature_width)
    )
    arrived, sources = (
        lax.all_to_all(outgoing, "sp", split_axis=0, concat_axis=0, tiled=True),
        lax.all_to_all(targets, "sp", split_axis=0, concat_axis=0, tiled=True),
    )
    selector = (sources.reshape(1, -1) == coarse_ids).astype(jnp.float32)
    gained = jnp.einsum(
        "cr,rsd->csd",
        selector,
        arrived.reshape(peer_count * capacity, samples, feature_width),
        precision=highest,
        preferred_element_type=jnp.float32,
    )
    coarse = coarse_state + gained
    normed = layer_norm(coarse)
    outward = project(normed, coarse_w_send)
    inward = project(normed, coarse_w_recv) + coarse_bias
    anchor_owner = coarse_owner[:, 0]
    everything = lax.all_gather(outward, "sp", axis=0, tiled=True)
    picked = everything[anchor_owner * coarse_rows + coarse_local]
    edge_terms = picked.reshape(coarse_rows, degree_coarse, samples, -1)
    summed = jnp.sum(jax.nn.silu(edge_terms + inward[:, None]), axis=1)
    coarse_out = coarse + project(summed, coarse_w_out)
    downward = project(
        jax.nn.silu(project(layer_norm(coarse_out), down_w_in) + down_bias), down_w_out
    )
    wanted = jnp.maximum(sources.reshape(-1), 0.0).astype(jnp.int32)
    replies = downward[wanted].reshape(peer_count, capacity, samples, feature_width)
    answered = lax.all_to_all(replies, "sp", split_axis=0, concat_axis=0, tiled=True)
    fine_out = (
        hidden_state + answered.reshape(peer_count * capacity, samples, feature_width)[places]
    )
    return (fine_out, coarse_out)


f32 = jnp.float32
bf16 = jnp.bfloat16


def load_rows(ref, rows, parts, start=0):
    return jnp.concatenate(
        [ref[pl.ds(start * parts + j, rows, stride=parts), :] for j in range(parts)], axis=1
    )


def store_rows(ref, values, parts, start=0):
    for j in range(parts):
        ref[pl.ds(start * parts + j, values.shape[0], stride=parts), :] = values[
            :, j * LANES : (j + 1) * LANES
        ]


def halves(values):
    high = values.astype(bf16)
    return high, (values - high.astype(f32)).astype(bf16)


def mm(a, b):
    return jnp.dot(a, b, preferred_element_type=f32)


def times(values, high, low):
    vh, vl = halves(values)
    return mm(vh, high) + (mm(vl, high) + mm(vh, low))


def take(one_hot, high, low):
    return mm(one_hot, high) + mm(one_hot, low)


def place():
    return lax.axis_index("sp").astype(jnp.int32)


def unit(values):
    width = values.shape[1]
    average = jnp.sum(values, axis=1, keepdims=True) * (1.0 / width)
    centered = values - average
    spread = jnp.sum(centered * centered, axis=1, keepdims=True) * (1.0 / width)
    return centered * lax.rsqrt(spread + epsilon)


def gate(half):
    return half + half * jnp.tanh(half)


def equal(column, count):
    ids = lax.broadcasted_iota(jnp.int32, (column.shape[0], count), 1).astype(f32)
    return jnp.where(ids == column, 1.0, 0.0).astype(bf16)


def turned(lines):
    pad = jnp.zeros((LANES - lines.shape[0], LANES), f32)
    return jnp.transpose(jnp.concatenate([lines, pad], axis=0))


def edge_hot(hot_ref, turn_ref, lines, degree, nodes, flip=None):
    turn_ref[...] = turned(lines)
    step = LANES // degree
    for k in range(degree):
        spread = turn_ref[pl.ds(k, step, stride=degree), :]
        if flip is not None:
            spread = jnp.bitwise_xor(spread.astype(jnp.int32), flip).astype(f32)
        for line in range(lines.shape[0]):
            start = k * nodes + line * step
            hot_ref[start : start + step, :] = equal(
                spread[:, line : line + 1], hot_ref.shape[1]
            )


def split_into(high_ref, low_ref, *matrices):
    for j, matrix in enumerate(matrices):
        size = matrix.shape[0]
        high_ref[j * size : (j + 1) * size, :], low_ref[j * size : (j + 1) * size, :] = halves(
            matrix
        )


def weights(high_ref, low_ref, j):
    size = high_ref.shape[1]
    return high_ref[j * size : (j + 1) * size, :], low_ref[j * size : (j + 1) * size, :]


def start_kernel(
    count, halo, state_hbm, sender_hbm, owner_hbm, local_hbm, cowner_hbm,
    clocal_hbm, fb_hbm, ub_hbm, cb_hbm, db_hbm,
    state_ref, ints_ref, pack_ref, swap_ref, diag_ref,
    sender_ref, owner_ref, local_ref, cowner_ref, clocal_ref, fb_ref, ub_ref, cb_ref, db_ref,
    sems,
):
    odd = place() % 2
    rim = diag_ref.shape[0]
    far = state_hbm.shape[0] - rim
    mine = pl.ds(pl.multiple_of((1 - odd) * far, LANES), rim)
    away = pl.ds(pl.multiple_of(odd * far, LANES), rim)
    pairs = [
        (sender_hbm, sender_ref),
        (owner_hbm, owner_ref),
        (local_hbm, local_ref),
        (cowner_hbm, cowner_ref),
        (clocal_hbm, clocal_ref),
        (fb_hbm, fb_ref),
        (ub_hbm, ub_ref),
        (cb_hbm, cb_ref),
        (db_hbm, db_ref),
        (state_hbm.at[mine, :], swap_ref.at[0:rim, :]),
        (state_hbm.at[away, :], diag_ref),
        (state_hbm, state_ref),
    ]
    copies = [pltpu.make_async_copy(a, b, sems.at[j]) for j, (a, b) in enumerate(pairs)]
    for copy in copies:
        copy.start()
    for copy in copies[:-3]:
        copy.wait()
    rows = state_hbm.shape[0] * LANES // fb_ref.shape[1]
    sender = sender_ref[...]
    before = rows + (1 - odd) * halo
    after = rows + odd * halo
    index = jnp.where(
        sender < halo,
        sender + before,
        jnp.where(sender < halo + rows, sender - halo, sender - (halo + rows) + after),
    )
    lines = [
        index.astype(f32),
        (owner_ref[...] * count + local_ref[...]).astype(f32),
        (cowner_ref[...] * count + clocal_ref[...]).astype(f32),
    ]
    rest = ints_ref.shape[0] - sum(x.shape[0] for x in lines)
    ints = jnp.concatenate(lines + [jnp.zeros((rest, LANES), f32)], axis=0)
    ints_ref[...] = ints
    swap_ref[rim:, :] = ints
    pack_ref[...] = jnp.concatenate(
        [fb_ref[...], ub_ref[...], cb_ref[...], db_ref[...]]
        + [jnp.zeros((3, fb_ref.shape[1]), f32)],
        axis=0,
    )
    for copy in copies[-3:]:
        copy.wait()


def near_kernel(
    edges, state_ref, ints_ref, ws_hbm, wr_hbm, wo_hbm, pack_ref,
    hot_ref, got_ref, into_ref, high_ref, low_ref, turn_ref, ws_ref, wr_ref, wo_ref, sems,
):
    rows, width = into_ref.shape
    parts = width // LANES
    pairs = ((ws_hbm, ws_ref), (wr_hbm, wr_ref), (wo_hbm, wo_ref))
    copies = [
        pltpu.make_async_copy(a.at[0], b, sems.at[j]) for j, (a, b) in enumerate(pairs)
    ]
    for copy in copies:
        copy.start()
    edge_hot(hot_ref, turn_ref, ints_ref[: edges // LANES, :], edges // rows, rows)
    normed = unit(load_rows(state_ref, rows, parts))
    for copy in copies:
        copy.wait()
    split_into(high_ref, low_ref, ws_ref[...], wo_ref[...])
    into_ref[...] = (times(normed, *halves(wr_ref[...])) + pack_ref[0:1, :]) * 0.5
    high, low = halves(times(normed, *weights(high_ref, low_ref, 0)) * 0.5)
    got_ref[...] = take(hot_ref[:, :rows], high, low)


def far_kernel(
    swap_ref, diag_ref, state_ref, hot_ref, got_ref, into_ref, high_ref, low_ref,
    out_full_ref, out_half_ref,
):
    rows, width = into_ref.shape
    parts = width // LANES
    rim = diag_ref.shape[0] // parts
    degree = hot_ref.shape[0] // rows
    far = jnp.concatenate(
        [load_rows(swap_ref, rim, parts), load_rows(diag_ref, rim, parts)], axis=0
    )
    high, low = halves(times(unit(far), *weights(high_ref, low_ref, 0)) * 0.5)
    total = None
    for k in range(degree):
        part = slice(k * rows, (k + 1) * rows)
        half = got_ref[part, :] + into_ref[...] + take(hot_ref[part, rows:], high, low)
        total = gate(half) if total is None else total + gate(half)
    store_rows(
        out_full_ref,
        load_rows(state_ref, rows, parts) + times(total, *weights(high_ref, low_ref, 1)),
        parts,
    )
    lines = out_half_ref.shape[0]
    start = pl.multiple_of(place() % 2 * (rows * parts - lines), LANES)
    out_half_ref[...] = out_full_ref[pl.ds(start, lines), :]


def near2_kernel(
    edges, count, state_ref, ints_ref, ints0_ref, hot_ref, ws_ref, wr_ref, wo_ref, wi_ref,
    wu_ref, pack_ref,
    got_ref, into_ref, own_high_ref, own_low_ref, hot2_ref, select_ref, high_ref, low_ref,
    turn_ref,
):
    rows, width = into_ref.shape
    parts = width // LANES
    senders = edges // LANES
    split_into(
        high_ref, low_ref, ws_ref[1], wr_ref[1], wo_ref[1], wi_ref[...], wu_ref[...]
    )
    normed = unit(load_rows(state_ref, rows, parts))
    into_ref[...] = (times(normed, *weights(high_ref, low_ref, 1)) + pack_ref[1:2, :]) * 0.5
    high, low = halves(times(normed, *weights(high_ref, low_ref, 0)) * 0.5)
    own_high_ref[...] = high
    own_low_ref[...] = low
    got_ref[...] = take(hot_ref[:, :rows], high, low)
    first = ints0_ref.shape[0] - ints_ref.shape[0]
    edge_hot(hot2_ref, turn_ref, ints0_ref[first : first + senders, :], edges // rows, rows)
    flip = place() * count
    line = senders
    for half, ref, base in ((0, ints_ref, 0), (1, ints0_ref, first)):
        for j in range(rows // LANES):
            parent = ref[base + line + j : base + line + j + 1, :].astype(jnp.int32)
            parent = jnp.bitwise_xor(parent, flip)
            ids = lax.broadcasted_iota(jnp.int32, (select_ref.shape[0], LANES), 0)
            ids = ids + jnp.bitwise_and(ids, -count)
            start = half * rows + j * LANES
            select_ref[:, start : start + LANES] = jnp.where(ids == parent, 1.0, 0.0).astype(
                bf16
            )


def up_kernel(
    swap_ref, pair_ref, diag_ref, state_ref, hot_ref, got_ref, into_ref, own_high_ref,
    own_low_ref, hot2_ref, select_ref, ints_ref, ints0_ref, high_ref, low_ref, pack_ref,
    last_ref, *refs,
):
    *slot_refs, th_ref, tl_ref = refs
    rows, width = into_ref.shape
    parts = width // LANES
    rim = diag_ref.shape[0] // parts
    degree = hot_ref.shape[0] // rows
    odd = place() % 2
    mine = pl.multiple_of((1 - odd) * (rows - rim), LANES)
    theirs = pl.multiple_of(odd * (rows - rim), LANES)
    other = load_rows(swap_ref, rows, parts)
    normed = unit(
        jnp.concatenate(
            [other, load_rows(pair_ref, rim, parts), load_rows(diag_ref, rim, parts)], axis=0
        )
    )
    sends = halves(times(normed, *weights(high_ref, low_ref, 0)) * 0.5)
    near = []
    for src, t_ref, own_ref in (
        (sends[0], th_ref, own_high_ref), (sends[1], tl_ref, own_low_ref),
    ):
        t_ref[:rows, :] = src[:rows, :]
        t_ref[rows : rows + rim, :] = own_ref[pl.ds(mine, rim), :]
        t_ref[rows + rim :, :] = src[rows : rows + rim, :]
        near.append(
            jnp.concatenate([t_ref[pl.ds(theirs, rim), :], src[rows + rim :, :]], axis=0)
        )
    into = (times(normed[:rows, :], *weights(high_ref, low_ref, 1)) + pack_ref[1:2, :]) * 0.5
    total, total2 = None, None
    for k in range(degree):
        part = slice(k * rows, (k + 1) * rows)
        half = got_ref[part, :] + into_ref[...] + take(hot_ref[part, rows:], *near)
        total = gate(half) if total is None else total + gate(half)
        half = into + take(hot2_ref[part, :], th_ref[...], tl_ref[...])
        total2 = gate(half) if total2 is None else total2 + gate(half)
    hidden = jnp.concatenate([load_rows(state_ref, rows, parts), other], axis=0) + times(
        jnp.concatenate([total, total2], axis=0), *weights(high_ref, low_ref, 2)
    )
    last_ref[...] = hidden[:rows, :]
    act = gate((times(unit(hidden), *weights(high_ref, low_ref, 3)) + pack_ref[2:3, :]) * 0.5)
    sums = take(select_ref[...], *halves(times(act, *weights(high_ref, low_ref, 4))))
    size = sums.shape[0] // len(slot_refs)
    first = hot_ref.shape[0] // LANES + rows // LANES
    base = ints0_ref.shape[0] - ints_ref.shape[0]
    anchor = (slot_refs[0].shape[0] - size * parts) // 4
    for j, slot in enumerate(slot_refs):
        store_rows(slot, sums[j * size : (j + 1) * size, :], parts)
        slot[size * parts :, :] = jnp.concatenate(
            [
                ints_ref[first : first + anchor, :],
                ints0_ref[base + first : base + first + anchor, :],
                jnp.zeros((2 * anchor, LANES), f32),
            ],
            axis=0,
        )


def middle_kernel(state_ref, *refs):
    out_ref = refs[-1]
    total = state_ref[...]
    for ref in refs[:-1]:
        total = total + ref[: out_ref.shape[0], :]
    out_ref[...] = total


def position(ids, flip, count, coarse):
    ids = jnp.bitwise_xor(ids.astype(jnp.int32), flip)
    slot = jnp.right_shift(ids, count.bit_length() - 1)
    return (
        jnp.bitwise_and(ids, count - 1)
        + jnp.right_shift(slot, 1) * count
        + jnp.bitwise_and(slot, 1) * (coarse // 2)
    )


def split_kernel(cs_ref, cr_ref, co_ref, di_ref, do_ref, high_ref, low_ref):
    split_into(
        high_ref, low_ref, cs_ref[...], cr_ref[...], co_ref[...], di_ref[...], do_ref[...]
    )


def edges_kernel(degree, count, ints_ref, *refs):
    *slot_refs, hot_ref, parent_ref, turn_ref = refs
    rows, coarse = parent_ref.shape
    flip = place() * count
    columns = turned(ints_ref[...])
    first = ints_ref.shape[0] // 2
    for j in range(rows // LANES):
        column = position(columns[:, first + j : first + j + 1], flip, count, coarse).astype(f32)
        parent_ref[j * LANES : (j + 1) * LANES, :] = equal(column, coarse)
    here = coarse * degree // LANES // len(slot_refs)
    line = here // 2
    lines = jnp.concatenate(
        [
            ref[ref.shape[0] - 2 * here + side * line : ref.shape[0] - 2 * here + (side + 1) * line, :]
            for side in range(2)
            for ref in slot_refs
        ],
        axis=0,
    )
    turn_ref[...] = turned(lines)
    step = LANES // degree
    lane = lax.broadcasted_iota(jnp.int32, (coarse, LANES), 1)
    table = jnp.zeros((coarse, LANES), f32)
    each = hot_ref.shape[0] // degree
    for k in range(degree):
        spread = position(turn_ref[pl.ds(k, step, stride=degree), :], flip, count, coarse)
        column = jnp.concatenate([spread[:, j : j + 1] for j in range(lines.shape[0])], axis=0)
        hot_ref[k * each : k * each + count, :] = equal(column[:count, :].astype(f32), coarse)
        high = jnp.right_shift(column, 8).astype(f32)
        low = jnp.bitwise_and(column, 255).astype(f32)
        table = jnp.where(lane == k, high, jnp.where(lane == degree + k, low, table))
    found = mm(parent_ref[...], table.astype(bf16))
    for k in range(degree):
        column = found[:, k : k + 1] * 256.0 + found[:, degree + k : degree + k + 1]
        hot_ref[k * each + count : (k + 1) * each, :] = equal(column, coarse)


def column_kernel(hot_ref, parent_ref, high_ref, low_ref, *refs):
    *blocks, got_ref, wanted_ref = refs
    _, width = wanted_ref.shape
    parts = width // LANES
    count = blocks[0].shape[0] // parts
    middle = jnp.concatenate([load_rows(b, count, parts) for b in blocks], axis=0)
    half = count * len(blocks)
    sends = halves(times(unit(middle), *weights(high_ref, low_ref, 0)) * 0.5)
    got_ref[...] = take(hot_ref[:, :half], *sends)
    wanted_ref[:count, :] = middle[:count, :]
    wanted_ref[count:, :] = take(parent_ref[:, :half], *halves(middle))


def coarse_kernel(
    last_ref, hot_ref, parent_ref, got_ref, wanted_ref, high_ref, low_ref, pack_ref, *refs
):
    *blocks, fine_hbm, coarse_hbm, fine_ref, coarse_ref, sems = refs
    rows, width = last_ref.shape
    parts = width // LANES
    count = coarse_ref.shape[0] // parts
    need = count + rows
    middle = jnp.concatenate([load_rows(b, count, parts) for b in blocks], axis=0)
    half = count * len(blocks)
    sends = halves(times(unit(middle), *weights(high_ref, low_ref, 0)) * 0.5)
    wanted = jnp.concatenate(
        [
            wanted_ref[:count, :],
            wanted_ref[count:, :] + take(parent_ref[:, half:], *halves(middle)),
        ],
        axis=0,
    )
    into = (times(unit(wanted), *weights(high_ref, low_ref, 1)) + pack_ref[3:4, :]) * 0.5
    total = None
    for k in range(hot_ref.shape[0] // need):
        part = slice(k * need, (k + 1) * need)
        term = gate(got_ref[part, :] + into + take(hot_ref[part, half:], *sends))
        total = term if total is None else total + term
    done = wanted + times(total, *weights(high_ref, low_ref, 2))
    store_rows(coarse_ref, done[:count, :], parts)
    copies = [pltpu.make_async_copy(coarse_ref, coarse_hbm, sems.at[0])]
    copies[0].start()
    act = gate(
        (times(unit(done[count:, :]), *weights(high_ref, low_ref, 3)) + pack_ref[4:5, :]) * 0.5
    )
    size = rows // 2
    for j in range(2):
        down = times(act[j * size : (j + 1) * size, :], *weights(high_ref, low_ref, 4))
        store_rows(fine_ref, last_ref[j * size : (j + 1) * size, :] + down, parts, j * size)
        piece = pl.ds(j * size * parts, size * parts)
        copies.append(
            pltpu.make_async_copy(fine_ref.at[piece, :], fine_hbm.at[piece, :], sems.at[j + 1])
        )
        copies[-1].start()
    for copy in copies:
        copy.wait()


VMEM = pl.BlockSpec(memory_space=pltpu.VMEM)
SMEM = pl.BlockSpec(memory_space=pltpu.SMEM)
HBM = pl.BlockSpec(memory_space=pltpu.HBM)


def call(kernel, in_specs, out_shapes, scratch=(), out_spec=VMEM):
    return pl.pallas_call(
        kernel,
        in_specs=in_specs,
        out_specs=[out_spec] * len(out_shapes),
        out_shape=out_shapes,
        scratch_shapes=scratch,
        compiler_params=pltpu.CompilerParams(vmem_limit_bytes=32 * 2**20),
    )


def move(values, pairs):
    return lax.ppermute(values, "sp", pairs)


def shape(*dims, kind=f32):
    return jax.ShapeDtypeStruct(dims, kind)


def kernel_shards(
    fine_state,
    coarse_state,
    fine_senders,
    up_owner,
    up_local,
    coarse_owner,
    coarse_local,
    fine_w_send,
    fine_w_recv,
    fine_bias,
    fine_w_out,
    up_w_in,
    up_bias,
    up_w_out,
    coarse_w_send,
    coarse_w_recv,
    coarse_bias,
    coarse_w_out,
    down_w_in,
    down_bias,
    down_w_out,
):
    peers = lax.axis_size("sp")
    me = lax.axis_index("sp").astype(jnp.int32)
    rows, _, width = fine_state.shape
    count = coarse_state.shape[0]
    parts = width // LANES
    edges = fine_senders.shape[0]
    coarse_edges = coarse_owner.shape[0]
    coarse = peers * count
    window = rows + 2 * HALO
    rim, own, full = HALO * parts, count * parts, rows * parts
    size = width
    swap = [(i, i ^ 1) for i in range(peers)]
    diag = [(i, (i + 1 if i % 2 else i - 1) % peers) for i in range(peers)]
    pair = [(i, (i + 2 if i % 2 else i - 2) % peers) for i in range(peers)]
    flips = [[(i, i ^ (2 * j)) for i in range(peers)] for j in range(peers // 2)]
    lines = lambda x: x.reshape(-1, LANES)
    row = lambda x: x.reshape(1, width)
    turn = pltpu.VMEM((LANES, LANES), f32)
    here = lambda *xs: [pltpu.with_memory_space_constraint(x, pltpu.HBM) for x in xs]
    hot_shape = shape(edges, window, kind=bf16)
    small = lambda ref: pltpu.VMEM(ref.shape, ref.dtype)

    small_args = [
        lines(fine_senders), lines(up_owner), lines(up_local), lines(coarse_owner),
        lines(coarse_local), fine_bias, row(up_bias), row(coarse_bias), row(down_bias),
    ]
    state, ints, pack, out_swap, out_diag = call(
        functools.partial(start_kernel, count, HALO),
        [HBM] * 10,
        [
            shape(full, LANES), shape(16, LANES), shape(8, width), shape(rim + 16, LANES),
            shape(rim, LANES),
        ],
        [small(x) for x in small_args] + [pltpu.SemaphoreType.DMA((12,))],
    )(*here(lines(fine_state), *small_args))
    swap0 = move(out_swap, swap)
    diag0 = move(out_diag, diag)
    hot, got, into, high, low = call(
        functools.partial(near_kernel, edges),
        [VMEM] * 2 + [HBM] * 3 + [VMEM],
        [hot_shape, shape(edges, width), shape(rows, width)]
        + [shape(2 * size, width, kind=bf16)] * 2,
        [turn] + [pltpu.VMEM((size, width), f32)] * 3 + [pltpu.SemaphoreType.DMA((3,))],
    )(state, ints, *here(fine_w_send, fine_w_recv, fine_w_out), pack)
    state, out_half = call(
        far_kernel, [VMEM] * 8, [shape(full, LANES), shape(rim, LANES)]
    )(swap0, diag0, state, hot, got, into, high, low)
    swap1 = move(state, swap)
    diag1 = move(out_half, diag)
    pair1 = move(out_half, pair)
    got, into, own_high, own_low, hot2, select, high, low = call(
        functools.partial(near2_kernel, edges, count),
        [VMEM] * 10,
        [shape(edges, width), shape(rows, width)]
        + [shape(rows, width, kind=bf16)] * 2
        + [hot_shape, shape(coarse // 2, 2 * rows, kind=bf16)]
        + [shape(5 * size, width, kind=bf16)] * 2,
        [turn],
    )(
        state, ints, swap0, hot, fine_w_send, fine_w_recv, fine_w_out, up_w_in, up_w_out,
        pack,
    )
    hidden, *slots = call(
        up_kernel,
        [VMEM] * 16,
        [shape(rows, width)]
        + [shape(own + 8 * coarse_edges // 256, LANES)] * (peers // 2),
        [pltpu.VMEM((window, width), bf16)] * 2,
    )(
        swap1, pair1, diag1, state, hot, got, into, own_high, own_low, hot2, select, ints, swap0,
        high, low, pack,
    )
    arrived = [slots[0]] + [move(slots[j], flips[j]) for j in range(1, peers // 2)]
    (middle,) = call(
        middle_kernel, [VMEM] * (1 + peers // 2), [shape(own, LANES)]
    )(lines(coarse_state), *arrived)
    columns = [middle] + [move(middle, flips[j]) for j in range(1, peers // 2)]
    across = [move(block, swap) for block in columns]
    degree = coarse_edges // count
    coarse_hot, parent_hot = call(
        functools.partial(edges_kernel, degree, count),
        [VMEM] * (1 + peers // 2),
        [
            shape(degree * (count + rows), coarse, kind=bf16),
            shape(rows, coarse, kind=bf16),
        ],
        [turn],
    )(ints, *arrived)
    high, low = call(
        split_kernel, [VMEM] * 5, [shape(5 * size, width, kind=bf16)] * 2
    )(coarse_w_send, coarse_w_recv, coarse_w_out, down_w_in, down_w_out)
    got, wanted = call(
        column_kernel,
        [VMEM] * (4 + peers // 2),
        [shape(degree * (count + rows), width), shape(count + rows, width)],
    )(coarse_hot, parent_hot, high, low, *columns)
    fine_out, coarse_out = call(
        coarse_kernel,
        [VMEM] * (8 + peers // 2),
        [shape(full, LANES), shape(own, LANES)],
        [
            pltpu.VMEM((full, LANES), f32), pltpu.VMEM((own, LANES), f32),
            pltpu.SemaphoreType.DMA((3,)),
        ],
        HBM,
    )(hidden, coarse_hot, parent_hot, got, wanted, high, low, pack, *across)
    return (fine_out.reshape(fine_state.shape), coarse_out.reshape(coarse_state.shape))


def shards(*args):
    fine_state, coarse_state, fine_senders = args[0], args[1], args[2]
    coarse_owner, layers = args[5], args[7].shape[0]
    peers = lax.axis_size("sp")
    rows, samples, width = fine_state.shape
    count = coarse_state.shape[0]
    fits = (
        samples == 1
        and layers == 2
        and width % LANES == 0
        and peers % 2 == 0
        and peers & (peers - 1) == 0
        and rows % LANES == 0
        and rows >= HALO
        and count & (count - 1) == 0
        and LANES % count == 0
        and coarse_owner.shape[0] % LANES == 0
        and coarse_owner.shape[0] == 4 * count
        and fine_senders.shape[0] == 8 * LANES
        and rows == 2 * LANES
        and coarse_owner.shape[0] == 2 * LANES
        and width == args[7].shape[2]
        and peers * count <= 1024
        and peers >= 4
        and rows >= 2 * HALO
    )
    if not fits:
        return general_shards(*args)
    return kernel_shards(*args)


def solution(mesh):
    in_specs = (
        P("sp", ("grp", "ch"), None),
        P("sp", ("grp", "ch"), None),
        P("sp"),
        P("sp", None),
        P("sp"),
        P("sp", None),
        P("sp"),
    ) + (P(),) * 14
    out_specs = (P("sp", ("grp", "ch"), None), P("sp", ("grp", "ch"), None))
    return jax.shard_map(shards, mesh=mesh, in_specs=in_specs, out_specs=out_specs, check_vma=False)
```

```python
import functools
import jax
import jax.numpy as jnp
from jax import lax
from jax.experimental import pallas as pl
from jax.experimental.pallas import tpu as pltpu
from jax.sharding import PartitionSpec as P

HALO = 128
LANES = 128


epsilon = 1e-05
highest = lax.Precision.HIGHEST


def extended_2(cells, sides, width):
    for axis, dim in sides:
        count = lax.axis_size(axis)
        head = lax.slice_in_dim(cells, 0, width, axis=dim)
        tail = lax.slice_in_dim(cells, cells.shape[dim] - width, cells.shape[dim], axis=dim)
        cells = jnp.concatenate(
            [
                lax.ppermute(tail, axis, [(i, (i + 1) % count) for i in range(count)]),
                cells,
                lax.ppermute(head, axis, [((i + 1) % count, i) for i in range(count)]),
            ],
            axis=dim,
        )
    return cells


def layer_norm(values):
    average = jnp.mean(values, axis=-1, keepdims=True)
    centered = values - average
    spread = jnp.mean(centered * centered, axis=-1, keepdims=True)
    return centered / jnp.sqrt(spread + epsilon)


def project(values, matrix):
    return jnp.einsum(
        "nsd,dh->nsh", values, matrix, precision=highest, preferred_element_type=jnp.float32
    )


def slot_ranks(owners, peer_count):
    matches = (owners[:, None] == jnp.arange(peer_count, dtype=jnp.int32)[None, :]).astype(
        jnp.int32
    )
    ranking = jnp.cumsum(matches, axis=0) - 1
    return jnp.sum(ranking * matches, axis=1)


def general_shards(
    fine_state,
    coarse_state,
    fine_senders,
    up_owner,
    up_local,
    coarse_owner,
    coarse_local,
    fine_w_send,
    fine_w_recv,
    fine_bias,
    fine_w_out,
    up_w_in,
    up_bias,
    up_w_out,
    coarse_w_send,
    coarse_w_recv,
    coarse_bias,
    coarse_w_out,
    down_w_in,
    down_bias,
    down_w_out,
):
    peer_count = lax.axis_size("sp")
    fine_rows = fine_state.shape[0]
    coarse_rows = coarse_state.shape[0]
    samples = fine_state.shape[1]
    feature_width = fine_state.shape[2]
    degree_fine = fine_senders.shape[0] // fine_rows
    degree_coarse = coarse_owner.shape[0] // coarse_rows
    hidden_state = fine_state
    for layer_index in range(fine_w_send.shape[0]):
        normed = layer_norm(hidden_state)
        outward = project(normed, fine_w_send[layer_index])
        inward = project(normed, fine_w_recv[layer_index]) + fine_bias[layer_index]
        extended = extended_2(outward, (("sp", 0),), HALO)
        gathered = extended[fine_senders].reshape(fine_rows, degree_fine, samples, -1)
        summed = jnp.sum(jax.nn.silu(gathered + inward[:, None]), axis=1)
        hidden_state = hidden_state + project(summed, fine_w_out[layer_index])
    capacity = max(4, 2 * fine_rows // peer_count)
    owners = up_owner[:, 0]
    places = owners * capacity + slot_ranks(owners, peer_count)
    targets = (
        jnp.full((peer_count * capacity,), -1.0, jnp.float32)
        .at[places]
        .set(up_local.astype(jnp.float32))
        .reshape(peer_count, capacity)
    )
    activated = jax.nn.silu(project(layer_norm(hidden_state), up_w_in) + up_bias)
    coarse_ids = jnp.arange(coarse_rows, dtype=jnp.float32)[:, None]
    messages = project(activated, up_w_out)
    outgoing = (
        jnp.zeros((peer_count * capacity, samples, feature_width), jnp.float32)
        .at[places]
        .set(messages)
        .reshape(peer_count, capacity, samples, feature_width)
    )
    arrived, sources = (
        lax.all_to_all(outgoing, "sp", split_axis=0, concat_axis=0, tiled=True),
        lax.all_to_all(targets, "sp", split_axis=0, concat_axis=0, tiled=True),
    )
    selector = (sources.reshape(1, -1) == coarse_ids).astype(jnp.float32)
    gained = jnp.einsum(
        "cr,rsd->csd",
        selector,
        arrived.reshape(peer_count * capacity, samples, feature_width),
        precision=highest,
        preferred_element_type=jnp.float32,
    )
    coarse = coarse_state + gained
    normed = layer_norm(coarse)
    outward = project(normed, coarse_w_send)
    inward = project(normed, coarse_w_recv) + coarse_bias
    anchor_owner = coarse_owner[:, 0]
    everything = lax.all_gather(outward, "sp", axis=0, tiled=True)
    picked = everything[anchor_owner * coarse_rows + coarse_local]
    edge_terms = picked.reshape(coarse_rows, degree_coarse, samples, -1)
    summed = jnp.sum(jax.nn.silu(edge_terms + inward[:, None]), axis=1)
    coarse_out = coarse + project(summed, coarse_w_out)
    downward = project(
        jax.nn.silu(project(layer_norm(coarse_out), down_w_in) + down_bias), down_w_out
    )
    wanted = jnp.maximum(sources.reshape(-1), 0.0).astype(jnp.int32)
    replies = downward[wanted].reshape(peer_count, capacity, samples, feature_width)
    answered = lax.all_to_all(replies, "sp", split_axis=0, concat_axis=0, tiled=True)
    fine_out = (
        hidden_state + answered.reshape(peer_count * capacity, samples, feature_width)[places]
    )
    return (fine_out, coarse_out)


f32 = jnp.float32
bf16 = jnp.bfloat16


def load_rows(ref, rows, parts, start=0):
    return jnp.concatenate(
        [ref[pl.ds(start * parts + j, rows, stride=parts), :] for j in range(parts)], axis=1
    )


def store_rows(ref, values, parts, start=0):
    for j in range(parts):
        ref[pl.ds(start * parts + j, values.shape[0], stride=parts), :] = values[
            :, j * LANES : (j + 1) * LANES
        ]


def halves(values):
    high = values.astype(bf16)
    return high, (values - high.astype(f32)).astype(bf16)


def mm(a, b):
    return jnp.dot(a, b, preferred_element_type=f32)


def times(values, high, low, pieces=1):
    size = values.shape[0] // pieces
    done = []
    for j in range(pieces):
        vh, vl = halves(values[j * size : (j + 1) * size, :])
        done.append(mm(vh, high) + (mm(vl, high) + mm(vh, low)))
    return jnp.concatenate(done, axis=0)


def take(one_hot, high, low):
    return mm(one_hot, high) + mm(one_hot, low)


def place():
    return lax.axis_index("sp").astype(jnp.int32)


def unit(values):
    width = values.shape[1]
    average = jnp.sum(values, axis=1, keepdims=True) * (1.0 / width)
    centered = values - average
    spread = jnp.sum(centered * centered, axis=1, keepdims=True) * (1.0 / width)
    return centered * lax.rsqrt(spread + epsilon)


def gate(half):
    return half + half * jnp.tanh(half)


def equal(column, count):
    ids = lax.broadcasted_iota(jnp.int32, (column.shape[0], count), 1).astype(f32)
    return jnp.where(ids == column, 1.0, 0.0).astype(bf16)


def turned(lines):
    pad = jnp.zeros((LANES - lines.shape[0], LANES), f32)
    return jnp.transpose(jnp.concatenate([lines, pad], axis=0))


def edge_hot(hot_ref, turn_ref, lines, degree, nodes, flip=None):
    turn_ref[...] = turned(lines)
    step = LANES // degree
    for k in range(degree):
        spread = turn_ref[pl.ds(k, step, stride=degree), :]
        if flip is not None:
            spread = jnp.bitwise_xor(spread.astype(jnp.int32), flip).astype(f32)
        for line in range(lines.shape[0]):
            start = k * nodes + line * step
            hot_ref[start : start + step, :] = equal(
                spread[:, line : line + 1], hot_ref.shape[1]
            )


def split_into(high_ref, low_ref, *matrices):
    for j, matrix in enumerate(matrices):
        size = matrix.shape[0]
        high_ref[j * size : (j + 1) * size, :], low_ref[j * size : (j + 1) * size, :] = halves(
            matrix
        )


def weights(high_ref, low_ref, j):
    size = high_ref.shape[1]
    return high_ref[j * size : (j + 1) * size, :], low_ref[j * size : (j + 1) * size, :]


def start_kernel(
    count, halo, state_hbm, sender_hbm, owner_hbm, local_hbm, cowner_hbm,
    clocal_hbm, fb_hbm, ub_hbm, cb_hbm, db_hbm,
    state_ref, ints_ref, pack_ref, swap_ref, diag_ref,
    sender_ref, owner_ref, local_ref, cowner_ref, clocal_ref, fb_ref, ub_ref, cb_ref, db_ref,
    sems,
):
    odd = place() % 2
    rim = diag_ref.shape[0]
    far = state_hbm.shape[0] - rim
    mine = pl.ds(pl.multiple_of((1 - odd) * far, LANES), rim)
    away = pl.ds(pl.multiple_of(odd * far, LANES), rim)
    pairs = [
        (sender_hbm, sender_ref),
        (owner_hbm, owner_ref),
        (local_hbm, local_ref),
        (cowner_hbm, cowner_ref),
        (clocal_hbm, clocal_ref),
        (fb_hbm, fb_ref),
        (ub_hbm, ub_ref),
        (cb_hbm, cb_ref),
        (db_hbm, db_ref),
        (state_hbm.at[mine, :], swap_ref.at[0:rim, :]),
        (state_hbm.at[away, :], diag_ref),
        (state_hbm, state_ref),
    ]
    copies = [pltpu.make_async_copy(a, b, sems.at[j]) for j, (a, b) in enumerate(pairs)]
    for copy in copies:
        copy.start()
    for copy in copies[:-3]:
        copy.wait()
    rows = state_hbm.shape[0] * LANES // fb_ref.shape[1]
    sender = sender_ref[...]
    before = rows + (1 - odd) * halo
    after = rows + odd * halo
    index = jnp.where(
        sender < halo,
        sender + before,
        jnp.where(sender < halo + rows, sender - halo, sender - (halo + rows) + after),
    )
    lines = [
        index.astype(f32),
        (owner_ref[...] * count + local_ref[...]).astype(f32),
        (cowner_ref[...] * count + clocal_ref[...]).astype(f32),
    ]
    rest = ints_ref.shape[0] - sum(x.shape[0] for x in lines)
    ints = jnp.concatenate(lines + [jnp.zeros((rest, LANES), f32)], axis=0)
    ints_ref[...] = ints
    swap_ref[rim:, :] = ints
    pack_ref[...] = jnp.concatenate(
        [fb_ref[...], ub_ref[...], cb_ref[...], db_ref[...]]
        + [jnp.zeros((3, fb_ref.shape[1]), f32)],
        axis=0,
    )
    for copy in copies[-3:]:
        copy.wait()


def near_kernel(
    edges, state_ref, ints_ref, ws_hbm, wr_hbm, wo_hbm, pack_ref,
    hot_ref, got_ref, into_ref, high_ref, low_ref, turn_ref, ws_ref, wr_ref, wo_ref, sems,
):
    rows, width = into_ref.shape
    parts = width // LANES
    pairs = ((ws_hbm, ws_ref), (wr_hbm, wr_ref), (wo_hbm, wo_ref))
    copies = [
        pltpu.make_async_copy(a.at[0], b, sems.at[j]) for j, (a, b) in enumerate(pairs)
    ]
    for copy in copies:
        copy.start()
    edge_hot(hot_ref, turn_ref, ints_ref[: edges // LANES, :], edges // rows, rows)
    normed = unit(load_rows(state_ref, rows, parts))
    for copy in copies:
        copy.wait()
    split_into(high_ref, low_ref, ws_ref[...], wo_ref[...])
    into_ref[...] = (times(normed, *halves(wr_ref[...])) + pack_ref[0:1, :]) * 0.5
    high, low = halves(times(normed, *weights(high_ref, low_ref, 0)) * 0.5)
    got_ref[...] = take(hot_ref[:, :rows], high, low)


def far_kernel(
    swap_ref, diag_ref, state_ref, hot_ref, got_ref, into_ref, high_ref, low_ref,
    out_full_ref, out_half_ref,
):
    rows, width = into_ref.shape
    parts = width // LANES
    rim = diag_ref.shape[0] // parts
    degree = hot_ref.shape[0] // rows
    far = jnp.concatenate(
        [load_rows(swap_ref, rim, parts), load_rows(diag_ref, rim, parts)], axis=0
    )
    high, low = halves(times(unit(far), *weights(high_ref, low_ref, 0), 2) * 0.5)
    total = None
    for k in range(degree):
        part = slice(k * rows, (k + 1) * rows)
        half = got_ref[part, :] + into_ref[...] + take(hot_ref[part, rows:], high, low)
        total = gate(half) if total is None else total + gate(half)
    store_rows(
        out_full_ref,
        load_rows(state_ref, rows, parts) + times(total, *weights(high_ref, low_ref, 1), 2),
        parts,
    )
    lines = out_half_ref.shape[0]
    start = pl.multiple_of(place() % 2 * (rows * parts - lines), LANES)
    out_half_ref[...] = out_full_ref[pl.ds(start, lines), :]


def near2_kernel(
    edges, count, state_ref, ints_ref, ints0_ref, hot_ref, ws_ref, wr_ref, wo_ref, wi_ref,
    wu_ref, pack_ref,
    got_ref, into_ref, own_high_ref, own_low_ref, hot2_ref, select_ref, high_ref, low_ref,
    turn_ref,
):
    rows, width = into_ref.shape
    parts = width // LANES
    senders = edges // LANES
    split_into(
        high_ref, low_ref, ws_ref[1], wr_ref[1], wo_ref[1], wi_ref[...], wu_ref[...]
    )
    normed = unit(load_rows(state_ref, rows, parts))
    into_ref[...] = (times(normed, *weights(high_ref, low_ref, 1)) + pack_ref[1:2, :]) * 0.5
    high, low = halves(times(normed, *weights(high_ref, low_ref, 0)) * 0.5)
    own_high_ref[...] = high
    own_low_ref[...] = low
    got_ref[...] = take(hot_ref[:, :rows], high, low)
    first = ints0_ref.shape[0] - ints_ref.shape[0]
    edge_hot(hot2_ref, turn_ref, ints0_ref[first : first + senders, :], edges // rows, rows)
    flip = place() * count
    line = senders
    for half, ref, base in ((0, ints_ref, 0), (1, ints0_ref, first)):
        for j in range(rows // LANES):
            parent = ref[base + line + j : base + line + j + 1, :].astype(jnp.int32)
            parent = jnp.bitwise_xor(parent, flip)
            ids = lax.broadcasted_iota(jnp.int32, (select_ref.shape[0], LANES), 0)
            ids = ids + jnp.bitwise_and(ids, -count)
            start = half * rows + j * LANES
            select_ref[:, start : start + LANES] = jnp.where(ids == parent, 1.0, 0.0).astype(
                bf16
            )


def up_kernel(
    swap_ref, pair_ref, diag_ref, state_ref, hot_ref, got_ref, into_ref, own_high_ref,
    own_low_ref, hot2_ref, select_ref, ints_ref, ints0_ref, high_ref, low_ref, pack_ref,
    last_ref, *refs,
):
    *slot_refs, th_ref, tl_ref = refs
    rows, width = into_ref.shape
    parts = width // LANES
    rim = diag_ref.shape[0] // parts
    degree = hot_ref.shape[0] // rows
    odd = place() % 2
    mine = pl.multiple_of((1 - odd) * (rows - rim), LANES)
    theirs = pl.multiple_of(odd * (rows - rim), LANES)
    other = load_rows(swap_ref, rows, parts)
    normed = unit(
        jnp.concatenate(
            [other, load_rows(pair_ref, rim, parts), load_rows(diag_ref, rim, parts)], axis=0
        )
    )
    sends = halves(times(normed, *weights(high_ref, low_ref, 0), 2) * 0.5)
    near = []
    for src, t_ref, own_ref in (
        (sends[0], th_ref, own_high_ref), (sends[1], tl_ref, own_low_ref),
    ):
        t_ref[:rows, :] = src[:rows, :]
        t_ref[rows : rows + rim, :] = own_ref[pl.ds(mine, rim), :]
        t_ref[rows + rim :, :] = src[rows : rows + rim, :]
        near.append(
            jnp.concatenate([t_ref[pl.ds(theirs, rim), :], src[rows + rim :, :]], axis=0)
        )
    into = (times(normed[:rows, :], *weights(high_ref, low_ref, 1)) + pack_ref[1:2, :]) * 0.5
    total, total2 = None, None
    for k in range(degree):
        part = slice(k * rows, (k + 1) * rows)
        half = got_ref[part, :] + into_ref[...] + take(hot_ref[part, rows:], *near)
        total = gate(half) if total is None else total + gate(half)
        half = into + take(hot2_ref[part, :], th_ref[...], tl_ref[...])
        total2 = gate(half) if total2 is None else total2 + gate(half)
    hidden = jnp.concatenate([load_rows(state_ref, rows, parts), other], axis=0) + times(
        jnp.concatenate([total, total2], axis=0), *weights(high_ref, low_ref, 2), 2
    )
    last_ref[...] = hidden[:rows, :]
    act = gate((times(unit(hidden), *weights(high_ref, low_ref, 3), 2) + pack_ref[2:3, :]) * 0.5)
    sums = take(select_ref[...], *halves(times(act, *weights(high_ref, low_ref, 4), 2)))
    size = sums.shape[0] // len(slot_refs)
    first = hot_ref.shape[0] // LANES + rows // LANES
    base = ints0_ref.shape[0] - ints_ref.shape[0]
    anchor = (slot_refs[0].shape[0] - size * parts) // 4
    for j, slot in enumerate(slot_refs):
        store_rows(slot, sums[j * size : (j + 1) * size, :], parts)
        slot[size * parts :, :] = jnp.concatenate(
            [
                ints_ref[first : first + anchor, :],
                ints0_ref[base + first : base + first + anchor, :],
                jnp.zeros((2 * anchor, LANES), f32),
            ],
            axis=0,
        )


def middle_kernel(state_ref, *refs):
    out_ref = refs[-1]
    total = state_ref[...]
    for ref in refs[:-1]:
        total = total + ref[: out_ref.shape[0], :]
    out_ref[...] = total


def position(ids, flip, count, coarse):
    ids = jnp.bitwise_xor(ids.astype(jnp.int32), flip)
    slot = jnp.right_shift(ids, count.bit_length() - 1)
    return (
        jnp.bitwise_and(ids, count - 1)
        + jnp.right_shift(slot, 1) * count
        + jnp.bitwise_and(slot, 1) * (coarse // 2)
    )


def split_kernel(cs_ref, cr_ref, co_ref, di_ref, do_ref, high_ref, low_ref):
    split_into(
        high_ref, low_ref, cs_ref[...], cr_ref[...], co_ref[...], di_ref[...], do_ref[...]
    )


def edges_kernel(degree, count, ints_ref, *refs):
    *slot_refs, hot_ref, parent_ref, turn_ref = refs
    rows, coarse = parent_ref.shape
    flip = place() * count
    columns = turned(ints_ref[...])
    first = ints_ref.shape[0] // 2
    for j in range(rows // LANES):
        column = position(columns[:, first + j : first + j + 1], flip, count, coarse).astype(f32)
        parent_ref[j * LANES : (j + 1) * LANES, :] = equal(column, coarse)
    here = coarse * degree // LANES // len(slot_refs)
    line = here // 2
    lines = jnp.concatenate(
        [
            ref[ref.shape[0] - 2 * here + side * line : ref.shape[0] - 2 * here + (side + 1) * line, :]
            for side in range(2)
            for ref in slot_refs
        ],
        axis=0,
    )
    turn_ref[...] = turned(lines)
    step = LANES // degree
    lane = lax.broadcasted_iota(jnp.int32, (coarse, LANES), 1)
    table = jnp.zeros((coarse, LANES), f32)
    each = hot_ref.shape[0] // degree
    for k in range(degree):
        spread = position(turn_ref[pl.ds(k, step, stride=degree), :], flip, count, coarse)
        column = jnp.concatenate([spread[:, j : j + 1] for j in range(lines.shape[0])], axis=0)
        hot_ref[k * each : k * each + count, :] = equal(column[:count, :].astype(f32), coarse)
        high = jnp.right_shift(column, 8).astype(f32)
        low = jnp.bitwise_and(column, 255).astype(f32)
        table = jnp.where(lane == k, high, jnp.where(lane == degree + k, low, table))
    found = mm(parent_ref[...], table.astype(bf16))
    for k in range(degree):
        column = found[:, k : k + 1] * 256.0 + found[:, degree + k : degree + k + 1]
        hot_ref[k * each + count : (k + 1) * each, :] = equal(column, coarse)


def column_kernel(hot_ref, parent_ref, high_ref, low_ref, *refs):
    *blocks, got_ref, wanted_ref = refs
    _, width = wanted_ref.shape
    parts = width // LANES
    count = blocks[0].shape[0] // parts
    middle = jnp.concatenate([load_rows(b, count, parts) for b in blocks], axis=0)
    half = count * len(blocks)
    sends = halves(times(unit(middle), *weights(high_ref, low_ref, 0)) * 0.5)
    got_ref[...] = take(hot_ref[:, :half], *sends)
    wanted_ref[:count, :] = middle[:count, :]
    wanted_ref[count:, :] = take(parent_ref[:, :half], *halves(middle))


def coarse_kernel(
    last_ref, hot_ref, parent_ref, got_ref, wanted_ref, high_ref, low_ref, pack_ref, *refs
):
    *blocks, fine_hbm, coarse_hbm, fine_ref, coarse_ref, sems = refs
    rows, width = last_ref.shape
    parts = width // LANES
    count = coarse_ref.shape[0] // parts
    need = count + rows
    middle = jnp.concatenate([load_rows(b, count, parts) for b in blocks], axis=0)
    half = count * len(blocks)
    sends = halves(times(unit(middle), *weights(high_ref, low_ref, 0)) * 0.5)
    wanted = jnp.concatenate(
        [
            wanted_ref[:count, :],
            wanted_ref[count:, :] + take(parent_ref[:, half:], *halves(middle)),
        ],
        axis=0,
    )
    into = (times(unit(wanted), *weights(high_ref, low_ref, 1)) + pack_ref[3:4, :]) * 0.5
    total = None
    for k in range(hot_ref.shape[0] // need):
        part = slice(k * need, (k + 1) * need)
        term = gate(got_ref[part, :] + into + take(hot_ref[part, half:], *sends))
        total = term if total is None else total + term
    done = wanted + times(total, *weights(high_ref, low_ref, 2))
    store_rows(coarse_ref, done[:count, :], parts)
    copies = [pltpu.make_async_copy(coarse_ref, coarse_hbm, sems.at[0])]
    copies[0].start()
    act = gate(
        (times(unit(done[count:, :]), *weights(high_ref, low_ref, 3)) + pack_ref[4:5, :]) * 0.5
    )
    size = rows // 2
    for j in range(2):
        down = times(act[j * size : (j + 1) * size, :], *weights(high_ref, low_ref, 4))
        store_rows(fine_ref, last_ref[j * size : (j + 1) * size, :] + down, parts, j * size)
        piece = pl.ds(j * size * parts, size * parts)
        copies.append(
            pltpu.make_async_copy(fine_ref.at[piece, :], fine_hbm.at[piece, :], sems.at[j + 1])
        )
        copies[-1].start()
    for copy in copies:
        copy.wait()


VMEM = pl.BlockSpec(memory_space=pltpu.VMEM)
SMEM = pl.BlockSpec(memory_space=pltpu.SMEM)
HBM = pl.BlockSpec(memory_space=pltpu.HBM)


def call(kernel, in_specs, out_shapes, scratch=(), out_spec=VMEM):
    return pl.pallas_call(
        kernel,
        in_specs=in_specs,
        out_specs=[out_spec] * len(out_shapes),
        out_shape=out_shapes,
        scratch_shapes=scratch,
        compiler_params=pltpu.CompilerParams(vmem_limit_bytes=32 * 2**20),
    )


def move(values, pairs):
    return lax.ppermute(values, "sp", pairs)


def shape(*dims, kind=f32):
    return jax.ShapeDtypeStruct(dims, kind)


def kernel_shards(
    fine_state,
    coarse_state,
    fine_senders,
    up_owner,
    up_local,
    coarse_owner,
    coarse_local,
    fine_w_send,
    fine_w_recv,
    fine_bias,
    fine_w_out,
    up_w_in,
    up_bias,
    up_w_out,
    coarse_w_send,
    coarse_w_recv,
    coarse_bias,
    coarse_w_out,
    down_w_in,
    down_bias,
    down_w_out,
):
    peers = lax.axis_size("sp")
    me = lax.axis_index("sp").astype(jnp.int32)
    rows, _, width = fine_state.shape
    count = coarse_state.shape[0]
    parts = width // LANES
    edges = fine_senders.shape[0]
    coarse_edges = coarse_owner.shape[0]
    coarse = peers * count
    window = rows + 2 * HALO
    rim, own, full = HALO * parts, count * parts, rows * parts
    size = width
    swap = [(i, i ^ 1) for i in range(peers)]
    diag = [(i, (i + 1 if i % 2 else i - 1) % peers) for i in range(peers)]
    pair = [(i, (i + 2 if i % 2 else i - 2) % peers) for i in range(peers)]
    flips = [[(i, i ^ (2 * j)) for i in range(peers)] for j in range(peers // 2)]
    lines = lambda x: x.reshape(-1, LANES)
    row = lambda x: x.reshape(1, width)
    turn = pltpu.VMEM((LANES, LANES), f32)
    here = lambda *xs: [pltpu.with_memory_space_constraint(x, pltpu.HBM) for x in xs]
    hot_shape = shape(edges, window, kind=bf16)
    small = lambda ref: pltpu.VMEM(ref.shape, ref.dtype)

    small_args = [
        lines(fine_senders), lines(up_owner), lines(up_local), lines(coarse_owner),
        lines(coarse_local), fine_bias, row(up_bias), row(coarse_bias), row(down_bias),
    ]
    state, ints, pack, out_swap, out_diag = call(
        functools.partial(start_kernel, count, HALO),
        [HBM] * 10,
        [
            shape(full, LANES), shape(16, LANES), shape(8, width), shape(rim + 16, LANES),
            shape(rim, LANES),
        ],
        [small(x) for x in small_args] + [pltpu.SemaphoreType.DMA((12,))],
    )(*here(lines(fine_state), *small_args))
    swap0 = move(out_swap, swap)
    diag0 = move(out_diag, diag)
    hot, got, into, high, low = call(
        functools.partial(near_kernel, edges),
        [VMEM] * 2 + [HBM] * 3 + [VMEM],
        [hot_shape, shape(edges, width), shape(rows, width)]
        + [shape(2 * size, width, kind=bf16)] * 2,
        [turn] + [pltpu.VMEM((size, width), f32)] * 3 + [pltpu.SemaphoreType.DMA((3,))],
    )(state, ints, *here(fine_w_send, fine_w_recv, fine_w_out), pack)
    state, out_half = call(
        far_kernel, [VMEM] * 8, [shape(full, LANES), shape(rim, LANES)]
    )(swap0, diag0, state, hot, got, into, high, low)
    swap1 = move(state, swap)
    diag1 = move(out_half, diag)
    pair1 = move(out_half, pair)
    got, into, own_high, own_low, hot2, select, high, low = call(
        functools.partial(near2_kernel, edges, count),
        [VMEM] * 10,
        [shape(edges, width), shape(rows, width)]
        + [shape(rows, width, kind=bf16)] * 2
        + [hot_shape, shape(coarse // 2, 2 * rows, kind=bf16)]
        + [shape(5 * size, width, kind=bf16)] * 2,
        [turn],
    )(
        state, ints, swap0, hot, fine_w_send, fine_w_recv, fine_w_out, up_w_in, up_w_out,
        pack,
    )
    hidden, *slots = call(
        up_kernel,
        [VMEM] * 16,
        [shape(rows, width)]
        + [shape(own + 8 * coarse_edges // 256, LANES)] * (peers // 2),
        [pltpu.VMEM((window, width), bf16)] * 2,
    )(
        swap1, pair1, diag1, state, hot, got, into, own_high, own_low, hot2, select, ints, swap0,
        high, low, pack,
    )
    arrived = [slots[0]] + [move(slots[j], flips[j]) for j in range(1, peers // 2)]
    (middle,) = call(
        middle_kernel, [VMEM] * (1 + peers // 2), [shape(own, LANES)]
    )(lines(coarse_state), *arrived)
    columns = [middle] + [move(middle, flips[j]) for j in range(1, peers // 2)]
    across = [move(block, swap) for block in columns]
    degree = coarse_edges // count
    coarse_hot, parent_hot = call(
        functools.partial(edges_kernel, degree, count),
        [VMEM] * (1 + peers // 2),
        [
            shape(degree * (count + rows), coarse, kind=bf16),
            shape(rows, coarse, kind=bf16),
        ],
        [turn],
    )(ints, *arrived)
    high, low = call(
        split_kernel, [VMEM] * 5, [shape(5 * size, width, kind=bf16)] * 2
    )(coarse_w_send, coarse_w_recv, coarse_w_out, down_w_in, down_w_out)
    got, wanted = call(
        column_kernel,
        [VMEM] * (4 + peers // 2),
        [shape(degree * (count + rows), width), shape(count + rows, width)],
    )(coarse_hot, parent_hot, high, low, *columns)
    fine_out, coarse_out = call(
        coarse_kernel,
        [VMEM] * (8 + peers // 2),
        [shape(full, LANES), shape(own, LANES)],
        [
            pltpu.VMEM((full, LANES), f32), pltpu.VMEM((own, LANES), f32),
            pltpu.SemaphoreType.DMA((3,)),
        ],
        HBM,
    )(hidden, coarse_hot, parent_hot, got, wanted, high, low, pack, *across)
    return (fine_out.reshape(fine_state.shape), coarse_out.reshape(coarse_state.shape))


def shards(*args):
    fine_state, coarse_state, fine_senders = args[0], args[1], args[2]
    coarse_owner, layers = args[5], args[7].shape[0]
    peers = lax.axis_size("sp")
    rows, samples, width = fine_state.shape
    count = coarse_state.shape[0]
    fits = (
        samples == 1
        and layers == 2
        and width % LANES == 0
        and peers % 2 == 0
        and peers & (peers - 1) == 0
        and rows % LANES == 0
        and rows >= HALO
        and count & (count - 1) == 0
        and LANES % count == 0
        and coarse_owner.shape[0] % LANES == 0
        and coarse_owner.shape[0] == 4 * count
        and fine_senders.shape[0] == 8 * LANES
        and rows == 2 * LANES
        and coarse_owner.shape[0] == 2 * LANES
        and width == args[7].shape[2]
        and peers * count <= 1024
        and peers >= 4
        and rows >= 2 * HALO
    )
    if not fits:
        return general_shards(*args)
    return kernel_shards(*args)


def solution(mesh):
    in_specs = (
        P("sp", ("grp", "ch"), None),
        P("sp", ("grp", "ch"), None),
        P("sp"),
        P("sp", None),
        P("sp"),
        P("sp", None),
        P("sp"),
    ) + (P(),) * 14
    out_specs = (P("sp", ("grp", "ch"), None), P("sp", ("grp", "ch"), None))
    return jax.shard_map(shards, mesh=mesh, in_specs=in_specs, out_specs=out_specs, check_vma=False)
```

```python
import functools
import jax
import jax.numpy as jnp
from jax import lax
from jax.experimental import pallas as pl
from jax.experimental.pallas import tpu as pltpu
from jax.sharding import PartitionSpec as P

HALO = 128
LANES = 128


epsilon = 1e-05
highest = lax.Precision.HIGHEST


def extended_2(cells, sides, width):
    for axis, dim in sides:
        count = lax.axis_size(axis)
        head = lax.slice_in_dim(cells, 0, width, axis=dim)
        tail = lax.slice_in_dim(cells, cells.shape[dim] - width, cells.shape[dim], axis=dim)
        cells = jnp.concatenate(
            [
                lax.ppermute(tail, axis, [(i, (i + 1) % count) for i in range(count)]),
                cells,
                lax.ppermute(head, axis, [((i + 1) % count, i) for i in range(count)]),
            ],
            axis=dim,
        )
    return cells


def layer_norm(values):
    average = jnp.mean(values, axis=-1, keepdims=True)
    centered = values - average
    spread = jnp.mean(centered * centered, axis=-1, keepdims=True)
    return centered / jnp.sqrt(spread + epsilon)


def project(values, matrix):
    return jnp.einsum(
        "nsd,dh->nsh", values, matrix, precision=highest, preferred_element_type=jnp.float32
    )


def slot_ranks(owners, peer_count):
    matches = (owners[:, None] == jnp.arange(peer_count, dtype=jnp.int32)[None, :]).astype(
        jnp.int32
    )
    ranking = jnp.cumsum(matches, axis=0) - 1
    return jnp.sum(ranking * matches, axis=1)


def general_shards(
    fine_state,
    coarse_state,
    fine_senders,
    up_owner,
    up_local,
    coarse_owner,
    coarse_local,
    fine_w_send,
    fine_w_recv,
    fine_bias,
    fine_w_out,
    up_w_in,
    up_bias,
    up_w_out,
    coarse_w_send,
    coarse_w_recv,
    coarse_bias,
    coarse_w_out,
    down_w_in,
    down_bias,
    down_w_out,
):
    peer_count = lax.axis_size("sp")
    fine_rows = fine_state.shape[0]
    coarse_rows = coarse_state.shape[0]
    samples = fine_state.shape[1]
    feature_width = fine_state.shape[2]
    degree_fine = fine_senders.shape[0] // fine_rows
    degree_coarse = coarse_owner.shape[0] // coarse_rows
    hidden_state = fine_state
    for layer_index in range(fine_w_send.shape[0]):
        normed = layer_norm(hidden_state)
        outward = project(normed, fine_w_send[layer_index])
        inward = project(normed, fine_w_recv[layer_index]) + fine_bias[layer_index]
        extended = extended_2(outward, (("sp", 0),), HALO)
        gathered = extended[fine_senders].reshape(fine_rows, degree_fine, samples, -1)
        summed = jnp.sum(jax.nn.silu(gathered + inward[:, None]), axis=1)
        hidden_state = hidden_state + project(summed, fine_w_out[layer_index])
    capacity = max(4, 2 * fine_rows // peer_count)
    owners = up_owner[:, 0]
    places = owners * capacity + slot_ranks(owners, peer_count)
    targets = (
        jnp.full((peer_count * capacity,), -1.0, jnp.float32)
        .at[places]
        .set(up_local.astype(jnp.float32))
        .reshape(peer_count, capacity)
    )
    activated = jax.nn.silu(project(layer_norm(hidden_state), up_w_in) + up_bias)
    coarse_ids = jnp.arange(coarse_rows, dtype=jnp.float32)[:, None]
    messages = project(activated, up_w_out)
    outgoing = (
        jnp.zeros((peer_count * capacity, samples, feature_width), jnp.float32)
        .at[places]
        .set(messages)
        .reshape(peer_count, capacity, samples, feature_width)
    )
    arrived, sources = (
        lax.all_to_all(outgoing, "sp", split_axis=0, concat_axis=0, tiled=True),
        lax.all_to_all(targets, "sp", split_axis=0, concat_axis=0, tiled=True),
    )
    selector = (sources.reshape(1, -1) == coarse_ids).astype(jnp.float32)
    gained = jnp.einsum(
        "cr,rsd->csd",
        selector,
        arrived.reshape(peer_count * capacity, samples, feature_width),
        precision=highest,
        preferred_element_type=jnp.float32,
    )
    coarse = coarse_state + gained
    normed = layer_norm(coarse)
    outward = project(normed, coarse_w_send)
    inward = project(normed, coarse_w_recv) + coarse_bias
    anchor_owner = coarse_owner[:, 0]
    everything = lax.all_gather(outward, "sp", axis=0, tiled=True)
    picked = everything[anchor_owner * coarse_rows + coarse_local]
    edge_terms = picked.reshape(coarse_rows, degree_coarse, samples, -1)
    summed = jnp.sum(jax.nn.silu(edge_terms + inward[:, None]), axis=1)
    coarse_out = coarse + project(summed, coarse_w_out)
    downward = project(
        jax.nn.silu(project(layer_norm(coarse_out), down_w_in) + down_bias), down_w_out
    )
    wanted = jnp.maximum(sources.reshape(-1), 0.0).astype(jnp.int32)
    replies = downward[wanted].reshape(peer_count, capacity, samples, feature_width)
    answered = lax.all_to_all(replies, "sp", split_axis=0, concat_axis=0, tiled=True)
    fine_out = (
        hidden_state + answered.reshape(peer_count * capacity, samples, feature_width)[places]
    )
    return (fine_out, coarse_out)


f32 = jnp.float32
bf16 = jnp.bfloat16


def load_rows(ref, rows, parts, start=0):
    return jnp.concatenate(
        [ref[pl.ds(start * parts + j, rows, stride=parts), :] for j in range(parts)], axis=1
    )


def store_rows(ref, values, parts, start=0):
    for j in range(parts):
        ref[pl.ds(start * parts + j, values.shape[0], stride=parts), :] = values[
            :, j * LANES : (j + 1) * LANES
        ]


def halves(values):
    high = values.astype(bf16)
    return high, (values - high.astype(f32)).astype(bf16)


def mm(a, b):
    return jnp.dot(a, b, preferred_element_type=f32)


def times(values, high, low, pieces=1):
    size = values.shape[0] // pieces
    done = []
    for j in range(pieces):
        vh, vl = halves(values[j * size : (j + 1) * size, :])
        done.append(mm(vh, high) + (mm(vl, high) + mm(vh, low)))
    return jnp.concatenate(done, axis=0)


def take(one_hot, high, low):
    return mm(one_hot, high) + mm(one_hot, low)


def place():
    return lax.axis_index("sp").astype(jnp.int32)


def unit(values):
    width = values.shape[1]
    average = jnp.sum(values, axis=1, keepdims=True) * (1.0 / width)
    centered = values - average
    spread = jnp.sum(centered * centered, axis=1, keepdims=True) * (1.0 / width)
    return centered * lax.rsqrt(spread + epsilon)


def gate(half):
    return half + half * jnp.tanh(half)


def equal(column, count):
    ids = lax.broadcasted_iota(jnp.int32, (column.shape[0], count), 1).astype(f32)
    return jnp.where(ids == column, 1.0, 0.0).astype(bf16)


def turned(lines):
    pad = jnp.zeros((LANES - lines.shape[0], LANES), f32)
    return jnp.transpose(jnp.concatenate([lines, pad], axis=0))


def edge_hot(hot_ref, turn_ref, lines, degree, nodes, flip=None):
    turn_ref[...] = turned(lines)
    step = LANES // degree
    for k in range(degree):
        spread = turn_ref[pl.ds(k, step, stride=degree), :]
        if flip is not None:
            spread = jnp.bitwise_xor(spread.astype(jnp.int32), flip).astype(f32)
        for line in range(lines.shape[0]):
            start = k * nodes + line * step
            hot_ref[start : start + step, :] = equal(
                spread[:, line : line + 1], hot_ref.shape[1]
            )


def split_into(high_ref, low_ref, *matrices):
    for j, matrix in enumerate(matrices):
        size = matrix.shape[0]
        high_ref[j * size : (j + 1) * size, :], low_ref[j * size : (j + 1) * size, :] = halves(
            matrix
        )


def weights(high_ref, low_ref, j):
    size = high_ref.shape[1]
    return high_ref[j * size : (j + 1) * size, :], low_ref[j * size : (j + 1) * size, :]


def start_kernel(
    count, halo, state_hbm, sender_hbm, owner_hbm, local_hbm, cowner_hbm,
    clocal_hbm, fb_hbm, ub_hbm, cb_hbm, db_hbm,
    state_ref, ints_ref, pack_ref, swap_ref, diag_ref,
    sender_ref, owner_ref, local_ref, cowner_ref, clocal_ref, fb_ref, ub_ref, cb_ref, db_ref,
    sems,
):
    odd = place() % 2
    rim = diag_ref.shape[0]
    far = state_hbm.shape[0] - rim
    mine = pl.ds(pl.multiple_of((1 - odd) * far, LANES), rim)
    away = pl.ds(pl.multiple_of(odd * far, LANES), rim)
    pairs = [
        (sender_hbm, sender_ref),
        (owner_hbm, owner_ref),
        (local_hbm, local_ref),
        (cowner_hbm, cowner_ref),
        (clocal_hbm, clocal_ref),
        (fb_hbm, fb_ref),
        (ub_hbm, ub_ref),
        (cb_hbm, cb_ref),
        (db_hbm, db_ref),
        (state_hbm.at[mine, :], swap_ref.at[0:rim, :]),
        (state_hbm.at[away, :], diag_ref),
        (state_hbm, state_ref),
    ]
    copies = [pltpu.make_async_copy(a, b, sems.at[j]) for j, (a, b) in enumerate(pairs)]
    for copy in copies:
        copy.start()
    for copy in copies[:-3]:
        copy.wait()
    rows = state_hbm.shape[0] * LANES // fb_ref.shape[1]
    sender = sender_ref[...]
    before = rows + (1 - odd) * halo
    after = rows + odd * halo
    index = jnp.where(
        sender < halo,
        sender + before,
        jnp.where(sender < halo + rows, sender - halo, sender - (halo + rows) + after),
    )
    lines = [
        index.astype(f32),
        (owner_ref[...] * count + local_ref[...]).astype(f32),
        (cowner_ref[...] * count + clocal_ref[...]).astype(f32),
    ]
    rest = ints_ref.shape[0] - sum(x.shape[0] for x in lines)
    ints = jnp.concatenate(lines + [jnp.zeros((rest, LANES), f32)], axis=0)
    ints_ref[...] = ints
    swap_ref[rim:, :] = ints
    pack_ref[...] = jnp.concatenate(
        [fb_ref[...], ub_ref[...], cb_ref[...], db_ref[...]]
        + [jnp.zeros((3, fb_ref.shape[1]), f32)],
        axis=0,
    )
    for copy in copies[-3:]:
        copy.wait()


def near_kernel(
    edges, state_ref, ints_ref, ws_hbm, wr_hbm, wo_hbm, pack_ref,
    hot_ref, got_ref, into_ref, high_ref, low_ref, turn_ref, ws_ref, wr_ref, wo_ref, sems,
):
    rows, width = into_ref.shape
    parts = width // LANES
    pairs = ((ws_hbm, ws_ref), (wr_hbm, wr_ref), (wo_hbm, wo_ref))
    copies = [
        pltpu.make_async_copy(a.at[0], b, sems.at[j]) for j, (a, b) in enumerate(pairs)
    ]
    for copy in copies:
        copy.start()
    edge_hot(hot_ref, turn_ref, ints_ref[: edges // LANES, :], edges // rows, rows)
    normed = unit(load_rows(state_ref, rows, parts))
    for copy in copies:
        copy.wait()
    split_into(high_ref, low_ref, ws_ref[...], wo_ref[...])
    into_ref[...] = (times(normed, *halves(wr_ref[...])) + pack_ref[0:1, :]) * 0.5
    high, low = halves(times(normed, *weights(high_ref, low_ref, 0)) * 0.5)
    got_ref[...] = take(hot_ref[:, :rows], high, low)


def far_kernel(
    swap_ref, diag_ref, state_ref, hot_ref, got_ref, into_ref, high_ref, low_ref,
    out_full_ref, out_half_ref,
):
    rows, width = into_ref.shape
    parts = width // LANES
    rim = diag_ref.shape[0] // parts
    degree = hot_ref.shape[0] // rows
    far = jnp.concatenate(
        [load_rows(swap_ref, rim, parts), load_rows(diag_ref, rim, parts)], axis=0
    )
    high, low = halves(times(unit(far), *weights(high_ref, low_ref, 0), 2) * 0.5)
    total = None
    for k in range(degree):
        part = slice(k * rows, (k + 1) * rows)
        half = got_ref[part, :] + into_ref[...] + take(hot_ref[part, rows:], high, low)
        total = gate(half) if total is None else total + gate(half)
    store_rows(
        out_full_ref,
        load_rows(state_ref, rows, parts) + times(total, *weights(high_ref, low_ref, 1), 2),
        parts,
    )
    lines = out_half_ref.shape[0]
    start = pl.multiple_of(place() % 2 * (rows * parts - lines), LANES)
    out_half_ref[...] = out_full_ref[pl.ds(start, lines), :]


def near2_kernel(
    edges, count, state_ref, ints_ref, ints0_ref, hot_ref, ws_ref, wr_ref, wo_ref, wi_ref,
    wu_ref, pack_ref,
    got_ref, into_ref, own_high_ref, own_low_ref, hot2_ref, select_ref, high_ref, low_ref,
    turn_ref,
):
    rows, width = into_ref.shape
    parts = width // LANES
    senders = edges // LANES
    split_into(
        high_ref, low_ref, ws_ref[1], wr_ref[1], wo_ref[1], wi_ref[...], wu_ref[...]
    )
    normed = unit(load_rows(state_ref, rows, parts))
    into_ref[...] = (times(normed, *weights(high_ref, low_ref, 1)) + pack_ref[1:2, :]) * 0.5
    high, low = halves(times(normed, *weights(high_ref, low_ref, 0)) * 0.5)
    own_high_ref[...] = high
    own_low_ref[...] = low
    got_ref[...] = take(hot_ref[:, :rows], high, low)
    first = ints0_ref.shape[0] - ints_ref.shape[0]
    edge_hot(hot2_ref, turn_ref, ints0_ref[first : first + senders, :], edges // rows, rows)
    flip = place() * count
    line = senders
    for half, ref, base in ((0, ints_ref, 0), (1, ints0_ref, first)):
        for j in range(rows // LANES):
            parent = ref[base + line + j : base + line + j + 1, :].astype(jnp.int32)
            parent = jnp.bitwise_xor(parent, flip)
            ids = lax.broadcasted_iota(jnp.int32, (select_ref.shape[0], LANES), 0)
            ids = ids + jnp.bitwise_and(ids, -count)
            start = half * rows + j * LANES
            select_ref[:, start : start + LANES] = jnp.where(ids == parent, 1.0, 0.0).astype(
                bf16
            )


def up_kernel(
    swap_ref, pair_ref, diag_ref, state_ref, hot_ref, got_ref, into_ref, own_high_ref,
    own_low_ref, hot2_ref, select_ref, ints_ref, ints0_ref, high_ref, low_ref, pack_ref,
    last_ref, *refs,
):
    *slot_refs, th_ref, tl_ref = refs
    rows, width = into_ref.shape
    parts = width // LANES
    rim = diag_ref.shape[0] // parts
    degree = hot_ref.shape[0] // rows
    odd = place() % 2
    mine = pl.multiple_of((1 - odd) * (rows - rim), LANES)
    theirs = pl.multiple_of(odd * (rows - rim), LANES)
    other = load_rows(swap_ref, rows, parts)
    normed = unit(
        jnp.concatenate(
            [other, load_rows(pair_ref, rim, parts), load_rows(diag_ref, rim, parts)], axis=0
        )
    )
    sends = halves(times(normed, *weights(high_ref, low_ref, 0), 2) * 0.5)
    near = []
    for src, t_ref, own_ref in (
        (sends[0], th_ref, own_high_ref), (sends[1], tl_ref, own_low_ref),
    ):
        t_ref[:rows, :] = src[:rows, :]
        t_ref[rows : rows + rim, :] = own_ref[pl.ds(mine, rim), :]
        t_ref[rows + rim :, :] = src[rows : rows + rim, :]
        near.append(
            jnp.concatenate([t_ref[pl.ds(theirs, rim), :], src[rows + rim :, :]], axis=0)
        )
    into = (times(normed[:rows, :], *weights(high_ref, low_ref, 1)) + pack_ref[1:2, :]) * 0.5
    total, total2 = None, None
    for k in range(degree):
        part = slice(k * rows, (k + 1) * rows)
        half = got_ref[part, :] + into_ref[...] + take(hot_ref[part, rows:], *near)
        total = gate(half) if total is None else total + gate(half)
        half = into + take(hot2_ref[part, :], th_ref[...], tl_ref[...])
        total2 = gate(half) if total2 is None else total2 + gate(half)
    hidden = jnp.concatenate([load_rows(state_ref, rows, parts), other], axis=0) + times(
        jnp.concatenate([total, total2], axis=0), *weights(high_ref, low_ref, 2), 2
    )
    last_ref[...] = hidden[:rows, :]
    act = gate((times(unit(hidden), *weights(high_ref, low_ref, 3), 2) + pack_ref[2:3, :]) * 0.5)
    sums = take(select_ref[...], *halves(times(act, *weights(high_ref, low_ref, 4), 2)))
    size = sums.shape[0] // len(slot_refs)
    first = hot_ref.shape[0] // LANES + rows // LANES
    base = ints0_ref.shape[0] - ints_ref.shape[0]
    anchor = (slot_refs[0].shape[0] - size * parts) // 4
    for j, slot in enumerate(slot_refs):
        store_rows(slot, sums[j * size : (j + 1) * size, :], parts)
        slot[size * parts :, :] = jnp.concatenate(
            [
                ints_ref[first : first + anchor, :],
                ints0_ref[base + first : base + first + anchor, :],
                jnp.zeros((2 * anchor, LANES), f32),
            ],
            axis=0,
        )


def middle_kernel(state_ref, *refs):
    out_ref = refs[-1]
    total = state_ref[...]
    for ref in refs[:-1]:
        total = total + ref[: out_ref.shape[0], :]
    out_ref[...] = total


def position(ids, flip):
    return jnp.bitwise_xor(ids.astype(jnp.int32), flip)


def split_kernel(cs_ref, cr_ref, co_ref, di_ref, do_ref, high_ref, low_ref):
    split_into(
        high_ref, low_ref, cs_ref[...], cr_ref[...], co_ref[...], di_ref[...], do_ref[...]
    )


def edges_kernel(degree, count, ints_ref, *refs):
    *slot_refs, hot_ref, parent_ref, turn_ref = refs
    rows, coarse = parent_ref.shape
    flip = place() * count
    columns = turned(ints_ref[...])
    first = ints_ref.shape[0] // 2
    for j in range(rows // LANES):
        column = position(columns[:, first + j : first + j + 1], flip).astype(f32)
        parent_ref[j * LANES : (j + 1) * LANES, :] = equal(column, coarse)
    here = coarse * degree // LANES // len(slot_refs)
    lines = jnp.concatenate(
        [ref[ref.shape[0] - 2 * here : ref.shape[0] - here, :] for ref in slot_refs], axis=0
    )
    turn_ref[...] = turned(lines)
    step = LANES // degree
    lane = lax.broadcasted_iota(jnp.int32, (coarse, LANES), 1)
    table = jnp.zeros((coarse, LANES), f32)
    each = hot_ref.shape[0] // degree
    for k in range(degree):
        spread = position(turn_ref[pl.ds(k, step, stride=degree), :], flip)
        column = jnp.concatenate([spread[:, j : j + 1] for j in range(lines.shape[0])], axis=0)
        hot_ref[k * each : k * each + count, :] = equal(column[:count, :].astype(f32), coarse)
        high = jnp.right_shift(column, 8).astype(f32)
        low = jnp.bitwise_and(column, 255).astype(f32)
        table = jnp.where(lane == k, high, jnp.where(lane == degree + k, low, table))
    found = mm(parent_ref[...], table.astype(bf16))
    for k in range(degree):
        column = found[:, k : k + 1] * 256.0 + found[:, degree + k : degree + k + 1]
        hot_ref[k * each + count : (k + 1) * each, :] = equal(column, coarse)


def column_kernel(hot_ref, parent_ref, high_ref, low_ref, *refs):
    *blocks, got_ref, wanted_ref = refs
    _, width = wanted_ref.shape
    parts = width // LANES
    count = blocks[0].shape[0] // parts
    middle = jnp.concatenate([load_rows(b, count, parts) for b in blocks], axis=0)
    half = count * len(blocks)
    sends = halves(times(unit(middle), *weights(high_ref, low_ref, 0)) * 0.5)
    got_ref[...] = take(hot_ref[:, :half], *sends)
    wanted_ref[:count, :] = middle[:count, :]
    wanted_ref[count:, :] = take(parent_ref[:, :half], *halves(middle))


def coarse_kernel(
    last_ref, hot_ref, parent_ref, got_ref, wanted_ref, high_ref, low_ref, pack_ref, *refs
):
    *blocks, fine_hbm, coarse_hbm, fine_ref, coarse_ref, sems = refs
    rows, width = last_ref.shape
    parts = width // LANES
    count = coarse_ref.shape[0] // parts
    need = count + rows
    middle = jnp.concatenate([load_rows(b, count, parts) for b in blocks], axis=0)
    half = count * len(blocks)
    sends = halves(times(unit(middle), *weights(high_ref, low_ref, 0)) * 0.5)
    wanted = jnp.concatenate(
        [
            wanted_ref[:count, :],
            wanted_ref[count:, :] + take(parent_ref[:, half:], *halves(middle)),
        ],
        axis=0,
    )
    into = (times(unit(wanted), *weights(high_ref, low_ref, 1)) + pack_ref[3:4, :]) * 0.5
    total = None
    for k in range(hot_ref.shape[0] // need):
        part = slice(k * need, (k + 1) * need)
        term = gate(got_ref[part, :] + into + take(hot_ref[part, half:], *sends))
        total = term if total is None else total + term
    done = wanted + times(total, *weights(high_ref, low_ref, 2))
    store_rows(coarse_ref, done[:count, :], parts)
    copies = [pltpu.make_async_copy(coarse_ref, coarse_hbm, sems.at[0])]
    copies[0].start()
    act = gate(
        (times(unit(done[count:, :]), *weights(high_ref, low_ref, 3)) + pack_ref[4:5, :]) * 0.5
    )
    size = rows // 2
    for j in range(2):
        down = times(act[j * size : (j + 1) * size, :], *weights(high_ref, low_ref, 4))
        store_rows(fine_ref, last_ref[j * size : (j + 1) * size, :] + down, parts, j * size)
        piece = pl.ds(j * size * parts, size * parts)
        copies.append(
            pltpu.make_async_copy(fine_ref.at[piece, :], fine_hbm.at[piece, :], sems.at[j + 1])
        )
        copies[-1].start()
    for copy in copies:
        copy.wait()


VMEM = pl.BlockSpec(memory_space=pltpu.VMEM)
SMEM = pl.BlockSpec(memory_space=pltpu.SMEM)
HBM = pl.BlockSpec(memory_space=pltpu.HBM)


def call(kernel, in_specs, out_shapes, scratch=(), out_spec=VMEM):
    return pl.pallas_call(
        kernel,
        in_specs=in_specs,
        out_specs=[out_spec] * len(out_shapes),
        out_shape=out_shapes,
        scratch_shapes=scratch,
        compiler_params=pltpu.CompilerParams(vmem_limit_bytes=32 * 2**20),
    )


def move(values, pairs):
    return lax.ppermute(values, "sp", pairs)


def shape(*dims, kind=f32):
    return jax.ShapeDtypeStruct(dims, kind)


def kernel_shards(
    fine_state,
    coarse_state,
    fine_senders,
    up_owner,
    up_local,
    coarse_owner,
    coarse_local,
    fine_w_send,
    fine_w_recv,
    fine_bias,
    fine_w_out,
    up_w_in,
    up_bias,
    up_w_out,
    coarse_w_send,
    coarse_w_recv,
    coarse_bias,
    coarse_w_out,
    down_w_in,
    down_bias,
    down_w_out,
):
    peers = lax.axis_size("sp")
    me = lax.axis_index("sp").astype(jnp.int32)
    rows, _, width = fine_state.shape
    count = coarse_state.shape[0]
    parts = width // LANES
    edges = fine_senders.shape[0]
    coarse_edges = coarse_owner.shape[0]
    coarse = peers * count
    window = rows + 2 * HALO
    rim, own, full = HALO * parts, count * parts, rows * parts
    size = width
    swap = [(i, i ^ 1) for i in range(peers)]
    diag = [(i, (i + 1 if i % 2 else i - 1) % peers) for i in range(peers)]
    pair = [(i, (i + 2 if i % 2 else i - 2) % peers) for i in range(peers)]
    flips = [[(i, i ^ (2 * j)) for i in range(peers)] for j in range(peers // 2)]
    lines = lambda x: x.reshape(-1, LANES)
    row = lambda x: x.reshape(1, width)
    turn = pltpu.VMEM((LANES, LANES), f32)
    here = lambda *xs: [pltpu.with_memory_space_constraint(x, pltpu.HBM) for x in xs]
    hot_shape = shape(edges, window, kind=bf16)
    small = lambda ref: pltpu.VMEM(ref.shape, ref.dtype)

    small_args = [
        lines(fine_senders), lines(up_owner), lines(up_local), lines(coarse_owner),
        lines(coarse_local), fine_bias, row(up_bias), row(coarse_bias), row(down_bias),
    ]
    state, ints, pack, out_swap, out_diag = call(
        functools.partial(start_kernel, count, HALO),
        [HBM] * 10,
        [
            shape(full, LANES), shape(16, LANES), shape(8, width), shape(rim + 16, LANES),
            shape(rim, LANES),
        ],
        [small(x) for x in small_args] + [pltpu.SemaphoreType.DMA((12,))],
    )(*here(lines(fine_state), *small_args))
    swap0 = move(out_swap, swap)
    diag0 = move(out_diag, diag)
    hot, got, into, high, low = call(
        functools.partial(near_kernel, edges),
        [VMEM] * 2 + [HBM] * 3 + [VMEM],
        [hot_shape, shape(edges, width), shape(rows, width)]
        + [shape(2 * size, width, kind=bf16)] * 2,
        [turn] + [pltpu.VMEM((size, width), f32)] * 3 + [pltpu.SemaphoreType.DMA((3,))],
    )(state, ints, *here(fine_w_send, fine_w_recv, fine_w_out), pack)
    state, out_half = call(
        far_kernel, [VMEM] * 8, [shape(full, LANES), shape(rim, LANES)]
    )(swap0, diag0, state, hot, got, into, high, low)
    swap1 = move(state, swap)
    diag1 = move(out_half, diag)
    pair1 = move(out_half, pair)
    got, into, own_high, own_low, hot2, select, high, low = call(
        functools.partial(near2_kernel, edges, count),
        [VMEM] * 10,
        [shape(edges, width), shape(rows, width)]
        + [shape(rows, width, kind=bf16)] * 2
        + [hot_shape, shape(coarse // 2, 2 * rows, kind=bf16)]
        + [shape(5 * size, width, kind=bf16)] * 2,
        [turn],
    )(
        state, ints, swap0, hot, fine_w_send, fine_w_recv, fine_w_out, up_w_in, up_w_out,
        pack,
    )
    hidden, *slots = call(
        up_kernel,
        [VMEM] * 16,
        [shape(rows, width)]
        + [shape(own + 8 * coarse_edges // 256, LANES)] * (peers // 2),
        [pltpu.VMEM((window, width), bf16)] * 2,
    )(
        swap1, pair1, diag1, state, hot, got, into, own_high, own_low, hot2, select, ints, swap0,
        high, low, pack,
    )
    arrived = [slots[0]] + [move(slots[j], flips[j]) for j in range(1, peers // 2)]
    (middle,) = call(
        middle_kernel, [VMEM] * (1 + peers // 2), [shape(own, LANES)]
    )(lines(coarse_state), *arrived)
    shift = lambda k: [(i, i ^ k) for i in range(peers)]
    near, far = [middle], [move(middle, shift(peers // 2))]
    for k in range(1, peers // 2):
        near.append(move(middle, shift(k)))
        far.append(move(far[0], shift(k)))
    degree = coarse_edges // count
    coarse_hot, parent_hot = call(
        functools.partial(edges_kernel, degree, count),
        [VMEM] * (1 + peers // 2),
        [
            shape(degree * (count + rows), coarse, kind=bf16),
            shape(rows, coarse, kind=bf16),
        ],
        [turn],
    )(ints, *arrived)
    high, low = call(
        split_kernel, [VMEM] * 5, [shape(5 * size, width, kind=bf16)] * 2
    )(coarse_w_send, coarse_w_recv, coarse_w_out, down_w_in, down_w_out)
    got, wanted = call(
        column_kernel,
        [VMEM] * (4 + peers // 2),
        [shape(degree * (count + rows), width), shape(count + rows, width)],
    )(coarse_hot, parent_hot, high, low, *near)
    fine_out, coarse_out = call(
        coarse_kernel,
        [VMEM] * (8 + peers // 2),
        [shape(full, LANES), shape(own, LANES)],
        [
            pltpu.VMEM((full, LANES), f32), pltpu.VMEM((own, LANES), f32),
            pltpu.SemaphoreType.DMA((3,)),
        ],
        HBM,
    )(hidden, coarse_hot, parent_hot, got, wanted, high, low, pack, *far)
    return (fine_out.reshape(fine_state.shape), coarse_out.reshape(coarse_state.shape))


def shards(*args):
    fine_state, coarse_state, fine_senders = args[0], args[1], args[2]
    coarse_owner, layers = args[5], args[7].shape[0]
    peers = lax.axis_size("sp")
    rows, samples, width = fine_state.shape
    count = coarse_state.shape[0]
    fits = (
        samples == 1
        and layers == 2
        and width % LANES == 0
        and peers % 2 == 0
        and peers & (peers - 1) == 0
        and rows % LANES == 0
        and rows >= HALO
        and count & (count - 1) == 0
        and LANES % count == 0
        and coarse_owner.shape[0] % LANES == 0
        and coarse_owner.shape[0] == 4 * count
        and fine_senders.shape[0] == 8 * LANES
        and rows == 2 * LANES
        and coarse_owner.shape[0] == 2 * LANES
        and width == args[7].shape[2]
        and peers * count <= 1024
        and peers >= 4
        and rows >= 2 * HALO
    )
    if not fits:
        return general_shards(*args)
    return kernel_shards(*args)


def solution(mesh):
    in_specs = (
        P("sp", ("grp", "ch"), None),
        P("sp", ("grp", "ch"), None),
        P("sp"),
        P("sp", None),
        P("sp"),
        P("sp", None),
        P("sp"),
    ) + (P(),) * 14
    out_specs = (P("sp", ("grp", "ch"), None), P("sp", ("grp", "ch"), None))
    return jax.shard_map(shards, mesh=mesh, in_specs=in_specs, out_specs=out_specs, check_vma=False)
```

```python
import functools
import jax
import jax.numpy as jnp
from jax import lax
from jax.experimental import pallas as pl
from jax.experimental.pallas import tpu as pltpu
from jax.sharding import PartitionSpec as P

HALO = 128
LANES = 128


epsilon = 1e-05
highest = lax.Precision.HIGHEST


def extended_2(cells, sides, width):
    for axis, dim in sides:
        count = lax.axis_size(axis)
        head = lax.slice_in_dim(cells, 0, width, axis=dim)
        tail = lax.slice_in_dim(cells, cells.shape[dim] - width, cells.shape[dim], axis=dim)
        cells = jnp.concatenate(
            [
                lax.ppermute(tail, axis, [(i, (i + 1) % count) for i in range(count)]),
                cells,
                lax.ppermute(head, axis, [((i + 1) % count, i) for i in range(count)]),
            ],
            axis=dim,
        )
    return cells


def layer_norm(values):
    average = jnp.mean(values, axis=-1, keepdims=True)
    centered = values - average
    spread = jnp.mean(centered * centered, axis=-1, keepdims=True)
    return centered / jnp.sqrt(spread + epsilon)


def project(values, matrix):
    return jnp.einsum(
        "nsd,dh->nsh", values, matrix, precision=highest, preferred_element_type=jnp.float32
    )


def slot_ranks(owners, peer_count):
    matches = (owners[:, None] == jnp.arange(peer_count, dtype=jnp.int32)[None, :]).astype(
        jnp.int32
    )
    ranking = jnp.cumsum(matches, axis=0) - 1
    return jnp.sum(ranking * matches, axis=1)


def general_shards(
    fine_state,
    coarse_state,
    fine_senders,
    up_owner,
    up_local,
    coarse_owner,
    coarse_local,
    fine_w_send,
    fine_w_recv,
    fine_bias,
    fine_w_out,
    up_w_in,
    up_bias,
    up_w_out,
    coarse_w_send,
    coarse_w_recv,
    coarse_bias,
    coarse_w_out,
    down_w_in,
    down_bias,
    down_w_out,
):
    peer_count = lax.axis_size("sp")
    fine_rows = fine_state.shape[0]
    coarse_rows = coarse_state.shape[0]
    samples = fine_state.shape[1]
    feature_width = fine_state.shape[2]
    degree_fine = fine_senders.shape[0] // fine_rows
    degree_coarse = coarse_owner.shape[0] // coarse_rows
    hidden_state = fine_state
    for layer_index in range(fine_w_send.shape[0]):
        normed = layer_norm(hidden_state)
        outward = project(normed, fine_w_send[layer_index])
        inward = project(normed, fine_w_recv[layer_index]) + fine_bias[layer_index]
        extended = extended_2(outward, (("sp", 0),), HALO)
        gathered = extended[fine_senders].reshape(fine_rows, degree_fine, samples, -1)
        summed = jnp.sum(jax.nn.silu(gathered + inward[:, None]), axis=1)
        hidden_state = hidden_state + project(summed, fine_w_out[layer_index])
    capacity = max(4, 2 * fine_rows // peer_count)
    owners = up_owner[:, 0]
    places = owners * capacity + slot_ranks(owners, peer_count)
    targets = (
        jnp.full((peer_count * capacity,), -1.0, jnp.float32)
        .at[places]
        .set(up_local.astype(jnp.float32))
        .reshape(peer_count, capacity)
    )
    activated = jax.nn.silu(project(layer_norm(hidden_state), up_w_in) + up_bias)
    coarse_ids = jnp.arange(coarse_rows, dtype=jnp.float32)[:, None]
    messages = project(activated, up_w_out)
    outgoing = (
        jnp.zeros((peer_count * capacity, samples, feature_width), jnp.float32)
        .at[places]
        .set(messages)
        .reshape(peer_count, capacity, samples, feature_width)
    )
    arrived, sources = (
        lax.all_to_all(outgoing, "sp", split_axis=0, concat_axis=0, tiled=True),
        lax.all_to_all(targets, "sp", split_axis=0, concat_axis=0, tiled=True),
    )
    selector = (sources.reshape(1, -1) == coarse_ids).astype(jnp.float32)
    gained = jnp.einsum(
        "cr,rsd->csd",
        selector,
        arrived.reshape(peer_count * capacity, samples, feature_width),
        precision=highest,
        preferred_element_type=jnp.float32,
    )
    coarse = coarse_state + gained
    normed = layer_norm(coarse)
    outward = project(normed, coarse_w_send)
    inward = project(normed, coarse_w_recv) + coarse_bias
    anchor_owner = coarse_owner[:, 0]
    everything = lax.all_gather(outward, "sp", axis=0, tiled=True)
    picked = everything[anchor_owner * coarse_rows + coarse_local]
    edge_terms = picked.reshape(coarse_rows, degree_coarse, samples, -1)
    summed = jnp.sum(jax.nn.silu(edge_terms + inward[:, None]), axis=1)
    coarse_out = coarse + project(summed, coarse_w_out)
    downward = project(
        jax.nn.silu(project(layer_norm(coarse_out), down_w_in) + down_bias), down_w_out
    )
    wanted = jnp.maximum(sources.reshape(-1), 0.0).astype(jnp.int32)
    replies = downward[wanted].reshape(peer_count, capacity, samples, feature_width)
    answered = lax.all_to_all(replies, "sp", split_axis=0, concat_axis=0, tiled=True)
    fine_out = (
        hidden_state + answered.reshape(peer_count * capacity, samples, feature_width)[places]
    )
    return (fine_out, coarse_out)


f32 = jnp.float32
bf16 = jnp.bfloat16


def load_rows(ref, rows, parts, start=0):
    return jnp.concatenate(
        [ref[pl.ds(start * parts + j, rows, stride=parts), :] for j in range(parts)], axis=1
    )


def store_rows(ref, values, parts, start=0):
    for j in range(parts):
        ref[pl.ds(start * parts + j, values.shape[0], stride=parts), :] = values[
            :, j * LANES : (j + 1) * LANES
        ]


def halves(values):
    high = values.astype(bf16)
    return high, (values - high.astype(f32)).astype(bf16)


def mm(a, b):
    return jnp.dot(a, b, preferred_element_type=f32)


def times(values, high, low, pieces=1):
    size = values.shape[0] // pieces
    done = []
    for j in range(pieces):
        vh, vl = halves(values[j * size : (j + 1) * size, :])
        done.append(mm(vh, high) + (mm(vl, high) + mm(vh, low)))
    return jnp.concatenate(done, axis=0)


def take(one_hot, high, low):
    return mm(one_hot, high) + mm(one_hot, low)


def place():
    return lax.axis_index("sp").astype(jnp.int32)


def unit(values):
    width = values.shape[1]
    average = jnp.sum(values, axis=1, keepdims=True) * (1.0 / width)
    centered = values - average
    spread = jnp.sum(centered * centered, axis=1, keepdims=True) * (1.0 / width)
    return centered * lax.rsqrt(spread + epsilon)


def gate(half):
    return half + half * jnp.tanh(half)


def equal(column, count):
    ids = lax.broadcasted_iota(jnp.int32, (column.shape[0], count), 1).astype(f32)
    return jnp.where(ids == column, 1.0, 0.0).astype(bf16)


def turned(lines):
    pad = jnp.zeros((LANES - lines.shape[0], LANES), f32)
    return jnp.transpose(jnp.concatenate([lines, pad], axis=0))


def edge_hot(hot_ref, turn_ref, lines, degree, nodes, flip=None):
    turn_ref[...] = turned(lines)
    step = LANES // degree
    for k in range(degree):
        spread = turn_ref[pl.ds(k, step, stride=degree), :]
        if flip is not None:
            spread = jnp.bitwise_xor(spread.astype(jnp.int32), flip).astype(f32)
        for line in range(lines.shape[0]):
            start = k * nodes + line * step
            hot_ref[start : start + step, :] = equal(
                spread[:, line : line + 1], hot_ref.shape[1]
            )


def split_into(high_ref, low_ref, *matrices):
    for j, matrix in enumerate(matrices):
        size = matrix.shape[0]
        high_ref[j * size : (j + 1) * size, :], low_ref[j * size : (j + 1) * size, :] = halves(
            matrix
        )


def weights(high_ref, low_ref, j):
    size = high_ref.shape[1]
    return high_ref[j * size : (j + 1) * size, :], low_ref[j * size : (j + 1) * size, :]


def start_kernel(
    count, halo, rows, state_hbm, sender_hbm, owner_hbm, local_hbm, cowner_hbm,
    clocal_hbm, ints_ref, swap_ref, diag_ref,
    sender_ref, owner_ref, local_ref, cowner_ref, clocal_ref, sems,
):
    odd = place() % 2
    rim = diag_ref.shape[0]
    far = state_hbm.shape[0] - rim
    mine = pl.ds(pl.multiple_of((1 - odd) * far, LANES), rim)
    away = pl.ds(pl.multiple_of(odd * far, LANES), rim)
    pairs = [
        (sender_hbm, sender_ref),
        (owner_hbm, owner_ref),
        (local_hbm, local_ref),
        (cowner_hbm, cowner_ref),
        (clocal_hbm, clocal_ref),
        (state_hbm.at[mine, :], swap_ref.at[0:rim, :]),
        (state_hbm.at[away, :], diag_ref),
    ]
    copies = [pltpu.make_async_copy(a, b, sems.at[j]) for j, (a, b) in enumerate(pairs)]
    for copy in copies:
        copy.start()
    for copy in copies[:-2]:
        copy.wait()
    sender = sender_ref[...]
    before = rows + (1 - odd) * halo
    after = rows + odd * halo
    index = jnp.where(
        sender < halo,
        sender + before,
        jnp.where(sender < halo + rows, sender - halo, sender - (halo + rows) + after),
    )
    lines = [
        index.astype(f32),
        (owner_ref[...] * count + local_ref[...]).astype(f32),
        (cowner_ref[...] * count + clocal_ref[...]).astype(f32),
    ]
    rest = ints_ref.shape[0] - sum(x.shape[0] for x in lines)
    ints = jnp.concatenate(lines + [jnp.zeros((rest, LANES), f32)], axis=0)
    ints_ref[...] = ints
    swap_ref[rim:, :] = ints
    for copy in copies[-2:]:
        copy.wait()


def near_kernel(
    edges, ints_ref, state_hbm, ws_hbm, wr_hbm, wo_hbm, fb_hbm, ub_hbm, cb_hbm, db_hbm,
    hot_ref, got_ref, into_ref, high_ref, low_ref, state_ref, pack_ref,
    turn_ref, ws_ref, wr_ref, wo_ref, fb_ref, ub_ref, cb_ref, db_ref, sems,
):
    rows, width = into_ref.shape
    parts = width // LANES
    pairs = (
        (state_hbm, state_ref), (ws_hbm.at[0], ws_ref), (wr_hbm.at[0], wr_ref),
        (wo_hbm.at[0], wo_ref), (fb_hbm, fb_ref), (ub_hbm, ub_ref), (cb_hbm, cb_ref),
        (db_hbm, db_ref),
    )
    copies = [pltpu.make_async_copy(a, b, sems.at[j]) for j, (a, b) in enumerate(pairs)]
    for copy in copies:
        copy.start()
    edge_hot(hot_ref, turn_ref, ints_ref[: edges // LANES, :], edges // rows, rows)
    for copy in copies:
        copy.wait()
    pack_ref[...] = jnp.concatenate(
        [fb_ref[...], ub_ref[...], cb_ref[...], db_ref[...]]
        + [jnp.zeros((3, width), f32)],
        axis=0,
    )
    normed = unit(load_rows(state_ref, rows, parts))
    split_into(high_ref, low_ref, ws_ref[...], wo_ref[...])
    into_ref[...] = (times(normed, *halves(wr_ref[...])) + pack_ref[0:1, :]) * 0.5
    high, low = halves(times(normed, *weights(high_ref, low_ref, 0)) * 0.5)
    got_ref[...] = take(hot_ref[:, :rows], high, low)


def far_kernel(
    swap_ref, diag_ref, state_ref, hot_ref, got_ref, into_ref, high_ref, low_ref,
    out_full_ref, out_half_ref,
):
    rows, width = into_ref.shape
    parts = width // LANES
    rim = diag_ref.shape[0] // parts
    degree = hot_ref.shape[0] // rows
    far = jnp.concatenate(
        [load_rows(swap_ref, rim, parts), load_rows(diag_ref, rim, parts)], axis=0
    )
    high, low = halves(times(unit(far), *weights(high_ref, low_ref, 0), 2) * 0.5)
    total = None
    for k in range(degree):
        part = slice(k * rows, (k + 1) * rows)
        half = got_ref[part, :] + into_ref[...] + take(hot_ref[part, rows:], high, low)
        total = gate(half) if total is None else total + gate(half)
    store_rows(
        out_full_ref,
        load_rows(state_ref, rows, parts) + times(total, *weights(high_ref, low_ref, 1), 2),
        parts,
    )
    lines = out_half_ref.shape[0]
    start = pl.multiple_of(place() % 2 * (rows * parts - lines), LANES)
    out_half_ref[...] = out_full_ref[pl.ds(start, lines), :]


def near2_kernel(
    edges, count, state_ref, ints_ref, ints0_ref, hot_ref, ws_ref, wr_ref, wo_ref, wi_ref,
    wu_ref, pack_ref,
    got_ref, into_ref, own_high_ref, own_low_ref, hot2_ref, select_ref, high_ref, low_ref,
    turn_ref,
):
    rows, width = into_ref.shape
    parts = width // LANES
    senders = edges // LANES
    split_into(
        high_ref, low_ref, ws_ref[1], wr_ref[1], wo_ref[1], wi_ref[...], wu_ref[...]
    )
    normed = unit(load_rows(state_ref, rows, parts))
    into_ref[...] = (times(normed, *weights(high_ref, low_ref, 1)) + pack_ref[1:2, :]) * 0.5
    high, low = halves(times(normed, *weights(high_ref, low_ref, 0)) * 0.5)
    own_high_ref[...] = high
    own_low_ref[...] = low
    got_ref[...] = take(hot_ref[:, :rows], high, low)
    first = ints0_ref.shape[0] - ints_ref.shape[0]
    edge_hot(hot2_ref, turn_ref, ints0_ref[first : first + senders, :], edges // rows, rows)
    flip = place() * count
    line = senders
    for half, ref, base in ((0, ints_ref, 0), (1, ints0_ref, first)):
        for j in range(rows // LANES):
            parent = ref[base + line + j : base + line + j + 1, :].astype(jnp.int32)
            parent = jnp.bitwise_xor(parent, flip)
            ids = lax.broadcasted_iota(jnp.int32, (select_ref.shape[0], LANES), 0)
            ids = ids + jnp.bitwise_and(ids, -count)
            start = half * rows + j * LANES
            select_ref[:, start : start + LANES] = jnp.where(ids == parent, 1.0, 0.0).astype(
                bf16
            )


def up_kernel(
    swap_ref, pair_ref, diag_ref, state_ref, hot_ref, got_ref, into_ref, own_high_ref,
    own_low_ref, hot2_ref, select_ref, ints_ref, ints0_ref, high_ref, low_ref, pack_ref,
    last_ref, *refs,
):
    *slot_refs, th_ref, tl_ref = refs
    rows, width = into_ref.shape
    parts = width // LANES
    rim = diag_ref.shape[0] // parts
    degree = hot_ref.shape[0] // rows
    odd = place() % 2
    mine = pl.multiple_of((1 - odd) * (rows - rim), LANES)
    theirs = pl.multiple_of(odd * (rows - rim), LANES)
    other = load_rows(swap_ref, rows, parts)
    normed = unit(
        jnp.concatenate(
            [other, load_rows(pair_ref, rim, parts), load_rows(diag_ref, rim, parts)], axis=0
        )
    )
    sends = halves(times(normed, *weights(high_ref, low_ref, 0), 2) * 0.5)
    near = []
    for src, t_ref, own_ref in (
        (sends[0], th_ref, own_high_ref), (sends[1], tl_ref, own_low_ref),
    ):
        t_ref[:rows, :] = src[:rows, :]
        t_ref[rows : rows + rim, :] = own_ref[pl.ds(mine, rim), :]
        t_ref[rows + rim :, :] = src[rows : rows + rim, :]
        near.append(
            jnp.concatenate([t_ref[pl.ds(theirs, rim), :], src[rows + rim :, :]], axis=0)
        )
    into = (times(normed[:rows, :], *weights(high_ref, low_ref, 1)) + pack_ref[1:2, :]) * 0.5
    total, total2 = None, None
    for k in range(degree):
        part = slice(k * rows, (k + 1) * rows)
        half = got_ref[part, :] + into_ref[...] + take(hot_ref[part, rows:], *near)
        total = gate(half) if total is None else total + gate(half)
        half = into + take(hot2_ref[part, :], th_ref[...], tl_ref[...])
        total2 = gate(half) if total2 is None else total2 + gate(half)
    hidden = jnp.concatenate([load_rows(state_ref, rows, parts), other], axis=0) + times(
        jnp.concatenate([total, total2], axis=0), *weights(high_ref, low_ref, 2), 2
    )
    last_ref[...] = hidden[:rows, :]
    act = gate((times(unit(hidden), *weights(high_ref, low_ref, 3), 2) + pack_ref[2:3, :]) * 0.5)
    sums = take(select_ref[...], *halves(times(act, *weights(high_ref, low_ref, 4), 2)))
    size = sums.shape[0] // len(slot_refs)
    first = hot_ref.shape[0] // LANES + rows // LANES
    base = ints0_ref.shape[0] - ints_ref.shape[0]
    anchor = (slot_refs[0].shape[0] - size * parts) // 4
    for j, slot in enumerate(slot_refs):
        store_rows(slot, sums[j * size : (j + 1) * size, :], parts)
        slot[size * parts :, :] = jnp.concatenate(
            [
                ints_ref[first : first + anchor, :],
                ints0_ref[base + first : base + first + anchor, :],
                jnp.zeros((2 * anchor, LANES), f32),
            ],
            axis=0,
        )


def middle_kernel(state_ref, *refs):
    out_ref = refs[-1]
    total = state_ref[...]
    for ref in refs[:-1]:
        total = total + ref[: out_ref.shape[0], :]
    out_ref[...] = total


def position(ids, flip):
    return jnp.bitwise_xor(ids.astype(jnp.int32), flip)


def split_kernel(cs_ref, cr_ref, co_ref, di_ref, do_ref, high_ref, low_ref):
    split_into(
        high_ref, low_ref, cs_ref[...], cr_ref[...], co_ref[...], di_ref[...], do_ref[...]
    )


def edges_kernel(degree, count, ints_ref, *refs):
    *slot_refs, hot_ref, parent_ref, turn_ref = refs
    rows, coarse = parent_ref.shape
    flip = place() * count
    columns = turned(ints_ref[...])
    first = ints_ref.shape[0] // 2
    for j in range(rows // LANES):
        column = position(columns[:, first + j : first + j + 1], flip).astype(f32)
        parent_ref[j * LANES : (j + 1) * LANES, :] = equal(column, coarse)
    here = coarse * degree // LANES // len(slot_refs)
    lines = jnp.concatenate(
        [ref[ref.shape[0] - 2 * here : ref.shape[0] - here, :] for ref in slot_refs], axis=0
    )
    turn_ref[...] = turned(lines)
    step = LANES // degree
    lane = lax.broadcasted_iota(jnp.int32, (coarse, LANES), 1)
    table = jnp.zeros((coarse, LANES), f32)
    each = hot_ref.shape[0] // degree
    for k in range(degree):
        spread = position(turn_ref[pl.ds(k, step, stride=degree), :], flip)
        column = jnp.concatenate([spread[:, j : j + 1] for j in range(lines.shape[0])], axis=0)
        hot_ref[k * each : k * each + count, :] = equal(column[:count, :].astype(f32), coarse)
        high = jnp.right_shift(column, 8).astype(f32)
        low = jnp.bitwise_and(column, 255).astype(f32)
        table = jnp.where(lane == k, high, jnp.where(lane == degree + k, low, table))
    found = mm(parent_ref[...], table.astype(bf16))
    for k in range(degree):
        column = found[:, k : k + 1] * 256.0 + found[:, degree + k : degree + k + 1]
        hot_ref[k * each + count : (k + 1) * each, :] = equal(column, coarse)


def column_kernel(hot_ref, parent_ref, high_ref, low_ref, *refs):
    *blocks, got_ref, wanted_ref = refs
    _, width = wanted_ref.shape
    parts = width // LANES
    count = blocks[0].shape[0] // parts
    middle = jnp.concatenate([load_rows(b, count, parts) for b in blocks], axis=0)
    half = count * len(blocks)
    sends = halves(times(unit(middle), *weights(high_ref, low_ref, 0)) * 0.5)
    got_ref[...] = take(hot_ref[:, :half], *sends)
    wanted_ref[:count, :] = middle[:count, :]
    wanted_ref[count:, :] = take(parent_ref[:, :half], *halves(middle))


def coarse_kernel(
    last_ref, hot_ref, parent_ref, got_ref, wanted_ref, high_ref, low_ref, pack_ref, *refs
):
    *blocks, fine_hbm, coarse_hbm, fine_ref, coarse_ref, sems = refs
    rows, width = last_ref.shape
    parts = width // LANES
    count = coarse_ref.shape[0] // parts
    need = count + rows
    middle = jnp.concatenate([load_rows(b, count, parts) for b in blocks], axis=0)
    half = count * len(blocks)
    sends = halves(times(unit(middle), *weights(high_ref, low_ref, 0)) * 0.5)
    wanted = jnp.concatenate(
        [
            wanted_ref[:count, :],
            wanted_ref[count:, :] + take(parent_ref[:, half:], *halves(middle)),
        ],
        axis=0,
    )
    into = (times(unit(wanted), *weights(high_ref, low_ref, 1)) + pack_ref[3:4, :]) * 0.5
    total = None
    for k in range(hot_ref.shape[0] // need):
        part = slice(k * need, (k + 1) * need)
        term = gate(got_ref[part, :] + into + take(hot_ref[part, half:], *sends))
        total = term if total is None else total + term
    done = wanted + times(total, *weights(high_ref, low_ref, 2))
    store_rows(coarse_ref, done[:count, :], parts)
    copies = [pltpu.make_async_copy(coarse_ref, coarse_hbm, sems.at[0])]
    copies[0].start()
    act = gate(
        (times(unit(done[count:, :]), *weights(high_ref, low_ref, 3)) + pack_ref[4:5, :]) * 0.5
    )
    size = rows // 2
    for j in range(2):
        down = times(act[j * size : (j + 1) * size, :], *weights(high_ref, low_ref, 4))
        store_rows(fine_ref, last_ref[j * size : (j + 1) * size, :] + down, parts, j * size)
        piece = pl.ds(j * size * parts, size * parts)
        copies.append(
            pltpu.make_async_copy(fine_ref.at[piece, :], fine_hbm.at[piece, :], sems.at[j + 1])
        )
        copies[-1].start()
    for copy in copies:
        copy.wait()


VMEM = pl.BlockSpec(memory_space=pltpu.VMEM)
SMEM = pl.BlockSpec(memory_space=pltpu.SMEM)
HBM = pl.BlockSpec(memory_space=pltpu.HBM)


def call(kernel, in_specs, out_shapes, scratch=(), out_spec=VMEM):
    return pl.pallas_call(
        kernel,
        in_specs=in_specs,
        out_specs=[out_spec] * len(out_shapes),
        out_shape=out_shapes,
        scratch_shapes=scratch,
        compiler_params=pltpu.CompilerParams(vmem_limit_bytes=32 * 2**20),
    )


def move(values, pairs):
    return lax.ppermute(values, "sp", pairs)


def shape(*dims, kind=f32):
    return jax.ShapeDtypeStruct(dims, kind)


def kernel_shards(
    fine_state,
    coarse_state,
    fine_senders,
    up_owner,
    up_local,
    coarse_owner,
    coarse_local,
    fine_w_send,
    fine_w_recv,
    fine_bias,
    fine_w_out,
    up_w_in,
    up_bias,
    up_w_out,
    coarse_w_send,
    coarse_w_recv,
    coarse_bias,
    coarse_w_out,
    down_w_in,
    down_bias,
    down_w_out,
):
    peers = lax.axis_size("sp")
    me = lax.axis_index("sp").astype(jnp.int32)
    rows, _, width = fine_state.shape
    count = coarse_state.shape[0]
    parts = width // LANES
    edges = fine_senders.shape[0]
    coarse_edges = coarse_owner.shape[0]
    coarse = peers * count
    window = rows + 2 * HALO
    rim, own, full = HALO * parts, count * parts, rows * parts
    size = width
    swap = [(i, i ^ 1) for i in range(peers)]
    diag = [(i, (i + 1 if i % 2 else i - 1) % peers) for i in range(peers)]
    pair = [(i, (i + 2 if i % 2 else i - 2) % peers) for i in range(peers)]
    flips = [[(i, i ^ (2 * j)) for i in range(peers)] for j in range(peers // 2)]
    lines = lambda x: x.reshape(-1, LANES)
    row = lambda x: x.reshape(1, width)
    turn = pltpu.VMEM((LANES, LANES), f32)
    here = lambda *xs: [pltpu.with_memory_space_constraint(x, pltpu.HBM) for x in xs]
    hot_shape = shape(edges, window, kind=bf16)
    small = lambda ref: pltpu.VMEM(ref.shape, ref.dtype)

    small_args = [
        lines(fine_senders), lines(up_owner), lines(up_local), lines(coarse_owner),
        lines(coarse_local),
    ]
    biases = [fine_bias, row(up_bias), row(coarse_bias), row(down_bias)]
    ints, out_swap, out_diag = call(
        functools.partial(start_kernel, count, HALO, rows),
        [HBM] * 6,
        [shape(16, LANES), shape(rim + 16, LANES), shape(rim, LANES)],
        [small(x) for x in small_args] + [pltpu.SemaphoreType.DMA((7,))],
    )(*here(lines(fine_state), *small_args))
    swap0 = move(out_swap, swap)
    diag0 = move(out_diag, diag)
    hot, got, into, high, low, state, pack = call(
        functools.partial(near_kernel, edges),
        [VMEM] + [HBM] * 8,
        [hot_shape, shape(edges, width), shape(rows, width)]
        + [shape(2 * size, width, kind=bf16)] * 2
        + [shape(full, LANES), shape(8, width)],
        [turn]
        + [pltpu.VMEM((size, width), f32)] * 3
        + [small(x) for x in biases]
        + [pltpu.SemaphoreType.DMA((8,))],
    )(ints, *here(lines(fine_state), fine_w_send, fine_w_recv, fine_w_out, *biases))
    state, out_half = call(
        far_kernel, [VMEM] * 8, [shape(full, LANES), shape(rim, LANES)]
    )(swap0, diag0, state, hot, got, into, high, low)
    swap1 = move(state, swap)
    diag1 = move(out_half, diag)
    pair1 = move(out_half, pair)
    got, into, own_high, own_low, hot2, select, high, low = call(
        functools.partial(near2_kernel, edges, count),
        [VMEM] * 10,
        [shape(edges, width), shape(rows, width)]
        + [shape(rows, width, kind=bf16)] * 2
        + [hot_shape, shape(coarse // 2, 2 * rows, kind=bf16)]
        + [shape(5 * size, width, kind=bf16)] * 2,
        [turn],
    )(
        state, ints, swap0, hot, fine_w_send, fine_w_recv, fine_w_out, up_w_in, up_w_out,
        pack,
    )
    hidden, *slots = call(
        up_kernel,
        [VMEM] * 16,
        [shape(rows, width)]
        + [shape(own + 8 * coarse_edges // 256, LANES)] * (peers // 2),
        [pltpu.VMEM((window, width), bf16)] * 2,
    )(
        swap1, pair1, diag1, state, hot, got, into, own_high, own_low, hot2, select, ints, swap0,
        high, low, pack,
    )
    arrived = [slots[0]] + [move(slots[j], flips[j]) for j in range(1, peers // 2)]
    (middle,) = call(
        middle_kernel, [VMEM] * (1 + peers // 2), [shape(own, LANES)]
    )(lines(coarse_state), *arrived)
    shift = lambda k: [(i, i ^ k) for i in range(peers)]
    near, far = [middle], [move(middle, shift(peers // 2))]
    for k in range(1, peers // 2):
        near.append(move(middle, shift(k)))
        far.append(move(far[0], shift(k)))
    degree = coarse_edges // count
    coarse_hot, parent_hot = call(
        functools.partial(edges_kernel, degree, count),
        [VMEM] * (1 + peers // 2),
        [
            shape(degree * (count + rows), coarse, kind=bf16),
            shape(rows, coarse, kind=bf16),
        ],
        [turn],
    )(ints, *arrived)
    high, low = call(
        split_kernel, [VMEM] * 5, [shape(5 * size, width, kind=bf16)] * 2
    )(coarse_w_send, coarse_w_recv, coarse_w_out, down_w_in, down_w_out)
    got, wanted = call(
        column_kernel,
        [VMEM] * (4 + peers // 2),
        [shape(degree * (count + rows), width), shape(count + rows, width)],
    )(coarse_hot, parent_hot, high, low, *near)
    fine_out, coarse_out = call(
        coarse_kernel,
        [VMEM] * (8 + peers // 2),
        [shape(full, LANES), shape(own, LANES)],
        [
            pltpu.VMEM((full, LANES), f32), pltpu.VMEM((own, LANES), f32),
            pltpu.SemaphoreType.DMA((3,)),
        ],
        HBM,
    )(hidden, coarse_hot, parent_hot, got, wanted, high, low, pack, *far)
    return (fine_out.reshape(fine_state.shape), coarse_out.reshape(coarse_state.shape))


def shards(*args):
    fine_state, coarse_state, fine_senders = args[0], args[1], args[2]
    coarse_owner, layers = args[5], args[7].shape[0]
    peers = lax.axis_size("sp")
    rows, samples, width = fine_state.shape
    count = coarse_state.shape[0]
    fits = (
        samples == 1
        and layers == 2
        and width % LANES == 0
        and peers % 2 == 0
        and peers & (peers - 1) == 0
        and rows % LANES == 0
        and rows >= HALO
        and count & (count - 1) == 0
        and LANES % count == 0
        and coarse_owner.shape[0] % LANES == 0
        and coarse_owner.shape[0] == 4 * count
        and fine_senders.shape[0] == 8 * LANES
        and rows == 2 * LANES
        and coarse_owner.shape[0] == 2 * LANES
        and width == args[7].shape[2]
        and peers * count <= 1024
        and peers >= 4
        and rows >= 2 * HALO
    )
    if not fits:
        return general_shards(*args)
    return kernel_shards(*args)


def solution(mesh):
    in_specs = (
        P("sp", ("grp", "ch"), None),
        P("sp", ("grp", "ch"), None),
        P("sp"),
        P("sp", None),
        P("sp"),
        P("sp", None),
        P("sp"),
    ) + (P(),) * 14
    out_specs = (P("sp", ("grp", "ch"), None), P("sp", ("grp", "ch"), None))
    return jax.shard_map(shards, mesh=mesh, in_specs=in_specs, out_specs=out_specs, check_vma=False)
```

```python
import functools
import jax
import jax.numpy as jnp
from jax import lax
from jax.experimental import pallas as pl
from jax.experimental.pallas import tpu as pltpu
from jax.sharding import PartitionSpec as P

HALO = 128
LANES = 128


epsilon = 1e-05
highest = lax.Precision.HIGHEST


def extended_2(cells, sides, width):
    for axis, dim in sides:
        count = lax.axis_size(axis)
        head = lax.slice_in_dim(cells, 0, width, axis=dim)
        tail = lax.slice_in_dim(cells, cells.shape[dim] - width, cells.shape[dim], axis=dim)
        cells = jnp.concatenate(
            [
                lax.ppermute(tail, axis, [(i, (i + 1) % count) for i in range(count)]),
                cells,
                lax.ppermute(head, axis, [((i + 1) % count, i) for i in range(count)]),
            ],
            axis=dim,
        )
    return cells


def layer_norm(values):
    average = jnp.mean(values, axis=-1, keepdims=True)
    centered = values - average
    spread = jnp.mean(centered * centered, axis=-1, keepdims=True)
    return centered / jnp.sqrt(spread + epsilon)


def project(values, matrix):
    return jnp.einsum(
        "nsd,dh->nsh", values, matrix, precision=highest, preferred_element_type=jnp.float32
    )


def slot_ranks(owners, peer_count):
    matches = (owners[:, None] == jnp.arange(peer_count, dtype=jnp.int32)[None, :]).astype(
        jnp.int32
    )
    ranking = jnp.cumsum(matches, axis=0) - 1
    return jnp.sum(ranking * matches, axis=1)


def general_shards(
    fine_state,
    coarse_state,
    fine_senders,
    up_owner,
    up_local,
    coarse_owner,
    coarse_local,
    fine_w_send,
    fine_w_recv,
    fine_bias,
    fine_w_out,
    up_w_in,
    up_bias,
    up_w_out,
    coarse_w_send,
    coarse_w_recv,
    coarse_bias,
    coarse_w_out,
    down_w_in,
    down_bias,
    down_w_out,
):
    peer_count = lax.axis_size("sp")
    fine_rows = fine_state.shape[0]
    coarse_rows = coarse_state.shape[0]
    samples = fine_state.shape[1]
    feature_width = fine_state.shape[2]
    degree_fine = fine_senders.shape[0] // fine_rows
    degree_coarse = coarse_owner.shape[0] // coarse_rows
    hidden_state = fine_state
    for layer_index in range(fine_w_send.shape[0]):
        normed = layer_norm(hidden_state)
        outward = project(normed, fine_w_send[layer_index])
        inward = project(normed, fine_w_recv[layer_index]) + fine_bias[layer_index]
        extended = extended_2(outward, (("sp", 0),), HALO)
        gathered = extended[fine_senders].reshape(fine_rows, degree_fine, samples, -1)
        summed = jnp.sum(jax.nn.silu(gathered + inward[:, None]), axis=1)
        hidden_state = hidden_state + project(summed, fine_w_out[layer_index])
    capacity = max(4, 2 * fine_rows // peer_count)
    owners = up_owner[:, 0]
    places = owners * capacity + slot_ranks(owners, peer_count)
    targets = (
        jnp.full((peer_count * capacity,), -1.0, jnp.float32)
        .at[places]
        .set(up_local.astype(jnp.float32))
        .reshape(peer_count, capacity)
    )
    activated = jax.nn.silu(project(layer_norm(hidden_state), up_w_in) + up_bias)
    coarse_ids = jnp.arange(coarse_rows, dtype=jnp.float32)[:, None]
    messages = project(activated, up_w_out)
    outgoing = (
        jnp.zeros((peer_count * capacity, samples, feature_width), jnp.float32)
        .at[places]
        .set(messages)
        .reshape(peer_count, capacity, samples, feature_width)
    )
    arrived, sources = (
        lax.all_to_all(outgoing, "sp", split_axis=0, concat_axis=0, tiled=True),
        lax.all_to_all(targets, "sp", split_axis=0, concat_axis=0, tiled=True),
    )
    selector = (sources.reshape(1, -1) == coarse_ids).astype(jnp.float32)
    gained = jnp.einsum(
        "cr,rsd->csd",
        selector,
        arrived.reshape(peer_count * capacity, samples, feature_width),
        precision=highest,
        preferred_element_type=jnp.float32,
    )
    coarse = coarse_state + gained
    normed = layer_norm(coarse)
    outward = project(normed, coarse_w_send)
    inward = project(normed, coarse_w_recv) + coarse_bias
    anchor_owner = coarse_owner[:, 0]
    everything = lax.all_gather(outward, "sp", axis=0, tiled=True)
    picked = everything[anchor_owner * coarse_rows + coarse_local]
    edge_terms = picked.reshape(coarse_rows, degree_coarse, samples, -1)
    summed = jnp.sum(jax.nn.silu(edge_terms + inward[:, None]), axis=1)
    coarse_out = coarse + project(summed, coarse_w_out)
    downward = project(
        jax.nn.silu(project(layer_norm(coarse_out), down_w_in) + down_bias), down_w_out
    )
    wanted = jnp.maximum(sources.reshape(-1), 0.0).astype(jnp.int32)
    replies = downward[wanted].reshape(peer_count, capacity, samples, feature_width)
    answered = lax.all_to_all(replies, "sp", split_axis=0, concat_axis=0, tiled=True)
    fine_out = (
        hidden_state + answered.reshape(peer_count * capacity, samples, feature_width)[places]
    )
    return (fine_out, coarse_out)


f32 = jnp.float32
bf16 = jnp.bfloat16


def load_rows(ref, rows, parts, start=0):
    return jnp.concatenate(
        [ref[pl.ds(start * parts + j, rows, stride=parts), :] for j in range(parts)], axis=1
    )


def store_rows(ref, values, parts, start=0):
    for j in range(parts):
        ref[pl.ds(start * parts + j, values.shape[0], stride=parts), :] = values[
            :, j * LANES : (j + 1) * LANES
        ]


def halves(values):
    high = values.astype(bf16)
    return high, (values - high.astype(f32)).astype(bf16)


def mm(a, b):
    return jnp.dot(a, b, preferred_element_type=f32)


def times(values, high, low, pieces=1):
    size = values.shape[0] // pieces
    done = []
    for j in range(pieces):
        vh, vl = halves(values[j * size : (j + 1) * size, :])
        done.append(mm(vh, high) + (mm(vl, high) + mm(vh, low)))
    return jnp.concatenate(done, axis=0)


def take(one_hot, high, low):
    return mm(one_hot, high) + mm(one_hot, low)


def place():
    return lax.axis_index("sp").astype(jnp.int32)


def unit(values):
    width = values.shape[1]
    average = jnp.sum(values, axis=1, keepdims=True) * (1.0 / width)
    centered = values - average
    spread = jnp.sum(centered * centered, axis=1, keepdims=True) * (1.0 / width)
    return centered * lax.rsqrt(spread + epsilon)


def gate(half):
    return half + half * jnp.tanh(half)


def equal(column, count):
    ids = lax.broadcasted_iota(jnp.int32, (column.shape[0], count), 1).astype(f32)
    return jnp.where(ids == column, 1.0, 0.0).astype(bf16)


def turned(lines):
    pad = jnp.zeros((LANES - lines.shape[0], LANES), f32)
    return jnp.transpose(jnp.concatenate([lines, pad], axis=0))


def edge_hot(hot_ref, turn_ref, lines, degree, nodes, flip=None):
    turn_ref[...] = turned(lines)
    step = LANES // degree
    for k in range(degree):
        spread = turn_ref[pl.ds(k, step, stride=degree), :]
        if flip is not None:
            spread = jnp.bitwise_xor(spread.astype(jnp.int32), flip).astype(f32)
        for line in range(lines.shape[0]):
            start = k * nodes + line * step
            hot_ref[start : start + step, :] = equal(
                spread[:, line : line + 1], hot_ref.shape[1]
            )


def split_into(high_ref, low_ref, *matrices):
    for j, matrix in enumerate(matrices):
        size = matrix.shape[0]
        high_ref[j * size : (j + 1) * size, :], low_ref[j * size : (j + 1) * size, :] = halves(
            matrix
        )


def weights(high_ref, low_ref, j):
    size = high_ref.shape[1]
    return high_ref[j * size : (j + 1) * size, :], low_ref[j * size : (j + 1) * size, :]


def start_kernel(
    count, halo, state_hbm, sender_hbm, owner_hbm, local_hbm, cowner_hbm,
    clocal_hbm, fb_hbm, ub_hbm, cb_hbm, db_hbm,
    state_ref, ints_ref, pack_ref, swap_ref, diag_ref,
    sender_ref, owner_ref, local_ref, cowner_ref, clocal_ref, fb_ref, ub_ref, cb_ref, db_ref,
    sems,
):
    odd = place() % 2
    rim = diag_ref.shape[0]
    far = state_hbm.shape[0] - rim
    mine = pl.ds(pl.multiple_of((1 - odd) * far, LANES), rim)
    away = pl.ds(pl.multiple_of(odd * far, LANES), rim)
    pairs = [
        (sender_hbm, sender_ref),
        (owner_hbm, owner_ref),
        (local_hbm, local_ref),
        (cowner_hbm, cowner_ref),
        (clocal_hbm, clocal_ref),
        (fb_hbm, fb_ref),
        (ub_hbm, ub_ref),
        (cb_hbm, cb_ref),
        (db_hbm, db_ref),
        (state_hbm.at[mine, :], swap_ref.at[0:rim, :]),
        (state_hbm.at[away, :], diag_ref),
        (state_hbm, state_ref),
    ]
    copies = [pltpu.make_async_copy(a, b, sems.at[j]) for j, (a, b) in enumerate(pairs)]
    for copy in copies:
        copy.start()
    for copy in copies[:-3]:
        copy.wait()
    rows = state_hbm.shape[0] * LANES // fb_ref.shape[1]
    sender = sender_ref[...]
    before = rows + (1 - odd) * halo
    after = rows + odd * halo
    index = jnp.where(
        sender < halo,
        sender + before,
        jnp.where(sender < halo + rows, sender - halo, sender - (halo + rows) + after),
    )
    lines = [
        index.astype(f32),
        (owner_ref[...] * count + local_ref[...]).astype(f32),
        (cowner_ref[...] * count + clocal_ref[...]).astype(f32),
    ]
    rest = ints_ref.shape[0] - sum(x.shape[0] for x in lines)
    ints = jnp.concatenate(lines + [jnp.zeros((rest, LANES), f32)], axis=0)
    ints_ref[...] = ints
    swap_ref[rim:, :] = ints
    pack_ref[...] = jnp.concatenate(
        [fb_ref[...], ub_ref[...], cb_ref[...], db_ref[...]]
        + [jnp.zeros((3, fb_ref.shape[1]), f32)],
        axis=0,
    )
    for copy in copies[-3:]:
        copy.wait()


def near_kernel(
    edges, state_ref, ints_ref, ws_hbm, wr_hbm, wo_hbm, pack_ref,
    hot_ref, got_ref, into_ref, high_ref, low_ref, turn_ref, ws_ref, wr_ref, wo_ref, sems,
):
    rows, width = into_ref.shape
    parts = width // LANES
    pairs = ((ws_hbm, ws_ref), (wr_hbm, wr_ref), (wo_hbm, wo_ref))
    copies = [
        pltpu.make_async_copy(a.at[0], b, sems.at[j]) for j, (a, b) in enumerate(pairs)
    ]
    for copy in copies:
        copy.start()
    edge_hot(hot_ref, turn_ref, ints_ref[: edges // LANES, :], edges // rows, rows)
    normed = unit(load_rows(state_ref, rows, parts))
    for copy in copies:
        copy.wait()
    split_into(high_ref, low_ref, ws_ref[...], wo_ref[...])
    into_ref[...] = (times(normed, *halves(wr_ref[...])) + pack_ref[0:1, :]) * 0.5
    high, low = halves(times(normed, *weights(high_ref, low_ref, 0)) * 0.5)
    got_ref[...] = take(hot_ref[:, :rows], high, low) + jnp.tile(into_ref[...], (edges // rows, 1))


def far_kernel(
    swap_ref, diag_ref, state_ref, hot_ref, got_ref, into_ref, high_ref, low_ref,
    out_full_ref, out_half_ref,
):
    rows, width = into_ref.shape
    parts = width // LANES
    rim = diag_ref.shape[0] // parts
    degree = hot_ref.shape[0] // rows
    far = jnp.concatenate(
        [load_rows(swap_ref, rim, parts), load_rows(diag_ref, rim, parts)], axis=0
    )
    high, low = halves(times(unit(far), *weights(high_ref, low_ref, 0), 2) * 0.5)
    total = None
    for k in range(degree):
        part = slice(k * rows, (k + 1) * rows)
        half = got_ref[part, :] + take(hot_ref[part, rows:], high, low)
        total = gate(half) if total is None else total + gate(half)
    store_rows(
        out_full_ref,
        load_rows(state_ref, rows, parts) + times(total, *weights(high_ref, low_ref, 1), 2),
        parts,
    )
    lines = out_half_ref.shape[0]
    start = pl.multiple_of(place() % 2 * (rows * parts - lines), LANES)
    out_half_ref[...] = out_full_ref[pl.ds(start, lines), :]


def near2_kernel(
    edges, count, state_ref, ints_ref, ints0_ref, hot_ref, ws_ref, wr_ref, wo_ref, wi_ref,
    wu_ref, pack_ref,
    got_ref, into_ref, own_high_ref, own_low_ref, hot2_ref, select_ref, high_ref, low_ref,
    turn_ref,
):
    rows, width = into_ref.shape
    parts = width // LANES
    senders = edges // LANES
    split_into(
        high_ref, low_ref, ws_ref[1], wr_ref[1], wo_ref[1], wi_ref[...], wu_ref[...]
    )
    normed = unit(load_rows(state_ref, rows, parts))
    into_ref[...] = (times(normed, *weights(high_ref, low_ref, 1)) + pack_ref[1:2, :]) * 0.5
    high, low = halves(times(normed, *weights(high_ref, low_ref, 0)) * 0.5)
    own_high_ref[...] = high
    own_low_ref[...] = low
    got_ref[...] = take(hot_ref[:, :rows], high, low) + jnp.tile(into_ref[...], (edges // rows, 1))
    first = ints0_ref.shape[0] - ints_ref.shape[0]
    edge_hot(hot2_ref, turn_ref, ints0_ref[first : first + senders, :], edges // rows, rows)
    flip = place() * count
    line = senders
    for half, ref, base in ((0, ints_ref, 0), (1, ints0_ref, first)):
        for j in range(rows // LANES):
            parent = ref[base + line + j : base + line + j + 1, :].astype(jnp.int32)
            parent = jnp.bitwise_xor(parent, flip)
            ids = lax.broadcasted_iota(jnp.int32, (select_ref.shape[0], LANES), 0)
            ids = ids + jnp.bitwise_and(ids, -count)
            start = half * rows + j * LANES
            select_ref[:, start : start + LANES] = jnp.where(ids == parent, 1.0, 0.0).astype(
                bf16
            )


def up_kernel(
    swap_ref, pair_ref, diag_ref, state_ref, hot_ref, got_ref, into_ref, own_high_ref,
    own_low_ref, hot2_ref, select_ref, ints_ref, ints0_ref, high_ref, low_ref, pack_ref,
    last_ref, *refs,
):
    *slot_refs, th_ref, tl_ref = refs
    rows, width = into_ref.shape
    parts = width // LANES
    rim = diag_ref.shape[0] // parts
    degree = hot_ref.shape[0] // rows
    odd = place() % 2
    mine = pl.multiple_of((1 - odd) * (rows - rim), LANES)
    theirs = pl.multiple_of(odd * (rows - rim), LANES)
    other = load_rows(swap_ref, rows, parts)
    normed = unit(
        jnp.concatenate(
            [other, load_rows(pair_ref, rim, parts), load_rows(diag_ref, rim, parts)], axis=0
        )
    )
    sends = halves(times(normed, *weights(high_ref, low_ref, 0), 2) * 0.5)
    near = []
    for src, t_ref, own_ref in (
        (sends[0], th_ref, own_high_ref), (sends[1], tl_ref, own_low_ref),
    ):
        t_ref[:rows, :] = src[:rows, :]
        t_ref[rows : rows + rim, :] = own_ref[pl.ds(mine, rim), :]
        t_ref[rows + rim :, :] = src[rows : rows + rim, :]
        near.append(
            jnp.concatenate([t_ref[pl.ds(theirs, rim), :], src[rows + rim :, :]], axis=0)
        )
    into = (times(normed[:rows, :], *weights(high_ref, low_ref, 1)) + pack_ref[1:2, :]) * 0.5
    total, total2 = None, None
    for k in range(degree):
        part = slice(k * rows, (k + 1) * rows)
        half = got_ref[part, :] + take(hot_ref[part, rows:], *near)
        total = gate(half) if total is None else total + gate(half)
        half = into + take(hot2_ref[part, :], th_ref[...], tl_ref[...])
        total2 = gate(half) if total2 is None else total2 + gate(half)
    hidden = jnp.concatenate([load_rows(state_ref, rows, parts), other], axis=0) + times(
        jnp.concatenate([total, total2], axis=0), *weights(high_ref, low_ref, 2), 2
    )
    last_ref[...] = hidden[:rows, :]
    act = gate((times(unit(hidden), *weights(high_ref, low_ref, 3), 2) + pack_ref[2:3, :]) * 0.5)
    sums = take(select_ref[...], *halves(times(act, *weights(high_ref, low_ref, 4), 2)))
    size = sums.shape[0] // len(slot_refs)
    first = hot_ref.shape[0] // LANES + rows // LANES
    base = ints0_ref.shape[0] - ints_ref.shape[0]
    anchor = (slot_refs[0].shape[0] - size * parts) // 4
    for j, slot in enumerate(slot_refs):
        store_rows(slot, sums[j * size : (j + 1) * size, :], parts)
        slot[size * parts :, :] = jnp.concatenate(
            [
                ints_ref[first : first + anchor, :],
                ints0_ref[base + first : base + first + anchor, :],
                jnp.zeros((2 * anchor, LANES), f32),
            ],
            axis=0,
        )


def middle_kernel(state_ref, *refs):
    out_ref = refs[-1]
    total = state_ref[...]
    for ref in refs[:-1]:
        total = total + ref[: out_ref.shape[0], :]
    out_ref[...] = total


def position(ids, flip):
    return jnp.bitwise_xor(ids.astype(jnp.int32), flip)


def split_kernel(cs_ref, cr_ref, co_ref, di_ref, do_ref, high_ref, low_ref):
    split_into(
        high_ref, low_ref, cs_ref[...], cr_ref[...], co_ref[...], di_ref[...], do_ref[...]
    )


def edges_kernel(degree, count, ints_ref, *refs):
    *slot_refs, hot_ref, parent_ref, turn_ref = refs
    rows, coarse = parent_ref.shape
    flip = place() * count
    columns = turned(ints_ref[...])
    first = ints_ref.shape[0] // 2
    for j in range(rows // LANES):
        column = position(columns[:, first + j : first + j + 1], flip).astype(f32)
        parent_ref[j * LANES : (j + 1) * LANES, :] = equal(column, coarse)
    here = coarse * degree // LANES // len(slot_refs)
    lines = jnp.concatenate(
        [ref[ref.shape[0] - 2 * here : ref.shape[0] - here, :] for ref in slot_refs], axis=0
    )
    turn_ref[...] = turned(lines)
    step = LANES // degree
    lane = lax.broadcasted_iota(jnp.int32, (coarse, LANES), 1)
    table = jnp.zeros((coarse, LANES), f32)
    each = hot_ref.shape[0] // degree
    for k in range(degree):
        spread = position(turn_ref[pl.ds(k, step, stride=degree), :], flip)
        column = jnp.concatenate([spread[:, j : j + 1] for j in range(lines.shape[0])], axis=0)
        hot_ref[k * each : k * each + count, :] = equal(column[:count, :].astype(f32), coarse)
        high = jnp.right_shift(column, 8).astype(f32)
        low = jnp.bitwise_and(column, 255).astype(f32)
        table = jnp.where(lane == k, high, jnp.where(lane == degree + k, low, table))
    found = mm(parent_ref[...], table.astype(bf16))
    for k in range(degree):
        column = found[:, k : k + 1] * 256.0 + found[:, degree + k : degree + k + 1]
        hot_ref[k * each + count : (k + 1) * each, :] = equal(column, coarse)


def column_kernel(hot_ref, parent_ref, high_ref, low_ref, *refs):
    *blocks, got_ref, wanted_ref = refs
    _, width = wanted_ref.shape
    parts = width // LANES
    count = blocks[0].shape[0] // parts
    middle = jnp.concatenate([load_rows(b, count, parts) for b in blocks], axis=0)
    half = count * len(blocks)
    sends = halves(times(unit(middle), *weights(high_ref, low_ref, 0)) * 0.5)
    got_ref[...] = take(hot_ref[:, :half], *sends)
    wanted_ref[:count, :] = middle[:count, :]
    wanted_ref[count:, :] = take(parent_ref[:, :half], *halves(middle))


def coarse_kernel(
    last_ref, hot_ref, parent_ref, got_ref, wanted_ref, high_ref, low_ref, pack_ref, *refs
):
    *blocks, fine_hbm, coarse_hbm, fine_ref, coarse_ref, sems = refs
    rows, width = last_ref.shape
    parts = width // LANES
    count = coarse_ref.shape[0] // parts
    need = count + rows
    middle = jnp.concatenate([load_rows(b, count, parts) for b in blocks], axis=0)
    half = count * len(blocks)
    sends = halves(times(unit(middle), *weights(high_ref, low_ref, 0)) * 0.5)
    wanted = jnp.concatenate(
        [
            wanted_ref[:count, :],
            wanted_ref[count:, :] + take(parent_ref[:, half:], *halves(middle)),
        ],
        axis=0,
    )
    into = (times(unit(wanted), *weights(high_ref, low_ref, 1)) + pack_ref[3:4, :]) * 0.5
    total = None
    for k in range(hot_ref.shape[0] // need):
        part = slice(k * need, (k + 1) * need)
        term = gate(got_ref[part, :] + into + take(hot_ref[part, half:], *sends))
        total = term if total is None else total + term
    done = wanted + times(total, *weights(high_ref, low_ref, 2))
    store_rows(coarse_ref, done[:count, :], parts)
    copies = [pltpu.make_async_copy(coarse_ref, coarse_hbm, sems.at[0])]
    copies[0].start()
    act = gate(
        (times(unit(done[count:, :]), *weights(high_ref, low_ref, 3)) + pack_ref[4:5, :]) * 0.5
    )
    size = rows // 2
    for j in range(2):
        down = times(act[j * size : (j + 1) * size, :], *weights(high_ref, low_ref, 4))
        store_rows(fine_ref, last_ref[j * size : (j + 1) * size, :] + down, parts, j * size)
        piece = pl.ds(j * size * parts, size * parts)
        copies.append(
            pltpu.make_async_copy(fine_ref.at[piece, :], fine_hbm.at[piece, :], sems.at[j + 1])
        )
        copies[-1].start()
    for copy in copies:
        copy.wait()


VMEM = pl.BlockSpec(memory_space=pltpu.VMEM)
SMEM = pl.BlockSpec(memory_space=pltpu.SMEM)
HBM = pl.BlockSpec(memory_space=pltpu.HBM)


def call(kernel, in_specs, out_shapes, scratch=(), out_spec=VMEM):
    return pl.pallas_call(
        kernel,
        in_specs=in_specs,
        out_specs=[out_spec] * len(out_shapes),
        out_shape=out_shapes,
        scratch_shapes=scratch,
        compiler_params=pltpu.CompilerParams(vmem_limit_bytes=32 * 2**20),
    )


def move(values, pairs):
    return lax.ppermute(values, "sp", pairs)


def shape(*dims, kind=f32):
    return jax.ShapeDtypeStruct(dims, kind)


def kernel_shards(
    fine_state,
    coarse_state,
    fine_senders,
    up_owner,
    up_local,
    coarse_owner,
    coarse_local,
    fine_w_send,
    fine_w_recv,
    fine_bias,
    fine_w_out,
    up_w_in,
    up_bias,
    up_w_out,
    coarse_w_send,
    coarse_w_recv,
    coarse_bias,
    coarse_w_out,
    down_w_in,
    down_bias,
    down_w_out,
):
    peers = lax.axis_size("sp")
    me = lax.axis_index("sp").astype(jnp.int32)
    rows, _, width = fine_state.shape
    count = coarse_state.shape[0]
    parts = width // LANES
    edges = fine_senders.shape[0]
    coarse_edges = coarse_owner.shape[0]
    coarse = peers * count
    window = rows + 2 * HALO
    rim, own, full = HALO * parts, count * parts, rows * parts
    size = width
    swap = [(i, i ^ 1) for i in range(peers)]
    diag = [(i, (i + 1 if i % 2 else i - 1) % peers) for i in range(peers)]
    pair = [(i, (i + 2 if i % 2 else i - 2) % peers) for i in range(peers)]
    flips = [[(i, i ^ (2 * j)) for i in range(peers)] for j in range(peers // 2)]
    lines = lambda x: x.reshape(-1, LANES)
    row = lambda x: x.reshape(1, width)
    turn = pltpu.VMEM((LANES, LANES), f32)
    here = lambda *xs: [pltpu.with_memory_space_constraint(x, pltpu.HBM) for x in xs]
    hot_shape = shape(edges, window, kind=bf16)
    small = lambda ref: pltpu.VMEM(ref.shape, ref.dtype)

    small_args = [
        lines(fine_senders), lines(up_owner), lines(up_local), lines(coarse_owner),
        lines(coarse_local), fine_bias, row(up_bias), row(coarse_bias), row(down_bias),
    ]
    state, ints, pack, out_swap, out_diag = call(
        functools.partial(start_kernel, count, HALO),
        [HBM] * 10,
        [
            shape(full, LANES), shape(16, LANES), shape(8, width), shape(rim + 16, LANES),
            shape(rim, LANES),
        ],
        [small(x) for x in small_args] + [pltpu.SemaphoreType.DMA((12,))],
    )(*here(lines(fine_state), *small_args))
    swap0 = move(out_swap, swap)
    diag0 = move(out_diag, diag)
    hot, got, into, high, low = call(
        functools.partial(near_kernel, edges),
        [VMEM] * 2 + [HBM] * 3 + [VMEM],
        [hot_shape, shape(edges, width), shape(rows, width)]
        + [shape(2 * size, width, kind=bf16)] * 2,
        [turn] + [pltpu.VMEM((size, width), f32)] * 3 + [pltpu.SemaphoreType.DMA((3,))],
    )(state, ints, *here(fine_w_send, fine_w_recv, fine_w_out), pack)
    state, out_half = call(
        far_kernel, [VMEM] * 8, [shape(full, LANES), shape(rim, LANES)]
    )(swap0, diag0, state, hot, got, into, high, low)
    swap1 = move(state, swap)
    diag1 = move(out_half, diag)
    pair1 = move(out_half, pair)
    got, into, own_high, own_low, hot2, select, high, low = call(
        functools.partial(near2_kernel, edges, count),
        [VMEM] * 10,
        [shape(edges, width), shape(rows, width)]
        + [shape(rows, width, kind=bf16)] * 2
        + [hot_shape, shape(coarse // 2, 2 * rows, kind=bf16)]
        + [shape(5 * size, width, kind=bf16)] * 2,
        [turn],
    )(
        state, ints, swap0, hot, fine_w_send, fine_w_recv, fine_w_out, up_w_in, up_w_out,
        pack,
    )
    hidden, *slots = call(
        up_kernel,
        [VMEM] * 16,
        [shape(rows, width)]
        + [shape(own + 8 * coarse_edges // 256, LANES)] * (peers // 2),
        [pltpu.VMEM((window, width), bf16)] * 2,
    )(
        swap1, pair1, diag1, state, hot, got, into, own_high, own_low, hot2, select, ints, swap0,
        high, low, pack,
    )
    arrived = [slots[0]] + [move(slots[j], flips[j]) for j in range(1, peers // 2)]
    (middle,) = call(
        middle_kernel, [VMEM] * (1 + peers // 2), [shape(own, LANES)]
    )(lines(coarse_state), *arrived)
    shift = lambda k: [(i, i ^ k) for i in range(peers)]
    near, far = [middle], [move(middle, shift(peers // 2))]
    for k in range(1, peers // 2):
        near.append(move(middle, shift(k)))
        far.append(move(far[0], shift(k)))
    degree = coarse_edges // count
    coarse_hot, parent_hot = call(
        functools.partial(edges_kernel, degree, count),
        [VMEM] * (1 + peers // 2),
        [
            shape(degree * (count + rows), coarse, kind=bf16),
            shape(rows, coarse, kind=bf16),
        ],
        [turn],
    )(ints, *arrived)
    high, low = call(
        split_kernel, [VMEM] * 5, [shape(5 * size, width, kind=bf16)] * 2
    )(coarse_w_send, coarse_w_recv, coarse_w_out, down_w_in, down_w_out)
    got, wanted = call(
        column_kernel,
        [VMEM] * (4 + peers // 2),
        [shape(degree * (count + rows), width), shape(count + rows, width)],
    )(coarse_hot, parent_hot, high, low, *near)
    fine_out, coarse_out = call(
        coarse_kernel,
        [VMEM] * (8 + peers // 2),
        [shape(full, LANES), shape(own, LANES)],
        [
            pltpu.VMEM((full, LANES), f32), pltpu.VMEM((own, LANES), f32),
            pltpu.SemaphoreType.DMA((3,)),
        ],
        HBM,
    )(hidden, coarse_hot, parent_hot, got, wanted, high, low, pack, *far)
    return (fine_out.reshape(fine_state.shape), coarse_out.reshape(coarse_state.shape))


def shards(*args):
    fine_state, coarse_state, fine_senders = args[0], args[1], args[2]
    coarse_owner, layers = args[5], args[7].shape[0]
    peers = lax.axis_size("sp")
    rows, samples, width = fine_state.shape
    count = coarse_state.shape[0]
    fits = (
        samples == 1
        and layers == 2
        and width % LANES == 0
        and peers % 2 == 0
        and peers & (peers - 1) == 0
        and rows % LANES == 0
        and rows >= HALO
        and count & (count - 1) == 0
        and LANES % count == 0
        and coarse_owner.shape[0] % LANES == 0
        and coarse_owner.shape[0] == 4 * count
        and fine_senders.shape[0] == 8 * LANES
        and rows == 2 * LANES
        and coarse_owner.shape[0] == 2 * LANES
        and width == args[7].shape[2]
        and peers * count <= 1024
        and peers >= 4
        and rows >= 2 * HALO
    )
    if not fits:
        return general_shards(*args)
    return kernel_shards(*args)


def solution(mesh):
    in_specs = (
        P("sp", ("grp", "ch"), None),
        P("sp", ("grp", "ch"), None),
        P("sp"),
        P("sp", None),
        P("sp"),
        P("sp", None),
        P("sp"),
    ) + (P(),) * 14
    out_specs = (P("sp", ("grp", "ch"), None), P("sp", ("grp", "ch"), None))
    return jax.shard_map(shards, mesh=mesh, in_specs=in_specs, out_specs=out_specs, check_vma=False)
```
